32 devices in a mesh: groups: 2 (over y), ep: 16 (over z, x, core).
Axes of the slice: x: 2, y: 2, z: 4, core: 2. Of those that a mesh axis runs over, the one named last changes fastest.
Arguments:
- queries: bfloat16 [32, 64, 512], P(('groups', 'ep')), parts along dimension 0, may hold values from -8 to 8
- key_cache: bfloat16 [32, 2, 512, 128], P(('groups', 'ep')), parts along dimension 0, may hold values from -6 to 6
- value_cache: bfloat16 [32, 2, 512, 128], P(('groups', 'ep')), parts along dimension 0, may hold values from -6 to 6
- key_block: bfloat16 [32, 64, 128], P(('groups', 'ep')), parts along dimension 0, may hold values from -8 to 8
- value_block: bfloat16 [32, 64, 128], P(('groups', 'ep')), parts along dimension 0, may hold values from -6 to 6
- cache_length_list: int32 [16], P('groups'), parts along dimension 0, may hold values from 0 to 512, as said below
- residual: bfloat16 [512, 2048], P(('groups', 'ep')), parts along dimension 0, may hold values from -6 to 6
- output_weight: bfloat16 [16, 512, 2048], P('ep'), may hold values from -3 to 3, as said below
- norm_gain: float32 [2048], replicated, may hold values from 0.1 to 1.9
- routes: int32 [512, 8], P(('groups', 'ep')), parts along dimension 0, may hold values from 0 to 15, all different within a row; in each aligned block of 16 rows (0 to 15, 16 to 31, ...) at most 16 rows name the same one
- route_logits: float32 [512, 8], P(('groups', 'ep')), parts along dimension 0, may hold values from -8 to 8
- w_gate: bfloat16 [16, 2048, 768], P('ep'), may hold values from -0.125 to 0.125
- w_up: bfloat16 [16, 2048, 768], P('ep'), may hold values from -0.125 to 0.125
- w_down: bfloat16 [16, 768, 2048], P('ep'), may hold values from -0.21875 to 0.21875
Outputs:
- attended: bfloat16 [512, 2048], P(('groups', 'ep')), parts along dimension 0
- expert_out: bfloat16 [512, 2048], P(('groups', 'ep')), parts along dimension 0
The draws below stay inside these ranges and needn't reach their ends.
There are 2 independent parts, one for each index of `groups`. The reference program is written for one: setup_inputs(seed, part) draws one part's arguments, and reference() takes and returns one part's arrays. A program takes and returns all parts, laid end to end along the dimension named above; an argument that names none is the same for every part. Nothing has to cross between parts.
Inputs may be any that keep to these rules, and one draw needn't show every extreme that they name: `cache_length_list`: multiples of 32; some sequence has exactly 512 in every draw. `output_weight`: entries p and q along the first dimension are equal where p - q is a multiple of 4. `routes`: each row names 8 different experts; at most 16 rows of one device name one expert, a bound that some block reaches.
All inputs are finite; a program needn't handle non-finite values.
Results may differ from the reference program's by a relative error of at most 0.0079.
Values may be sent and summed in bfloat16 or wider, within the bound.
No kernel may reach another device: no remote copies, remote signals or barrier semaphores. Data moves between devices by JAX's collectives and lax.ppermute only.
A program may use at most 64 MiB of HBM per device.

```python
import math
import jax
import jax.numpy as jnp
import numpy as np
from jax import lax

MODEL_WIDTH = 2048
QUERY_HEADS = 16
KEY_VALUE_HEADS = 4
HEAD_SIZE = 128
H = 768
TOP = 8
BLOCK_ROWS = 32
CACHE_SLOTS = 512
GROUP_SEQUENCES = 2
SEQUENCE_GROUPS = 4
SEQS = 8
ROWS_DEV = 16
ROWS = 256
EXPERTS = 16
CAP = 16
N_EP = 16


def draw_queries(key, part):
    value_entries = jnp.clip(jax.random.normal(jax.random.fold_in(key, 11), (SEQUENCE_GROUPS * KEY_VALUE_HEADS, GROUP_SEQUENCES * BLOCK_ROWS, QUERY_HEADS // KEY_VALUE_HEADS * HEAD_SIZE), jnp.float32), -6.0, 6.0)
    return value_entries.astype(jnp.bfloat16)


def draw_key_block(key, part):
    value_entries = jnp.clip(jax.random.normal(jax.random.fold_in(key, 12), (SEQUENCE_GROUPS * KEY_VALUE_HEADS, GROUP_SEQUENCES * BLOCK_ROWS, HEAD_SIZE), jnp.float32), -6.0, 6.0)
    return value_entries.astype(jnp.bfloat16)


def draw_cache_length_list(key, part):
    counts = jax.random.randint(jax.random.fold_in(key, 13), (SEQS,), 0, CACHE_SLOTS // BLOCK_ROWS + 1)
    counts = counts.at[0].set(CACHE_SLOTS // BLOCK_ROWS)
    return (counts * BLOCK_ROWS).astype(jnp.int32)


def draw_output_weight(key, part):
    start_offset = jnp.clip(jax.random.normal(jax.random.fold_in(key, 21), (KEY_VALUE_HEADS, QUERY_HEADS // KEY_VALUE_HEADS * HEAD_SIZE, MODEL_WIDTH), jnp.float32), -6.0, 6.0)
    start_offset = start_offset * (MODEL_WIDTH // 16) ** (-0.5)
    return jnp.tile(start_offset, (SEQUENCE_GROUPS, 1, 1)).astype(jnp.bfloat16)


def steps_of(own_key, extent, shards, least, top_value):
    level = 1.0
    for dim, blocks in shards:
        steps = jax.random.uniform(jax.random.fold_in(jax.random.fold_in(own_key, 6), dim), (blocks,), jnp.float32, least / len(shards), top_value / len(shards))
        level = level * jnp.repeat(jnp.exp(steps), extent[dim] // blocks).reshape((-1,) + (1,) * (len(extent) - 1 - dim))
    return level


def routed_block(own_key, own, number, rows, count, top, most, skew):
    ranking = jax.random.permutation(own_key, count)
    crowded, ordinary = portions_of(count, rows * top, most, skew, True), portions_of(count, rows * top, most, skew, False)
    places = jnp.arange(count)

    def named(sizes, offset_by):
        used = int((sizes > 0).sum())
        fixed = max(1, used // 4)
        moved = fixed + (places - fixed + offset_by * (used - fixed)) % max(1, count - fixed)
        return jnp.zeros((count,), jnp.int32).at[ranking[jnp.where(places < fixed, places, moved)]].set(jnp.asarray(sizes, jnp.int32))

    sizes = jnp.where(number % 4 == 0, named(crowded, number // 4), named(ordinary, number - number // 4 - 1))
    mixed = jax.random.permutation(jax.random.fold_in(own, 3), count)
    donor, sink = mixed[0:count // 2 * 2:2], mixed[1:count // 2 * 2:2]
    margin = jnp.minimum(sizes[donor] - 1, most - sizes[sink]) // 2
    margin = jnp.where((donor == ranking[0]) | (sink == ranking[0]) | (sizes[sink] == 0), 0, jnp.maximum(margin, 0))
    moved = jax.random.randint(jax.random.fold_in(own, 4), (count // 2,), 0, 1 << 20) % (margin + 1)
    sizes = sizes.at[donor].add(-moved).at[sink].add(moved)
    items = jnp.searchsorted(jnp.cumsum(sizes), jnp.arange(rows * top), side="right").astype(jnp.int32)
    listing = items.reshape(top, rows).T
    listing = listing[jax.random.permutation(jax.random.fold_in(own, 1), rows)]
    offset_by = jax.random.randint(jax.random.fold_in(own, 2), (rows, 1), 0, top)
    return jnp.take_along_axis(listing, (jnp.arange(top)[None, :] + offset_by) % top, axis=1)


def portions_of(number_of, total, most, slope, full):
    portions = [(1 << 20) // math.isqrt(grade ** slope) + 1 for grade in range(1, number_of + 1)]
    largest = most if full else min(most, max(-(-total // number_of), total * portions[0] // sum(portions)))
    least = 1 if total - largest >= number_of - 1 else 0
    given, spare = [largest] + [least] * (number_of - 1), total - largest - least * (number_of - 1)
    while spare > 0:
        candidates = [i for i in range(1, number_of) if given[i] < largest] or [i for i in range(1, number_of) if given[i] < most]
        mass, left = sum([portions[i] for i in candidates]), spare
        for i in candidates:
            extra = min(most - given[i], max(1, left * portions[i] // mass), spare)
            given[i] = given[i] + extra
            spare = spare - extra
    return np.array(given)


def bell_draw(own_key, shape, scale, limit, cuts=(), held_as=jnp.bfloat16):
    entries = scale * jax.random.normal(own_key, shape, jnp.float32)
    if cuts:
        entries = entries * steps_of(own_key, shape, cuts, -0.22, 0.18)
    return jnp.clip(entries, -limit, limit).astype(held_as)


def setup_inputs(seed: int = 0, part: int = 0) -> dict:
    splits = jax.random.split(jax.random.key(seed), 15)
    part_keys = jax.random.split(jax.random.fold_in(splits[14], part), 15)
    queries = draw_queries(jax.random.fold_in(jax.random.fold_in(splits[14], part), 71), part)
    key_cache = bell_draw(part_keys[1], (SEQUENCE_GROUPS * KEY_VALUE_HEADS, GROUP_SEQUENCES, CACHE_SLOTS, HEAD_SIZE), 1.0, 6.0, ((0, 16),))
    value_cache = bell_draw(part_keys[2], (SEQUENCE_GROUPS * KEY_VALUE_HEADS, GROUP_SEQUENCES, CACHE_SLOTS, HEAD_SIZE), 1.0, 6.0, ((0, 16),))
    key_block = draw_key_block(jax.random.fold_in(jax.random.fold_in(splits[14], part), 71), part)
    value_block = bell_draw(part_keys[4], (SEQUENCE_GROUPS * KEY_VALUE_HEADS, GROUP_SEQUENCES * BLOCK_ROWS, HEAD_SIZE), 1.0, 6.0, ((0, 16),))
    cache_length_list = draw_cache_length_list(jax.random.fold_in(jax.random.fold_in(splits[14], part), 71), part)
    residual = bell_draw(part_keys[6], (ROWS, MODEL_WIDTH), 1.0, 6.0, ((0, 16),))
    output_weight = draw_output_weight(jax.random.fold_in(splits[14], 71), part)
    norm_gain = jnp.clip(1.0 + 0.18 * jax.random.normal(splits[8], (MODEL_WIDTH,), jnp.float32), 0.1, 1.9)
    routes_keys = jax.random.split(jax.random.fold_in(part_keys[9], 1), ROWS // ROWS_DEV)
    routes_turns = jax.random.permutation(jax.random.fold_in(part_keys[9], 3), ROWS // ROWS_DEV)
    routes = jax.vmap(lambda own, number: routed_block(jax.random.fold_in(part_keys[9], 2), own, number, ROWS_DEV, EXPERTS, TOP, CAP, 2))(routes_keys, routes_turns).reshape((ROWS, TOP))
    route_logits = bell_draw(part_keys[10], (ROWS, TOP), 2.0, 8.0, ((0, 16),), jnp.float32)
    w_gate = bell_draw(splits[11], (EXPERTS, MODEL_WIDTH, H), MODEL_WIDTH ** -0.5, 0.125, ((0, 16),))
    w_up = bell_draw(splits[12], (EXPERTS, MODEL_WIDTH, H), MODEL_WIDTH ** -0.5, 0.125, ((0, 16),))
    w_down = bell_draw(splits[13], (EXPERTS, H, MODEL_WIDTH), H ** -0.5, 0.21875, ((0, 16),))
    return {"queries": queries, "key_cache": key_cache, "value_cache": value_cache, "key_block": key_block, "value_block": value_block, "cache_length_list": cache_length_list, "residual": residual, "output_weight": output_weight, "norm_gain": norm_gain, "routes": routes, "route_logits": route_logits, "w_gate": w_gate, "w_up": w_up, "w_down": w_down}


ROUTE_SCALE = 2.5
EPSILON = 1e-06

def attend_sequence_group(inputs):
    query_head_group, keys_of_cache, values_of_cache, keys_of_block, values_of_block, group_lens, w_group = inputs
    group_results = QUERY_HEADS // KEY_VALUE_HEADS
    heads_of_query = query_head_group.astype(jnp.float32).reshape(KEY_VALUE_HEADS, GROUP_SEQUENCES, BLOCK_ROWS, group_results, HEAD_SIZE)
    key_row_list = jnp.concatenate([keys_of_cache, keys_of_block.reshape(KEY_VALUE_HEADS, GROUP_SEQUENCES, BLOCK_ROWS, HEAD_SIZE)], 2).astype(jnp.float32)
    value_row_list = jnp.concatenate([values_of_cache, values_of_block.reshape(KEY_VALUE_HEADS, GROUP_SEQUENCES, BLOCK_ROWS, HEAD_SIZE)], 2).astype(jnp.float32)
    scores = jnp.einsum('ksrgd,kspd->ksgrp', heads_of_query, key_row_list) / math.sqrt(HEAD_SIZE)
    position = jnp.arange(CACHE_SLOTS + BLOCK_ROWS, dtype=jnp.int32)
    live_slots = (position[None, :] < group_lens[:, None]) | (position[None, :] >= CACHE_SLOTS)
    scores = jnp.where(live_slots[None, :, None, None, :], scores, -1e+30)
    largest = lax.optimization_barrier(jnp.max(scores, -1, keepdims=True))
    expo = jnp.exp(scores - largest)
    probs = (expo / lax.optimization_barrier(jnp.sum(expo, -1, keepdims=True))).astype(jnp.bfloat16)
    probs = lax.optimization_barrier(probs).astype(jnp.float32)
    mixed_heads = jnp.einsum('ksgrp,kspd->srkgd', probs, value_row_list)
    attn_heads = mixed_heads.reshape(GROUP_SEQUENCES * BLOCK_ROWS, QUERY_HEADS * HEAD_SIZE).astype(jnp.bfloat16)
    return jnp.dot(attn_heads, w_group, preferred_element_type=jnp.float32)

def run_expert(rows_in, gate_matrix, up_matrix, down_matrix):
    gate_part = jnp.dot(rows_in, gate_matrix, preferred_element_type=jnp.float32)
    up_part = jnp.dot(rows_in, up_matrix, preferred_element_type=jnp.float32)
    active = (jax.nn.silu(gate_part) * up_part).astype(jnp.bfloat16)
    return jnp.dot(active, down_matrix, preferred_element_type=jnp.float32).astype(jnp.bfloat16)

def reference(queries, key_cache, value_cache, key_block, value_block, cache_length_list, residual, output_weight, norm_gain, routes, route_logits, w_gate, w_up, w_down):
    group_results = QUERY_HEADS // KEY_VALUE_HEADS
    groups_projected = lax.map(attend_sequence_group, (queries.reshape(SEQUENCE_GROUPS, KEY_VALUE_HEADS, GROUP_SEQUENCES * BLOCK_ROWS, group_results * HEAD_SIZE), key_cache.reshape(SEQUENCE_GROUPS, KEY_VALUE_HEADS, GROUP_SEQUENCES, CACHE_SLOTS, HEAD_SIZE), value_cache.reshape(SEQUENCE_GROUPS, KEY_VALUE_HEADS, GROUP_SEQUENCES, CACHE_SLOTS, HEAD_SIZE), key_block.reshape(SEQUENCE_GROUPS, KEY_VALUE_HEADS, GROUP_SEQUENCES * BLOCK_ROWS, HEAD_SIZE), value_block.reshape(SEQUENCE_GROUPS, KEY_VALUE_HEADS, GROUP_SEQUENCES * BLOCK_ROWS, HEAD_SIZE), cache_length_list.reshape(SEQUENCE_GROUPS, GROUP_SEQUENCES).astype(jnp.int32), output_weight.reshape(SEQUENCE_GROUPS, QUERY_HEADS * HEAD_SIZE, MODEL_WIDTH)))
    projected = groups_projected.reshape(ROWS, MODEL_WIDTH)
    hidden = residual.astype(jnp.float32) + projected
    attended = hidden.astype(jnp.bfloat16)
    normed = (hidden * lax.rsqrt(lax.optimization_barrier(jnp.mean(hidden * hidden, -1, keepdims=True)) + EPSILON) * norm_gain).astype(jnp.bfloat16)
    sig_values = jax.nn.sigmoid(route_logits)
    route_weights = ROUTE_SCALE * sig_values / lax.optimization_barrier(jnp.sum(sig_values, -1, keepdims=True))
    flat_ids = routes.reshape(N_EP, ROWS_DEV * TOP).astype(jnp.int32)
    onehot = (flat_ids[:, :, None] == jnp.arange(EXPERTS, dtype=jnp.int32)[None, None, :]).astype(jnp.int32)
    slot_rank = (lax.optimization_barrier(jnp.sum(jnp.cumsum(onehot, 1) * onehot, -1)) - 1).astype(jnp.int32)
    block_index = jnp.broadcast_to(jnp.arange(N_EP, dtype=jnp.int32)[:, None], flat_ids.shape)
    row_index = (block_index * ROWS_DEV + jnp.arange(ROWS_DEV * TOP, dtype=jnp.int32)[None, :] // TOP).astype(jnp.int32)
    table = jnp.full((EXPERTS, N_EP, CAP), ROWS, jnp.int32).at[flat_ids, block_index, slot_rank].set(row_index)
    weight_table = jnp.zeros((EXPERTS, N_EP, CAP), jnp.float32).at[flat_ids, block_index, slot_rank].set(route_weights.reshape(N_EP, ROWS_DEV * TOP))
    normed_pad = jnp.concatenate([normed, jnp.zeros((1, MODEL_WIDTH), jnp.bfloat16)], 0)

    def accumulate(carry, inputs):
        index_rows, weight_rows, gate_matrix, up_matrix, down_matrix = inputs
        index_flat = index_rows.reshape(-1)
        output_rows = run_expert(normed_pad[index_flat], gate_matrix, up_matrix, down_matrix)
        carry = carry.at[index_flat].add(weight_rows.reshape(-1)[:, None] * output_rows.astype(jnp.float32))
        return (carry, None)
    summed, _ = lax.scan(accumulate, jnp.zeros((ROWS + 1, MODEL_WIDTH), jnp.float32), (table, weight_table, w_gate, w_up, w_down))
    expert_out = summed[:ROWS].astype(jnp.bfloat16)
    return (attended, expert_out)
```

```python
import math

import jax
import jax.numpy as jnp
from jax import lax
from jax.sharding import PartitionSpec as P

MODEL_WIDTH = 2048
QUERY_HEADS = 16
KEY_VALUE_HEADS = 4
HEAD_SIZE = 128


ROUTE_SCALE = 2.5
EPSILON = 1e-06
LANES = 128


def swapped(block, axis, distance):
    count = lax.axis_size(axis)
    route = []
    for low in range(count):
        high = low | 1 << distance
        if high != low and high < count:
            route += [(low, high), (high, low)]
    return lax.ppermute(block, axis, route)


def exchanged(block, axis, mask):
    count = lax.axis_size(axis)
    return lax.ppermute(block, axis, [(index, index ^ mask) for index in range(count)])


def on_device(
    queries,
    key_cache,
    value_cache,
    key_block,
    value_block,
    cache_length_list,
    residual,
    output_weight,
    norm_gain,
    routes,
    route_logits,
    w_gate,
    w_up,
    w_down,
):
    group_results = QUERY_HEADS // KEY_VALUE_HEADS
    shard_worker = lax.axis_index("ep")
    sequence_group_index = shard_worker // KEY_VALUE_HEADS
    head_shard_index = shard_worker % KEY_VALUE_HEADS
    seq_grp = key_cache.shape[1]
    cache_len = key_cache.shape[2]
    rows_per_group = queries.shape[1]
    block_len = rows_per_group // seq_grp
    live_lens = lax.dynamic_slice_in_dim(cache_length_list, sequence_group_index * seq_grp, seq_grp)
    heads_of_query = queries[0].reshape(seq_grp, block_len, group_results, HEAD_SIZE)
    keys_of_block = key_block[0].reshape(seq_grp, block_len, HEAD_SIZE)
    values_of_block = value_block[0].reshape(seq_grp, block_len, HEAD_SIZE)
    score_cache = jnp.einsum(
        "srgd,spd->sgrp", heads_of_query, key_cache[0], preferred_element_type=jnp.float32
    ) / math.sqrt(HEAD_SIZE)
    score_block = jnp.einsum(
        "srgd,spd->sgrp", heads_of_query, keys_of_block, preferred_element_type=jnp.float32
    ) / math.sqrt(HEAD_SIZE)
    position = jnp.arange(cache_len, dtype=jnp.int32)
    live_slots = position[None, :] < live_lens[:, None]
    score_cache = jnp.where(live_slots[:, None, None, :], score_cache, -1e30)
    largest = jnp.maximum(
        jnp.max(score_cache, -1, keepdims=True), jnp.max(score_block, -1, keepdims=True)
    )
    exp_cache = jnp.exp(score_cache - largest)
    exp_block = jnp.exp(score_block - largest)
    denominator = jnp.sum(exp_cache, -1, keepdims=True) + jnp.sum(exp_block, -1, keepdims=True)
    prob_cache = (exp_cache / denominator).astype(jnp.bfloat16)
    prob_block = (exp_block / denominator).astype(jnp.bfloat16)
    mixed_heads = jnp.einsum(
        "sgrp,spd->srgd", prob_cache, value_cache[0], preferred_element_type=jnp.float32
    )
    mixed_heads = mixed_heads + jnp.einsum(
        "sgrp,spd->srgd", prob_block, values_of_block, preferred_element_type=jnp.float32
    )
    attn_rows = mixed_heads.reshape(rows_per_group, group_results * HEAD_SIZE).astype(jnp.bfloat16)
    partial_value = jnp.dot(attn_rows, output_weight[0], preferred_element_type=jnp.float32)
    tree_levels = KEY_VALUE_HEADS.bit_length() - 1
    projected = partial_value.reshape((2,) * tree_levels + (-1, MODEL_WIDTH))
    for bit_pos in range(tree_levels):
        cut = tree_levels - 1 - bit_pos
        low_half = lax.index_in_dim(projected, 0, cut, keepdims=False)
        high_half = lax.index_in_dim(projected, 1, cut, keepdims=False)
        upper_side = head_shard_index >> bit_pos & 1 == 1
        kept_rows = jnp.where(upper_side, high_half, low_half)
        sent_rows = jnp.where(upper_side, low_half, high_half).astype(jnp.bfloat16)
        projected = kept_rows + swapped(sent_rows, "ep", bit_pos).astype(jnp.float32)
    hidden = residual.astype(jnp.float32) + projected
    attended = hidden.astype(jnp.bfloat16)
    normed = (
        hidden * lax.rsqrt(jnp.mean(hidden * hidden, -1, keepdims=True) + EPSILON) * norm_gain
    ).astype(jnp.bfloat16)
    sig_values = jax.nn.sigmoid(route_logits)
    route_weights = ROUTE_SCALE * sig_values / jnp.sum(sig_values, -1, keepdims=True)
    owners = lax.axis_size("ep")
    exp_dev = w_gate.shape[0]
    experts = owners * exp_dev
    row_count = residual.shape[0]
    top_k = routes.shape[1]
    capacity = max(2, 2 * row_count * top_k // experts)
    sends_all = row_count <= capacity and exp_dev == 1 and owners & owners - 1 == 0
    run_experts = every_row if sends_all and 2 * experts <= LANES else routed_rows
    expert_out = run_experts(normed, routes, route_weights, w_gate, w_up, w_down, capacity)
    return (attended, expert_out)


def every_row(normed, routes, route_weights, w_gate, w_up, w_down, capacity):
    owners = lax.axis_size("ep")
    row_count = normed.shape[0]
    ids = jnp.arange(owners, dtype=jnp.int32)
    named = routes[:, :, None] == ids[None, None, :]
    table = jnp.sum(jnp.where(named, route_weights[:, :, None], 0.0), 1)
    high = lax.reduce_precision(table, 8, 7)
    pad = jnp.zeros((row_count, LANES - 2 * owners), jnp.float32)
    extra = jnp.concatenate([high, table - high, pad], 1).astype(jnp.bfloat16)
    packet = jnp.concatenate([normed, extra], 1)
    chips = owners // 2
    mine = [packet] + [exchanged(packet, "ep", 2 * k) for k in range(1, chips)]
    mine = jnp.stack(mine)
    other = exchanged(mine, "ep", 1)
    rows = jnp.stack([mine, other]).reshape(owners * row_count, -1)
    own = (ids == lax.axis_index("ep")).astype(jnp.float32)
    codes = rows[:, MODEL_WIDTH : MODEL_WIDTH + 2 * owners].astype(jnp.float32)
    weight = jnp.sum((codes[:, :owners] + codes[:, owners:]) * own, 1, keepdims=True)
    rows = rows[:, :MODEL_WIDTH]
    gate_part = jnp.dot(rows, w_gate[0], preferred_element_type=jnp.float32)
    up_part = jnp.dot(rows, w_up[0], preferred_element_type=jnp.float32)
    active = (jax.nn.silu(gate_part) * up_part).astype(jnp.bfloat16)
    result = jnp.dot(active, w_down[0], preferred_element_type=jnp.float32) * weight
    result = result.reshape(2, chips, row_count, MODEL_WIDTH)
    back = exchanged(result[1].astype(jnp.bfloat16), "ep", 1).astype(jnp.float32)
    total = result[0] + back
    halves = total.astype(jnp.bfloat16)
    summed = total[0]
    for k in range(1, chips):
        summed = summed + exchanged(halves[k], "ep", 2 * k).astype(jnp.float32)
    return summed.astype(jnp.bfloat16)


def routed_rows(normed, routes, route_weights, w_gate, w_up, w_down, capacity):
    owners = lax.axis_size("ep")
    exp_dev = w_gate.shape[0]
    experts = owners * exp_dev
    row_count = normed.shape[0]
    top_k = routes.shape[1]
    flat_ids = routes.reshape(-1)
    onehot = (flat_ids[:, None] == jnp.arange(experts, dtype=jnp.int32)[None, :]).astype(jnp.int32)
    slot_rank = jnp.sum(jnp.cumsum(onehot, 0) * onehot, 1) - 1
    target = flat_ids * capacity + slot_rank
    source_rows = jnp.repeat(normed, top_k, axis=0)
    outgoing = (
        jnp.zeros((experts * capacity, MODEL_WIDTH), jnp.bfloat16).at[target].set(source_rows)
    )
    outgoing = outgoing.reshape(owners, exp_dev, capacity, MODEL_WIDTH)
    arrived = lax.all_to_all(outgoing, "ep", split_axis=0, concat_axis=0, tiled=True)
    gate_part = jnp.einsum("nesd,edh->nesh", arrived, w_gate, preferred_element_type=jnp.float32)
    up_part = jnp.einsum("nesd,edh->nesh", arrived, w_up, preferred_element_type=jnp.float32)
    active = (jax.nn.silu(gate_part) * up_part).astype(jnp.bfloat16)
    result = jnp.einsum(
        "nesh,ehd->nesd", active, w_down, preferred_element_type=jnp.float32
    ).astype(jnp.bfloat16)
    returned = lax.all_to_all(result, "ep", split_axis=0, concat_axis=0, tiled=True)
    fetched = returned.reshape(experts * capacity, MODEL_WIDTH)[target].reshape(
        row_count, top_k, MODEL_WIDTH
    )
    weighted = jnp.sum(route_weights[:, :, None] * fetched.astype(jnp.float32), 1)
    expert_out = weighted.astype(jnp.bfloat16)
    return expert_out


def solution(mesh):
    return jax.shard_map(
        on_device,
        mesh=mesh,
        in_specs=(
            P(("groups", "ep"), None, None),
            P(("groups", "ep"), None, None, None),
            P(("groups", "ep"), None, None, None),
            P(("groups", "ep"), None, None),
            P(("groups", "ep"), None, None),
            P("groups"),
            P(("groups", "ep"), None),
            P("ep", None, None),
            P(),
            P(("groups", "ep"), None),
            P(("groups", "ep"), None),
            P("ep", None, None),
            P("ep", None, None),
            P("ep", None, None),
        ),
        out_specs=(P(("groups", "ep"), None), P(("groups", "ep"), None)),
        check_vma=False,
    )
```

```python
import math

import jax
import jax.numpy as jnp
from jax import lax
from jax.experimental import pallas as pl
from jax.experimental.pallas import tpu as pltpu
from jax.sharding import PartitionSpec as P

MODEL_WIDTH = 2048
QUERY_HEADS = 16
KEY_VALUE_HEADS = 4
HEAD_SIZE = 128


ROUTE_SCALE = 2.5
EPSILON = 1e-06
LANES = 128
WIDE = MODEL_WIDTH + LANES
CHUNK = 256


def exchanged(block, mask):
    count = lax.axis_size("ep")
    return lax.ppermute(block, "ep", [(index, index ^ mask) for index in range(count)])


def attend_kernel(
    lens_hbm, q_hbm, kc_hbm, vc_hbm, kb_hbm, vb_hbm, res_hbm, routes_hbm, logits_hbm, w_hbm,
    sent, kept,
    lens, q, kc, vc, kb, vb, res, routes, logits, w, attn, sems,
):
    pairs = (
        (lens_hbm, lens), (q_hbm, q), (kb_hbm, kb), (kc_hbm, kc), (vb_hbm, vb), (vc_hbm, vc),
        (routes_hbm, routes), (logits_hbm, logits), (res_hbm, res), (w_hbm, w),
    )
    copies = [pltpu.make_async_copy(a, b, sems.at[i]) for i, (a, b) in enumerate(pairs)]
    for copy in copies:
        copy.start()
    worker = lax.axis_index("ep")
    shard = lax.rem(worker, KEY_VALUE_HEADS)
    group = lax.div(worker, KEY_VALUE_HEADS)
    seqs, slots = kc.shape[1], kc.shape[2]
    block = q.shape[1] // seqs
    heads = q.shape[2] // HEAD_SIZE
    rows = res.shape[0]
    scale = 1.0 / math.sqrt(HEAD_SIZE)
    nt = (((1,), (1,)), ((), ()))
    for copy in copies[:6]:
        copy.wait()
    for t in range(seqs):
        live = lens[group * seqs + t]
        part = slice(t * block, (t + 1) * block)
        queries = jnp.concatenate(
            [q[0, part, g * HEAD_SIZE : (g + 1) * HEAD_SIZE] for g in range(heads)], 0
        )
        cache = lax.dot_general(queries, kc[0, t], nt, preferred_element_type=jnp.float32) * scale
        fresh = lax.dot_general(queries, kb[0, part], nt, preferred_element_type=jnp.float32) * scale
        position = lax.broadcasted_iota(jnp.int32, cache.shape, 1)
        cache = jnp.where(position < live, cache, -1e30)
        largest = jnp.maximum(
            jnp.max(cache, -1, keepdims=True), jnp.max(fresh, -1, keepdims=True)
        )
        cache = jnp.exp(cache - largest)
        fresh = jnp.exp(fresh - largest)
        total = jnp.sum(cache, -1, keepdims=True) + jnp.sum(fresh, -1, keepdims=True)
        share = 1.0 / total
        mixed = jnp.dot(
            (cache * share).astype(jnp.bfloat16), vc[0, t], preferred_element_type=jnp.float32
        ) + jnp.dot(
            (fresh * share).astype(jnp.bfloat16), vb[0, part], preferred_element_type=jnp.float32
        )
        for g in range(heads):
            attn[part, g * HEAD_SIZE : (g + 1) * HEAD_SIZE] = mixed[
                g * block : (g + 1) * block
            ].astype(jnp.bfloat16)
    for copy in copies[6:9]:
        copy.wait()
    experts = lax.axis_size("ep")
    sig = 1.0 / (1.0 + jnp.exp(-logits[...]))
    weights = ROUTE_SCALE * sig / jnp.sum(sig, -1, keepdims=True)
    lane = lax.broadcasted_iota(jnp.int32, (rows, LANES), 1)
    name = jnp.where(lane < experts, lane, lane - experts)
    table = jnp.zeros((rows, LANES), jnp.float32)
    for k in range(routes.shape[1]):
        table = table + jnp.where(routes[:, k : k + 1] == name, weights[:, k : k + 1], 0.0)
    high = table.astype(jnp.bfloat16).astype(jnp.float32)
    kept[:rows, MODEL_WIDTH:] = jnp.where(lane < experts, high, table - high)
    kept[rows:, MODEL_WIDTH:] = jnp.zeros((rows, LANES), jnp.float32)
    sent[:, MODEL_WIDTH:] = jnp.zeros((2 * rows, LANES), jnp.bfloat16)
    copies[9].wait()
    picked = [
        attn[pl.ds(pl.multiple_of((shard ^ mask) * rows, rows), rows), :] for mask in (1, 3, 0, 2)
    ]
    picked = jnp.concatenate(picked, 0)
    for n in range(0, MODEL_WIDTH, 2 * CHUNK):
        cols = slice(n, n + 2 * CHUNK)
        out = jnp.dot(picked, w[0, :, cols], preferred_element_type=jnp.float32)
        sent[:, cols] = out[: 2 * rows].astype(jnp.bfloat16)
        kept[:rows, cols] = out[2 * rows : 3 * rows] + res[:, cols].astype(jnp.float32)
        kept[rows:, cols] = out[3 * rows :]


def norm_kernel(kept, core, chip, gain, attended, packet):
    rows = attended.shape[0]
    for mine in (True, False):
        here = slice(0, rows) if mine else slice(rows, 2 * rows)
        there = slice(rows, 2 * rows) if mine else slice(0, rows)
        hidden = kept[here, :] + core[here, :].astype(jnp.float32) + chip[there, :].astype(jnp.float32)
        table = hidden[:, MODEL_WIDTH:]
        hidden = hidden[:, :MODEL_WIDTH]
        if mine:
            attended[...] = hidden.astype(jnp.bfloat16)
        mean = jnp.sum(hidden * hidden, -1, keepdims=True) * (1.0 / MODEL_WIDTH)
        packet[here, :MODEL_WIDTH] = (hidden * lax.rsqrt(mean + EPSILON) * gain[...]).astype(jnp.bfloat16)
        packet[here, MODEL_WIDTH:] = table.astype(jnp.bfloat16)


def expert_kernel(mine, other, w_gate, w_up, w_down, keep, send, x, act):
    half = mine.shape[0]
    experts = lax.axis_size("ep")
    own = lax.axis_index("ep")
    x[:half, :] = mine[...]
    x[half:, :] = other[...]
    lane = lax.broadcasted_iota(jnp.int32, (2 * half, LANES), 1)
    codes = x[:, MODEL_WIDTH:].astype(jnp.float32)
    chosen = (lane == own) | (lane == own + experts)
    weight = jnp.sum(jnp.where(chosen, codes, 0.0), 1, keepdims=True)
    rows = x[:, :MODEL_WIDTH]
    hidden_units = w_gate.shape[2]
    for n in range(0, hidden_units, CHUNK):
        cols = slice(n, n + CHUNK)
        gate = jnp.dot(rows, w_gate[0, :, cols], preferred_element_type=jnp.float32)
        up = jnp.dot(rows, w_up[0, :, cols], preferred_element_type=jnp.float32)
        act[:, cols] = (gate / (1.0 + jnp.exp(-gate)) * up).astype(jnp.bfloat16)
    for n in range(0, MODEL_WIDTH, CHUNK):
        cols = slice(n, n + CHUNK)
        out = jnp.dot(act[...], w_down[0, :, cols], preferred_element_type=jnp.float32) * weight
        keep[:, cols] = out[:half]
        send[:, cols] = out[half:].astype(jnp.bfloat16)


def every_row(
    queries, key_cache, value_cache, key_block, value_block, cache_length_list, residual,
    output_weight, norm_gain, routes, route_logits, w_gate, w_up, w_down,
):
    rows = residual.shape[0]
    owners = lax.axis_size("ep")
    anywhere = pl.BlockSpec(memory_space=pl.ANY)
    whole = pl.BlockSpec(memory_space=pltpu.VMEM)
    operands = (
        cache_length_list, queries, key_cache, value_cache, key_block, value_block, residual,
        routes, route_logits, output_weight,
    )
    scratch = [pltpu.SMEM(cache_length_list.shape, jnp.int32)]
    scratch += [pltpu.VMEM(a.shape, a.dtype) for a in operands[1:]]
    scratch += [
        pltpu.VMEM((queries.shape[1], queries.shape[2]), jnp.bfloat16),
        pltpu.SemaphoreType.DMA((len(operands),)),
    ]
    sent, kept = pl.pallas_call(
        attend_kernel,
        out_shape=(
            jax.ShapeDtypeStruct((2 * rows, WIDE), jnp.bfloat16),
            jax.ShapeDtypeStruct((2 * rows, WIDE), jnp.float32),
        ),
        in_specs=[anywhere] * len(operands),
        out_specs=(whole, whole),
        scratch_shapes=scratch,
        name="attend",
    )(*operands)
    core = exchanged(sent, 1)
    chip = exchanged((kept + core.astype(jnp.float32)).astype(jnp.bfloat16), 2)
    attended, packet = pl.pallas_call(
        norm_kernel,
        out_shape=(
            jax.ShapeDtypeStruct((rows, MODEL_WIDTH), jnp.bfloat16),
            jax.ShapeDtypeStruct((2 * rows, WIDE), jnp.bfloat16),
        ),
        in_specs=[whole] * 4,
        out_specs=(whole, whole),
        name="norm",
    )(kept, core, chip, norm_gain[None])
    far = exchanged(packet[:rows], 8)
    across = exchanged(packet, 12)
    near = exchanged(packet, 4)
    passed = exchanged(far, 2)
    mine = jnp.concatenate([packet, near, far, passed, across], 0)
    other = exchanged(mine, 1)
    half = mine.shape[0]
    keep, send = pl.pallas_call(
        expert_kernel,
        out_shape=(
            jax.ShapeDtypeStruct((half, MODEL_WIDTH), jnp.float32),
            jax.ShapeDtypeStruct((half, MODEL_WIDTH), jnp.bfloat16),
        ),
        in_specs=[whole] * 5,
        out_specs=(whole, whole),
        scratch_shapes=[
            pltpu.VMEM((2 * half, WIDE), jnp.bfloat16),
            pltpu.VMEM((2 * half, w_gate.shape[2]), jnp.bfloat16),
        ],
        compiler_params=pltpu.CompilerParams(vmem_limit_bytes=40 << 20),
        name="expert",
    )(mine, other, w_gate, w_up, w_down)
    total = keep + exchanged(send, 1).astype(jnp.float32)
    total = total.reshape(owners // 4, 2, rows, MODEL_WIDTH)
    to_chip = total[:, 1].astype(jnp.bfloat16)
    far_sums = total[2:, 0] + exchanged(to_chip[2:], 2).astype(jnp.float32)
    near_sums = total[:2, 0] + exchanged(to_chip[:2], 2).astype(jnp.float32)
    far_sums = far_sums.astype(jnp.bfloat16)
    across = exchanged(far_sums[1], 12)
    far = exchanged(far_sums[0], 8)
    near = exchanged(near_sums[1].astype(jnp.bfloat16), 4)
    summed = near_sums[0] + near.astype(jnp.float32)
    summed = summed + far.astype(jnp.float32) + across.astype(jnp.float32)
    return (attended, summed.astype(jnp.bfloat16))


def swapped(block, axis, distance):
    count = lax.axis_size(axis)
    route = []
    for low in range(count):
        high = low | 1 << distance
        if high != low and high < count:
            route += [(low, high), (high, low)]
    return lax.ppermute(block, axis, route)


def routed_rows(
    queries,
    key_cache,
    value_cache,
    key_block,
    value_block,
    cache_length_list,
    residual,
    output_weight,
    norm_gain,
    routes,
    route_logits,
    w_gate,
    w_up,
    w_down,
):
    group_results = QUERY_HEADS // KEY_VALUE_HEADS
    shard_worker = lax.axis_index("ep")
    sequence_group_index = shard_worker // KEY_VALUE_HEADS
    head_shard_index = shard_worker % KEY_VALUE_HEADS
    seq_grp = key_cache.shape[1]
    cache_len = key_cache.shape[2]
    rows_per_group = queries.shape[1]
    block_len = rows_per_group // seq_grp
    live_lens = lax.dynamic_slice_in_dim(cache_length_list, sequence_group_index * seq_grp, seq_grp)
    heads_of_query = queries[0].reshape(seq_grp, block_len, group_results, HEAD_SIZE)
    keys_of_block = key_block[0].reshape(seq_grp, block_len, HEAD_SIZE)
    values_of_block = value_block[0].reshape(seq_grp, block_len, HEAD_SIZE)
    score_cache = jnp.einsum(
        "srgd,spd->sgrp", heads_of_query, key_cache[0], preferred_element_type=jnp.float32
    ) / math.sqrt(HEAD_SIZE)
    score_block = jnp.einsum(
        "srgd,spd->sgrp", heads_of_query, keys_of_block, preferred_element_type=jnp.float32
    ) / math.sqrt(HEAD_SIZE)
    position = jnp.arange(cache_len, dtype=jnp.int32)
    live_slots = position[None, :] < live_lens[:, None]
    score_cache = jnp.where(live_slots[:, None, None, :], score_cache, -1e30)
    largest = jnp.maximum(
        jnp.max(score_cache, -1, keepdims=True), jnp.max(score_block, -1, keepdims=True)
    )
    exp_cache = jnp.exp(score_cache - largest)
    exp_block = jnp.exp(score_block - largest)
    denominator = jnp.sum(exp_cache, -1, keepdims=True) + jnp.sum(exp_block, -1, keepdims=True)
    prob_cache = (exp_cache / denominator).astype(jnp.bfloat16)
    prob_block = (exp_block / denominator).astype(jnp.bfloat16)
    mixed_heads = jnp.einsum(
        "sgrp,spd->srgd", prob_cache, value_cache[0], preferred_element_type=jnp.float32
    )
    mixed_heads = mixed_heads + jnp.einsum(
        "sgrp,spd->srgd", prob_block, values_of_block, preferred_element_type=jnp.float32
    )
    attn_rows = mixed_heads.reshape(rows_per_group, group_results * HEAD_SIZE).astype(jnp.bfloat16)
    partial_value = jnp.dot(attn_rows, output_weight[0], preferred_element_type=jnp.float32)
    tree_levels = KEY_VALUE_HEADS.bit_length() - 1
    projected = partial_value
    for bit_pos in reversed(range(tree_levels)):
        half_rows = projected.shape[0] // 2
        low_half = projected[:half_rows]
        high_half = projected[half_rows:]
        upper_side = head_shard_index >> bit_pos & 1 == 1
        kept_rows = jnp.where(upper_side, high_half, low_half)
        sent_rows = jnp.where(upper_side, low_half, high_half)
        projected = kept_rows + swapped(sent_rows, "ep", bit_pos)
    hidden = residual.astype(jnp.float32) + projected
    attended = hidden.astype(jnp.bfloat16)
    normed = (
        hidden * lax.rsqrt(jnp.mean(hidden * hidden, -1, keepdims=True) + EPSILON) * norm_gain
    ).astype(jnp.bfloat16)
    sig_values = jax.nn.sigmoid(route_logits)
    route_weights = ROUTE_SCALE * sig_values / jnp.sum(sig_values, -1, keepdims=True)
    owners = lax.axis_size("ep")
    exp_dev = w_gate.shape[0]
    experts = owners * exp_dev
    row_count = residual.shape[0]
    top_k = routes.shape[1]
    capacity = max(2, 2 * row_count * top_k // experts)
    flat_ids = routes.reshape(-1)
    onehot = (flat_ids[:, None] == jnp.arange(experts, dtype=jnp.int32)[None, :]).astype(jnp.int32)
    slot_rank = jnp.sum(jnp.cumsum(onehot, 0) * onehot, 1) - 1
    target = flat_ids * capacity + slot_rank
    source_rows = jnp.repeat(normed, top_k, axis=0)
    outgoing = (
        jnp.zeros((experts * capacity, MODEL_WIDTH), jnp.bfloat16).at[target].set(source_rows)
    )
    outgoing = outgoing.reshape(owners, exp_dev, capacity, MODEL_WIDTH)
    arrived = lax.all_to_all(outgoing, "ep", split_axis=0, concat_axis=0, tiled=True)
    gate_part = jnp.einsum("nesd,edh->nesh", arrived, w_gate, preferred_element_type=jnp.float32)
    up_part = jnp.einsum("nesd,edh->nesh", arrived, w_up, preferred_element_type=jnp.float32)
    active = (jax.nn.silu(gate_part) * up_part).astype(jnp.bfloat16)
    result = jnp.einsum(
        "nesh,ehd->nesd", active, w_down, preferred_element_type=jnp.float32
    ).astype(jnp.bfloat16)
    returned = lax.all_to_all(result, "ep", split_axis=0, concat_axis=0, tiled=True)
    fetched = returned.reshape(experts * capacity, MODEL_WIDTH)[target].reshape(
        row_count, top_k, MODEL_WIDTH
    )
    weighted = jnp.sum(route_weights[:, :, None] * fetched.astype(jnp.float32), 1)
    expert_out = weighted.astype(jnp.bfloat16)
    return (attended, expert_out)


def on_device(*inputs):
    row_count, top_k = inputs[9].shape
    owners = lax.axis_size("ep")
    experts = owners * inputs[11].shape[0]
    capacity = max(2, 2 * row_count * top_k // experts)
    all_rows = row_count <= capacity and experts == owners == 4 * KEY_VALUE_HEADS
    return (every_row if all_rows else routed_rows)(*inputs)


def solution(mesh):
    return jax.shard_map(
        on_device,
        mesh=mesh,
        in_specs=(
            P(("groups", "ep"), None, None),
            P(("groups", "ep"), None, None, None),
            P(("groups", "ep"), None, None, None),
            P(("groups", "ep"), None, None),
            P(("groups", "ep"), None, None),
            P("groups"),
            P(("groups", "ep"), None),
            P("ep", None, None),
            P(),
            P(("groups", "ep"), None),
            P(("groups", "ep"), None),
            P("ep", None, None),
            P("ep", None, None),
            P("ep", None, None),
        ),
        out_specs=(P(("groups", "ep"), None), P(("groups", "ep"), None)),
        check_vma=False,
    )
```

```python
import math

import jax
import jax.numpy as jnp
from jax import lax
from jax.experimental import pallas as pl
from jax.experimental.pallas import tpu as pltpu
from jax.sharding import PartitionSpec as P

MODEL_WIDTH = 2048
QUERY_HEADS = 16
KEY_VALUE_HEADS = 4
HEAD_SIZE = 128


ROUTE_SCALE = 2.5
EPSILON = 1e-06
LANES = 128
WIDE = MODEL_WIDTH + LANES
CHUNK = 256


def exchanged(block, mask):
    count = lax.axis_size("ep")
    return lax.ppermute(block, "ep", [(index, index ^ mask) for index in range(count)])


def attend_kernel(
    lens_hbm, q_hbm, kc_hbm, vc_hbm, kb_hbm, vb_hbm, res_hbm, routes_hbm, logits_hbm, w_hbm,
    sent, kept,
    lens, q, kc, vc, kb, vb, res, routes, logits, w, attn, sems,
):
    pairs = (
        (lens_hbm, lens), (q_hbm, q), (kb_hbm, kb), (kc_hbm, kc), (vb_hbm, vb), (vc_hbm, vc),
        (routes_hbm, routes), (logits_hbm, logits), (res_hbm, res), (w_hbm, w),
    )
    copies = [pltpu.make_async_copy(a, b, sems.at[i]) for i, (a, b) in enumerate(pairs)]
    for copy in copies:
        copy.start()
    worker = lax.axis_index("ep")
    shard = lax.rem(worker, KEY_VALUE_HEADS)
    group = lax.div(worker, KEY_VALUE_HEADS)
    seqs, slots = kc.shape[1], kc.shape[2]
    block = q.shape[1] // seqs
    heads = q.shape[2] // HEAD_SIZE
    rows = res.shape[0]
    scale = 1.0 / math.sqrt(HEAD_SIZE)
    nt = (((1,), (1,)), ((), ()))
    for copy in copies[:6]:
        copy.wait()
    for t in range(seqs):
        live = lens[group * seqs + t]
        part = slice(t * block, (t + 1) * block)
        queries = jnp.concatenate(
            [q[0, part, g * HEAD_SIZE : (g + 1) * HEAD_SIZE] for g in range(heads)], 0
        )
        cache = lax.dot_general(queries, kc[0, t], nt, preferred_element_type=jnp.float32) * scale
        fresh = lax.dot_general(queries, kb[0, part], nt, preferred_element_type=jnp.float32) * scale
        position = lax.broadcasted_iota(jnp.int32, cache.shape, 1)
        cache = jnp.where(position < live, cache, -1e30)
        largest = jnp.maximum(
            jnp.max(cache, -1, keepdims=True), jnp.max(fresh, -1, keepdims=True)
        )
        cache = jnp.exp(cache - largest)
        fresh = jnp.exp(fresh - largest)
        total = jnp.sum(cache, -1, keepdims=True) + jnp.sum(fresh, -1, keepdims=True)
        share = 1.0 / total
        mixed = jnp.dot(
            (cache * share).astype(jnp.bfloat16), vc[0, t], preferred_element_type=jnp.float32
        ) + jnp.dot(
            (fresh * share).astype(jnp.bfloat16), vb[0, part], preferred_element_type=jnp.float32
        )
        for g in range(heads):
            attn[part, g * HEAD_SIZE : (g + 1) * HEAD_SIZE] = mixed[
                g * block : (g + 1) * block
            ].astype(jnp.bfloat16)
    for copy in copies[6:9]:
        copy.wait()
    experts = lax.axis_size("ep")
    sig = 1.0 / (1.0 + jnp.exp(-logits[...]))
    weights = ROUTE_SCALE * sig / jnp.sum(sig, 0, keepdims=True)
    line = lax.broadcasted_iota(jnp.int32, (LANES, rows), 0)
    name = jnp.where(line < experts, line, line - experts)
    table = jnp.zeros((LANES, rows), jnp.float32)
    for k in range(routes.shape[0]):
        table = table + jnp.where(routes[k : k + 1, :] == name, weights[k : k + 1, :], 0.0)
    high = table.astype(jnp.bfloat16).astype(jnp.float32)
    table = jnp.where(line < experts, high, table - high).astype(jnp.bfloat16)
    row = lax.broadcasted_iota(jnp.int32, (rows, rows), 0)
    unit = jnp.where(row == lax.broadcasted_iota(jnp.int32, (rows, rows), 1), 1.0, 0.0)
    kept[:rows, MODEL_WIDTH:] = lax.dot_general(
        unit.astype(jnp.bfloat16), table, nt, preferred_element_type=jnp.float32
    )
    kept[rows:, MODEL_WIDTH:] = jnp.zeros((rows, LANES), jnp.float32)
    sent[:, MODEL_WIDTH:] = jnp.zeros((2 * rows, LANES), jnp.bfloat16)
    copies[9].wait()
    picked = [
        attn[pl.ds(pl.multiple_of((shard ^ mask) * rows, rows), rows), :] for mask in (1, 3, 0, 2)
    ]
    picked = jnp.concatenate(picked, 0)
    for n in range(0, MODEL_WIDTH, 2 * CHUNK):
        cols = slice(n, n + 2 * CHUNK)
        out = jnp.dot(picked, w[0, :, cols], preferred_element_type=jnp.float32)
        sent[:, cols] = out[: 2 * rows].astype(jnp.bfloat16)
        kept[:rows, cols] = out[2 * rows : 3 * rows] + res[:, cols].astype(jnp.float32)
        kept[rows:, cols] = out[3 * rows :]


def norm_kernel(kept, core, chip, gain, attended, packet):
    rows = attended.shape[0]
    for mine in (True, False):
        here = slice(0, rows) if mine else slice(rows, 2 * rows)
        there = slice(rows, 2 * rows) if mine else slice(0, rows)
        hidden = kept[here, :] + core[here, :].astype(jnp.float32) + chip[there, :].astype(jnp.float32)
        table = hidden[:, MODEL_WIDTH:]
        hidden = hidden[:, :MODEL_WIDTH]
        if mine:
            attended[...] = hidden.astype(jnp.bfloat16)
        mean = jnp.sum(hidden * hidden, -1, keepdims=True) * (1.0 / MODEL_WIDTH)
        packet[here, :MODEL_WIDTH] = (hidden * lax.rsqrt(mean + EPSILON) * gain[...]).astype(jnp.bfloat16)
        packet[here, MODEL_WIDTH:] = table.astype(jnp.bfloat16)


def expert_kernel(mine, other, w_gate, w_up, w_down, keep, send, x, act):
    half = mine.shape[0]
    experts = lax.axis_size("ep")
    own = lax.axis_index("ep")
    x[:half, :] = mine[...]
    x[half:, :] = other[...]
    lane = lax.broadcasted_iota(jnp.int32, (2 * half, LANES), 1)
    codes = x[:, MODEL_WIDTH:].astype(jnp.float32)
    chosen = (lane == own) | (lane == own + experts)
    weight = jnp.sum(jnp.where(chosen, codes, 0.0), 1, keepdims=True)
    rows = x[:, :MODEL_WIDTH]
    hidden_units = w_gate.shape[2]
    for n in range(0, hidden_units, CHUNK):
        cols = slice(n, n + CHUNK)
        gate = jnp.dot(rows, w_gate[0, :, cols], preferred_element_type=jnp.float32)
        up = jnp.dot(rows, w_up[0, :, cols], preferred_element_type=jnp.float32)
        act[:, cols] = (gate / (1.0 + jnp.exp(-gate)) * up).astype(jnp.bfloat16)
    for n in range(0, MODEL_WIDTH, CHUNK):
        cols = slice(n, n + CHUNK)
        out = jnp.dot(act[...], w_down[0, :, cols], preferred_element_type=jnp.float32) * weight
        keep[:, cols] = out[:half]
        send[:, cols] = out[half:].astype(jnp.bfloat16)


def every_row(
    queries, key_cache, value_cache, key_block, value_block, cache_length_list, residual,
    output_weight, norm_gain, routes, route_logits, w_gate, w_up, w_down,
):
    rows = residual.shape[0]
    owners = lax.axis_size("ep")
    anywhere = pl.BlockSpec(memory_space=pl.ANY)
    whole = pl.BlockSpec(memory_space=pltpu.VMEM)
    operands = (
        cache_length_list, queries, key_cache, value_cache, key_block, value_block, residual,
        routes.T, route_logits.T, output_weight,
    )
    operands = tuple(pltpu.with_memory_space_constraint(a, pltpu.HBM) for a in operands)
    scratch = [pltpu.SMEM(cache_length_list.shape, jnp.int32)]
    scratch += [pltpu.VMEM(a.shape, a.dtype) for a in operands[1:]]
    scratch += [
        pltpu.VMEM((queries.shape[1], queries.shape[2]), jnp.bfloat16),
        pltpu.SemaphoreType.DMA((len(operands),)),
    ]
    sent, kept = pl.pallas_call(
        attend_kernel,
        out_shape=(
            jax.ShapeDtypeStruct((2 * rows, WIDE), jnp.bfloat16),
            jax.ShapeDtypeStruct((2 * rows, WIDE), jnp.float32),
        ),
        in_specs=[anywhere] * len(operands),
        out_specs=(whole, whole),
        scratch_shapes=scratch,
        compiler_params=pltpu.CompilerParams(vmem_limit_bytes=12 << 20),
        cost_estimate=pl.CostEstimate(flops=1 << 30, bytes_accessed=1 << 23, transcendentals=1 << 18),
        name="attend",
    )(*operands)
    sent, w_gate, w_up, w_down = lax.optimization_barrier((sent, w_gate, w_up, w_down))
    core = exchanged(sent, 1)
    chip = exchanged((kept + core.astype(jnp.float32)).astype(jnp.bfloat16), 2)
    attended, packet = pl.pallas_call(
        norm_kernel,
        out_shape=(
            jax.ShapeDtypeStruct((rows, MODEL_WIDTH), jnp.bfloat16),
            jax.ShapeDtypeStruct((2 * rows, WIDE), jnp.bfloat16),
        ),
        in_specs=[whole] * 4,
        out_specs=(whole, whole),
        compiler_params=pltpu.CompilerParams(vmem_limit_bytes=6 << 20),
        cost_estimate=pl.CostEstimate(flops=1 << 34, bytes_accessed=1 << 21, transcendentals=1 << 10),
        name="norm",
    )(kept, core, chip, norm_gain[None])
    far = exchanged(packet[:rows], 8)
    across = exchanged(packet, 12)
    near = exchanged(packet, 4)
    passed = exchanged(far, 2)
    mine = jnp.concatenate([packet, near, far, passed, across], 0)
    other = exchanged(mine, 1)
    half = mine.shape[0]
    keep, send = pl.pallas_call(
        expert_kernel,
        out_shape=(
            jax.ShapeDtypeStruct((half, MODEL_WIDTH), jnp.float32),
            jax.ShapeDtypeStruct((half, MODEL_WIDTH), jnp.bfloat16),
        ),
        in_specs=[whole] * 5,
        out_specs=(whole, whole),
        scratch_shapes=[
            pltpu.VMEM((2 * half, WIDE), jnp.bfloat16),
            pltpu.VMEM((2 * half, w_gate.shape[2]), jnp.bfloat16),
        ],
        compiler_params=pltpu.CompilerParams(vmem_limit_bytes=12 << 20),
        cost_estimate=pl.CostEstimate(flops=1 << 31, bytes_accessed=1 << 23, transcendentals=1 << 18),
        name="expert",
    )(mine, other, w_gate, w_up, w_down)
    total = keep + exchanged(send, 1).astype(jnp.float32)
    total = total.reshape(owners // 4, 2, rows, MODEL_WIDTH)
    to_chip = total[:, 1].astype(jnp.bfloat16)
    far_sums = total[2:, 0] + exchanged(to_chip[2:], 2).astype(jnp.float32)
    near_sums = total[:2, 0] + exchanged(to_chip[:2], 2).astype(jnp.float32)
    far_sums = far_sums.astype(jnp.bfloat16)
    across = exchanged(far_sums[1], 12)
    far = exchanged(far_sums[0], 8)
    near = exchanged(near_sums[1].astype(jnp.bfloat16), 4)
    summed = near_sums[0] + near.astype(jnp.float32)
    summed = summed + far.astype(jnp.float32) + across.astype(jnp.float32)
    return (attended, summed.astype(jnp.bfloat16))


def swapped(block, axis, distance):
    count = lax.axis_size(axis)
    route = []
    for low in range(count):
        high = low | 1 << distance
        if high != low and high < count:
            route += [(low, high), (high, low)]
    return lax.ppermute(block, axis, route)


def routed_rows(
    queries,
    key_cache,
    value_cache,
    key_block,
    value_block,
    cache_length_list,
    residual,
    output_weight,
    norm_gain,
    routes,
    route_logits,
    w_gate,
    w_up,
    w_down,
):
    group_results = QUERY_HEADS // KEY_VALUE_HEADS
    shard_worker = lax.axis_index("ep")
    sequence_group_index = shard_worker // KEY_VALUE_HEADS
    head_shard_index = shard_worker % KEY_VALUE_HEADS
    seq_grp = key_cache.shape[1]
    cache_len = key_cache.shape[2]
    rows_per_group = queries.shape[1]
    block_len = rows_per_group // seq_grp
    live_lens = lax.dynamic_slice_in_dim(cache_length_list, sequence_group_index * seq_grp, seq_grp)
    heads_of_query = queries[0].reshape(seq_grp, block_len, group_results, HEAD_SIZE)
    keys_of_block = key_block[0].reshape(seq_grp, block_len, HEAD_SIZE)
    values_of_block = value_block[0].reshape(seq_grp, block_len, HEAD_SIZE)
    score_cache = jnp.einsum(
        "srgd,spd->sgrp", heads_of_query, key_cache[0], preferred_element_type=jnp.float32
    ) / math.sqrt(HEAD_SIZE)
    score_block = jnp.einsum(
        "srgd,spd->sgrp", heads_of_query, keys_of_block, preferred_element_type=jnp.float32
    ) / math.sqrt(HEAD_SIZE)
    position = jnp.arange(cache_len, dtype=jnp.int32)
    live_slots = position[None, :] < live_lens[:, None]
    score_cache = jnp.where(live_slots[:, None, None, :], score_cache, -1e30)
    largest = jnp.maximum(
        jnp.max(score_cache, -1, keepdims=True), jnp.max(score_block, -1, keepdims=True)
    )
    exp_cache = jnp.exp(score_cache - largest)
    exp_block = jnp.exp(score_block - largest)
    denominator = jnp.sum(exp_cache, -1, keepdims=True) + jnp.sum(exp_block, -1, keepdims=True)
    prob_cache = (exp_cache / denominator).astype(jnp.bfloat16)
    prob_block = (exp_block / denominator).astype(jnp.bfloat16)
    mixed_heads = jnp.einsum(
        "sgrp,spd->srgd", prob_cache, value_cache[0], preferred_element_type=jnp.float32
    )
    mixed_heads = mixed_heads + jnp.einsum(
        "sgrp,spd->srgd", prob_block, values_of_block, preferred_element_type=jnp.float32
    )
    attn_rows = mixed_heads.reshape(rows_per_group, group_results * HEAD_SIZE).astype(jnp.bfloat16)
    partial_value = jnp.dot(attn_rows, output_weight[0], preferred_element_type=jnp.float32)
    tree_levels = KEY_VALUE_HEADS.bit_length() - 1
    projected = partial_value
    for bit_pos in reversed(range(tree_levels)):
        half_rows = projected.shape[0] // 2
        low_half = projected[:half_rows]
        high_half = projected[half_rows:]
        upper_side = head_shard_index >> bit_pos & 1 == 1
        kept_rows = jnp.where(upper_side, high_half, low_half)
        sent_rows = jnp.where(upper_side, low_half, high_half)
        projected = kept_rows + swapped(sent_rows, "ep", bit_pos)
    hidden = residual.astype(jnp.float32) + projected
    attended = hidden.astype(jnp.bfloat16)
    normed = (
        hidden * lax.rsqrt(jnp.mean(hidden * hidden, -1, keepdims=True) + EPSILON) * norm_gain
    ).astype(jnp.bfloat16)
    sig_values = jax.nn.sigmoid(route_logits)
    route_weights = ROUTE_SCALE * sig_values / jnp.sum(sig_values, -1, keepdims=True)
    owners = lax.axis_size("ep")
    exp_dev = w_gate.shape[0]
    experts = owners * exp_dev
    row_count = residual.shape[0]
    top_k = routes.shape[1]
    capacity = max(2, 2 * row_count * top_k // experts)
    flat_ids = routes.reshape(-1)
    onehot = (flat_ids[:, None] == jnp.arange(experts, dtype=jnp.int32)[None, :]).astype(jnp.int32)
    slot_rank = jnp.sum(jnp.cumsum(onehot, 0) * onehot, 1) - 1
    target = flat_ids * capacity + slot_rank
    source_rows = jnp.repeat(normed, top_k, axis=0)
    outgoing = (
        jnp.zeros((experts * capacity, MODEL_WIDTH), jnp.bfloat16).at[target].set(source_rows)
    )
    outgoing = outgoing.reshape(owners, exp_dev, capacity, MODEL_WIDTH)
    arrived = lax.all_to_all(outgoing, "ep", split_axis=0, concat_axis=0, tiled=True)
    gate_part = jnp.einsum("nesd,edh->nesh", arrived, w_gate, preferred_element_type=jnp.float32)
    up_part = jnp.einsum("nesd,edh->nesh", arrived, w_up, preferred_element_type=jnp.float32)
    active = (jax.nn.silu(gate_part) * up_part).astype(jnp.bfloat16)
    result = jnp.einsum(
        "nesh,ehd->nesd", active, w_down, preferred_element_type=jnp.float32
    ).astype(jnp.bfloat16)
    returned = lax.all_to_all(result, "ep", split_axis=0, concat_axis=0, tiled=True)
    fetched = returned.reshape(experts * capacity, MODEL_WIDTH)[target].reshape(
        row_count, top_k, MODEL_WIDTH
    )
    weighted = jnp.sum(route_weights[:, :, None] * fetched.astype(jnp.float32), 1)
    expert_out = weighted.astype(jnp.bfloat16)
    return (attended, expert_out)


def on_device(*inputs):
    row_count, top_k = inputs[9].shape
    owners = lax.axis_size("ep")
    experts = owners * inputs[11].shape[0]
    capacity = max(2, 2 * row_count * top_k // experts)
    all_rows = row_count <= capacity and experts == owners == 4 * KEY_VALUE_HEADS
    return (every_row if all_rows else routed_rows)(*inputs)


def solution(mesh):
    return jax.shard_map(
        on_device,
        mesh=mesh,
        in_specs=(
            P(("groups", "ep"), None, None),
            P(("groups", "ep"), None, None, None),
            P(("groups", "ep"), None, None, None),
            P(("groups", "ep"), None, None),
            P(("groups", "ep"), None, None),
            P("groups"),
            P(("groups", "ep"), None),
            P("ep", None, None),
            P(),
            P(("groups", "ep"), None),
            P(("groups", "ep"), None),
            P("ep", None, None),
            P("ep", None, None),
            P("ep", None, None),
        ),
        out_specs=(P(("groups", "ep"), None), P(("groups", "ep"), None)),
        check_vma=False,
    )
```

```python
import functools
import math

import jax
import jax.numpy as jnp
from jax import lax
from jax.experimental import pallas as pl
from jax.experimental.pallas import tpu as pltpu
from jax.sharding import PartitionSpec as P


MODEL_WIDTH = 2048
QUERY_HEADS = 16
KEY_VALUE_HEADS = 4
HEAD_SIZE = 128


ROUTE_SCALE = 2.5
EPSILON = 1e-06
LANES = 128
WIDE = MODEL_WIDTH + LANES
CHUNK = 256


def exchanged(block, mask):
    count = lax.axis_size("ep")
    return lax.ppermute(block, "ep", [(index, index ^ mask) for index in range(count)])


def attend_kernel(
    lens_hbm, q_hbm, kc_hbm, vc_hbm, kb_hbm, vb_hbm, res_hbm, routes_hbm, logits_hbm, w_hbm,
    sent, kept,
    lens, q, kc, vc, kb, vb, res, routes, logits, w, attn, sems,
):
    pairs = (
        (lens_hbm, lens), (q_hbm, q), (kb_hbm, kb), (kc_hbm, kc), (vb_hbm, vb), (vc_hbm, vc),
        (routes_hbm, routes), (logits_hbm, logits), (res_hbm, res), (w_hbm, w),
    )
    copies = [pltpu.make_async_copy(a, b, sems.at[i]) for i, (a, b) in enumerate(pairs)]
    for copy in copies:
        copy.start()
    worker = lax.axis_index("ep")
    shard = lax.rem(worker, KEY_VALUE_HEADS)
    group = lax.div(worker, KEY_VALUE_HEADS)
    seqs = kc.shape[1]
    block = q.shape[1] // seqs
    heads = q.shape[2] // HEAD_SIZE
    rows = res.shape[0]
    scale = 1.0 / math.sqrt(HEAD_SIZE)
    nt = (((1,), (1,)), ((), ()))
    for copy in copies[:6]:
        copy.wait()
    for t in range(seqs):
        live = lens[group * seqs + t]
        part = slice(t * block, (t + 1) * block)
        queries = jnp.concatenate(
            [q[0, part, g * HEAD_SIZE : (g + 1) * HEAD_SIZE] for g in range(heads)], 0
        )
        cache = lax.dot_general(queries, kc[0, t], nt, preferred_element_type=jnp.float32) * scale
        fresh = lax.dot_general(queries, kb[0, part], nt, preferred_element_type=jnp.float32) * scale
        position = lax.broadcasted_iota(jnp.int32, cache.shape, 1)
        cache = jnp.where(position < live, cache, -1e30)
        largest = jnp.maximum(
            jnp.max(cache, -1, keepdims=True), jnp.max(fresh, -1, keepdims=True)
        )
        cache = jnp.exp(cache - largest)
        fresh = jnp.exp(fresh - largest)
        total = jnp.sum(cache, -1, keepdims=True) + jnp.sum(fresh, -1, keepdims=True)
        share = 1.0 / total
        mixed = jnp.dot(
            (cache * share).astype(jnp.bfloat16), vc[0, t], preferred_element_type=jnp.float32
        ) + jnp.dot(
            (fresh * share).astype(jnp.bfloat16), vb[0, part], preferred_element_type=jnp.float32
        )
        for g in range(heads):
            attn[part, g * HEAD_SIZE : (g + 1) * HEAD_SIZE] = mixed[
                g * block : (g + 1) * block
            ].astype(jnp.bfloat16)
    for copy in copies[6:9]:
        copy.wait()
    experts = lax.axis_size("ep")
    sig = 1.0 / (1.0 + jnp.exp(-logits[...]))
    weights = ROUTE_SCALE * sig / jnp.sum(sig, 0, keepdims=True)
    line = lax.broadcasted_iota(jnp.int32, (LANES, rows), 0)
    name = jnp.where(line < experts, line, line - experts)
    table = jnp.zeros((LANES, rows), jnp.float32)
    for k in range(routes.shape[0]):
        table = table + jnp.where(routes[k : k + 1, :] == name, weights[k : k + 1, :], 0.0)
    high = table.astype(jnp.bfloat16).astype(jnp.float32)
    table = jnp.where(line < experts, high, table - high).astype(jnp.bfloat16)
    row = lax.broadcasted_iota(jnp.int32, (rows, rows), 0)
    unit = jnp.where(row == lax.broadcasted_iota(jnp.int32, (rows, rows), 1), 1.0, 0.0)
    kept[:rows, MODEL_WIDTH:] = lax.dot_general(
        unit.astype(jnp.bfloat16), table, nt, preferred_element_type=jnp.float32
    )
    kept[rows:, MODEL_WIDTH:] = jnp.zeros((rows, LANES), jnp.float32)
    sent[:, MODEL_WIDTH:] = jnp.zeros((2 * rows, LANES), jnp.bfloat16)
    copies[9].wait()
    picked = [
        attn[pl.ds(pl.multiple_of((shard ^ mask) * rows, rows), rows), :] for mask in (1, 3, 0, 2)
    ]
    picked = jnp.concatenate(picked, 0)
    for n in range(0, MODEL_WIDTH, 2 * CHUNK):
        cols = slice(n, n + 2 * CHUNK)
        out = jnp.dot(picked, w[0, :, cols], preferred_element_type=jnp.float32)
        sent[:, cols] = out[: 2 * rows].astype(jnp.bfloat16)
        kept[:rows, cols] = out[2 * rows : 3 * rows] + res[:, cols].astype(jnp.float32)
        kept[rows:, cols] = out[3 * rows :]


def norm_kernel(block, kept, core, chip, gain, *outs):
    packet = outs[-1]
    rows = packet.shape[0]
    here = slice(block * rows, (block + 1) * rows)
    hidden = kept[here, :] + core[here, :].astype(jnp.float32) + chip[...].astype(jnp.float32)
    table = hidden[:, MODEL_WIDTH:]
    hidden = hidden[:, :MODEL_WIDTH]
    if block == 0:
        outs[0][...] = hidden.astype(jnp.bfloat16)
    mean = jnp.sum(hidden * hidden, -1, keepdims=True) * (1.0 / MODEL_WIDTH)
    packet[:, :MODEL_WIDTH] = (hidden * lax.rsqrt(mean + EPSILON) * gain[...]).astype(jnp.bfloat16)
    packet[:, MODEL_WIDTH:] = table.astype(jnp.bfloat16)


def expert_kernel(mine, other, w_gate, w_up, w_down, keep, send, x, act):
    half = mine.shape[0]
    experts = lax.axis_size("ep")
    own = lax.axis_index("ep")
    x[:half, :] = mine[...]
    x[half:, :] = other[...]
    lane = lax.broadcasted_iota(jnp.int32, (2 * half, LANES), 1)
    codes = x[:, MODEL_WIDTH:].astype(jnp.float32)
    chosen = (lane == own) | (lane == own + experts)
    weight = jnp.sum(jnp.where(chosen, codes, 0.0), 1, keepdims=True)
    rows = x[:, :MODEL_WIDTH]
    hidden_units = w_gate.shape[2]
    for n in range(0, hidden_units, CHUNK):
        cols = slice(n, n + CHUNK)
        gate = jnp.dot(rows, w_gate[0, :, cols], preferred_element_type=jnp.float32)
        up = jnp.dot(rows, w_up[0, :, cols], preferred_element_type=jnp.float32)
        act[:, cols] = (gate / (1.0 + jnp.exp(-gate)) * up).astype(jnp.bfloat16)
    for n in range(0, MODEL_WIDTH, CHUNK):
        cols = slice(n, n + CHUNK)
        out = jnp.dot(act[...], w_down[0, :, cols], preferred_element_type=jnp.float32) * weight
        keep[:, cols] = out[:half]
        send[:, cols] = out[half:].astype(jnp.bfloat16)


def every_row(
    queries, key_cache, value_cache, key_block, value_block, cache_length_list, residual,
    output_weight, norm_gain, routes, route_logits, w_gate, w_up, w_down,
):
    rows = residual.shape[0]
    owners = lax.axis_size("ep")
    anywhere = pl.BlockSpec(memory_space=pl.ANY)
    whole = pl.BlockSpec(memory_space=pltpu.VMEM)
    operands = (
        cache_length_list, queries, key_cache, value_cache, key_block, value_block, residual,
        routes.T, route_logits.T, output_weight,
    )
    operands = tuple(pltpu.with_memory_space_constraint(a, pltpu.HBM) for a in operands)
    scratch = [pltpu.SMEM(cache_length_list.shape, jnp.int32)]
    scratch += [pltpu.VMEM(a.shape, a.dtype) for a in operands[1:]]
    scratch += [
        pltpu.VMEM((queries.shape[1], queries.shape[2]), jnp.bfloat16),
        pltpu.SemaphoreType.DMA((len(operands),)),
    ]
    sent, kept = pl.pallas_call(
        attend_kernel,
        out_shape=(
            jax.ShapeDtypeStruct((2 * rows, WIDE), jnp.bfloat16),
            jax.ShapeDtypeStruct((2 * rows, WIDE), jnp.float32),
        ),
        in_specs=[anywhere] * len(operands),
        out_specs=(whole, whole),
        scratch_shapes=scratch,
        compiler_params=pltpu.CompilerParams(vmem_limit_bytes=12 << 20),
        cost_estimate=pl.CostEstimate(flops=1 << 30, bytes_accessed=1 << 23, transcendentals=1 << 18),
        name="attend",
    )(*operands)
    sent, w_gate, w_up, w_down = lax.optimization_barrier((sent, w_gate, w_up, w_down))
    core = exchanged(sent, 1)
    sums = (kept + core.astype(jnp.float32)).astype(jnp.bfloat16)
    chip_own = exchanged(sums[rows:], 2)
    chip_pair = exchanged(sums[:rows], 2)

    def normed(block, chip):
        outs = (jax.ShapeDtypeStruct((rows, MODEL_WIDTH), jnp.bfloat16),) * (block == 0)
        outs += (jax.ShapeDtypeStruct((rows, WIDE), jnp.bfloat16),)
        return pl.pallas_call(
            functools.partial(norm_kernel, block),
            out_shape=outs,
            in_specs=[whole] * 4,
            out_specs=(whole,) * len(outs),
            compiler_params=pltpu.CompilerParams(vmem_limit_bytes=6 << 20),
            cost_estimate=pl.CostEstimate(
                flops=1 << 34, bytes_accessed=1 << 20, transcendentals=1 << 10
            ),
            name="norm",
        )(kept, core, chip, norm_gain[None])

    attended, own = normed(0, chip_own)
    far = exchanged(own, 8)
    (pair,) = normed(1, chip_pair)
    packet = jnp.concatenate([own, pair], 0)
    across = exchanged(packet, 12)
    near = exchanged(packet, 4)
    passed = exchanged(far, 2)
    mine = jnp.concatenate([packet, near, far, passed, across], 0)
    other = exchanged(mine, 1)
    half = mine.shape[0]
    keep, send = pl.pallas_call(
        expert_kernel,
        out_shape=(
            jax.ShapeDtypeStruct((half, MODEL_WIDTH), jnp.float32),
            jax.ShapeDtypeStruct((half, MODEL_WIDTH), jnp.bfloat16),
        ),
        in_specs=[whole] * 5,
        out_specs=(whole, whole),
        scratch_shapes=[
            pltpu.VMEM((2 * half, WIDE), jnp.bfloat16),
            pltpu.VMEM((2 * half, w_gate.shape[2]), jnp.bfloat16),
        ],
        compiler_params=pltpu.CompilerParams(vmem_limit_bytes=12 << 20),
        cost_estimate=pl.CostEstimate(flops=1 << 31, bytes_accessed=1 << 23, transcendentals=1 << 18),
        name="expert",
    )(mine, other, w_gate, w_up, w_down)
    total = keep + exchanged(send, 1).astype(jnp.float32)
    total = total.reshape(owners // 4, 2, rows, MODEL_WIDTH)
    to_chip = total[:, 1].astype(jnp.bfloat16)
    got_far = exchanged(to_chip[2:], 2)
    got_near = exchanged(to_chip[:2], 2)
    far_sums = (total[2:, 0] + got_far.astype(jnp.float32)).astype(jnp.bfloat16)
    across = exchanged(far_sums[1], 12)
    far = exchanged(far_sums[0], 8)
    near_sum = (total[1, 0] + got_near[1].astype(jnp.float32)).astype(jnp.bfloat16)
    near = exchanged(near_sum, 4)
    summed = total[0, 0] + got_near[0].astype(jnp.float32) + near.astype(jnp.float32)
    summed = summed + far.astype(jnp.float32) + across.astype(jnp.float32)
    return (attended, summed.astype(jnp.bfloat16))


def swapped(block, axis, distance):
    count = lax.axis_size(axis)
    route = []
    for low in range(count):
        high = low | 1 << distance
        if high != low and high < count:
            route += [(low, high), (high, low)]
    return lax.ppermute(block, axis, route)


def routed_rows(
    queries,
    key_cache,
    value_cache,
    key_block,
    value_block,
    cache_length_list,
    residual,
    output_weight,
    norm_gain,
    routes,
    route_logits,
    w_gate,
    w_up,
    w_down,
):
    group_results = QUERY_HEADS // KEY_VALUE_HEADS
    shard_worker = lax.axis_index("ep")
    sequence_group_index = shard_worker // KEY_VALUE_HEADS
    head_shard_index = shard_worker % KEY_VALUE_HEADS
    seq_grp = key_cache.shape[1]
    cache_len = key_cache.shape[2]
    rows_per_group = queries.shape[1]
    block_len = rows_per_group // seq_grp
    live_lens = lax.dynamic_slice_in_dim(cache_length_list, sequence_group_index * seq_grp, seq_grp)
    heads_of_query = queries[0].reshape(seq_grp, block_len, group_results, HEAD_SIZE)
    keys_of_block = key_block[0].reshape(seq_grp, block_len, HEAD_SIZE)
    values_of_block = value_block[0].reshape(seq_grp, block_len, HEAD_SIZE)
    score_cache = jnp.einsum(
        "srgd,spd->sgrp", heads_of_query, key_cache[0], preferred_element_type=jnp.float32
    ) / math.sqrt(HEAD_SIZE)
    score_block = jnp.einsum(
        "srgd,spd->sgrp", heads_of_query, keys_of_block, preferred_element_type=jnp.float32
    ) / math.sqrt(HEAD_SIZE)
    position = jnp.arange(cache_len, dtype=jnp.int32)
    live_slots = position[None, :] < live_lens[:, None]
    score_cache = jnp.where(live_slots[:, None, None, :], score_cache, -1e30)
    largest = jnp.maximum(
        jnp.max(score_cache, -1, keepdims=True), jnp.max(score_block, -1, keepdims=True)
    )
    exp_cache = jnp.exp(score_cache - largest)
    exp_block = jnp.exp(score_block - largest)
    denominator = jnp.sum(exp_cache, -1, keepdims=True) + jnp.sum(exp_block, -1, keepdims=True)
    prob_cache = (exp_cache / denominator).astype(jnp.bfloat16)
    prob_block = (exp_block / denominator).astype(jnp.bfloat16)
    mixed_heads = jnp.einsum(
        "sgrp,spd->srgd", prob_cache, value_cache[0], preferred_element_type=jnp.float32
    )
    mixed_heads = mixed_heads + jnp.einsum(
        "sgrp,spd->srgd", prob_block, values_of_block, preferred_element_type=jnp.float32
    )
    attn_rows = mixed_heads.reshape(rows_per_group, group_results * HEAD_SIZE).astype(jnp.bfloat16)
    partial_value = jnp.dot(attn_rows, output_weight[0], preferred_element_type=jnp.float32)
    tree_levels = KEY_VALUE_HEADS.bit_length() - 1
    projected = partial_value
    for bit_pos in reversed(range(tree_levels)):
        half_rows = projected.shape[0] // 2
        low_half = projected[:half_rows]
        high_half = projected[half_rows:]
        upper_side = head_shard_index >> bit_pos & 1 == 1
        kept_rows = jnp.where(upper_side, high_half, low_half)
        sent_rows = jnp.where(upper_side, low_half, high_half)
        projected = kept_rows + swapped(sent_rows, "ep", bit_pos)
    hidden = residual.astype(jnp.float32) + projected
    attended = hidden.astype(jnp.bfloat16)
    normed = (
        hidden * lax.rsqrt(jnp.mean(hidden * hidden, -1, keepdims=True) + EPSILON) * norm_gain
    ).astype(jnp.bfloat16)
    sig_values = jax.nn.sigmoid(route_logits)
    route_weights = ROUTE_SCALE * sig_values / jnp.sum(sig_values, -1, keepdims=True)
    owners = lax.axis_size("ep")
    exp_dev = w_gate.shape[0]
    experts = owners * exp_dev
    row_count = residual.shape[0]
    top_k = routes.shape[1]
    capacity = max(2, 2 * row_count * top_k // experts)
    flat_ids = routes.reshape(-1)
    onehot = (flat_ids[:, None] == jnp.arange(experts, dtype=jnp.int32)[None, :]).astype(jnp.int32)
    slot_rank = jnp.sum(jnp.cumsum(onehot, 0) * onehot, 1) - 1
    target = flat_ids * capacity + slot_rank
    source_rows = jnp.repeat(normed, top_k, axis=0)
    outgoing = (
        jnp.zeros((experts * capacity, MODEL_WIDTH), jnp.bfloat16).at[target].set(source_rows)
    )
    outgoing = outgoing.reshape(owners, exp_dev, capacity, MODEL_WIDTH)
    arrived = lax.all_to_all(outgoing, "ep", split_axis=0, concat_axis=0, tiled=True)
    gate_part = jnp.einsum("nesd,edh->nesh", arrived, w_gate, preferred_element_type=jnp.float32)
    up_part = jnp.einsum("nesd,edh->nesh", arrived, w_up, preferred_element_type=jnp.float32)
    active = (jax.nn.silu(gate_part) * up_part).astype(jnp.bfloat16)
    result = jnp.einsum(
        "nesh,ehd->nesd", active, w_down, preferred_element_type=jnp.float32
    ).astype(jnp.bfloat16)
    returned = lax.all_to_all(result, "ep", split_axis=0, concat_axis=0, tiled=True)
    fetched = returned.reshape(experts * capacity, MODEL_WIDTH)[target].reshape(
        row_count, top_k, MODEL_WIDTH
    )
    weighted = jnp.sum(route_weights[:, :, None] * fetched.astype(jnp.float32), 1)
    expert_out = weighted.astype(jnp.bfloat16)
    return (attended, expert_out)


def on_device(*inputs):
    row_count, top_k = inputs[9].shape
    owners = lax.axis_size("ep")
    experts = owners * inputs[11].shape[0]
    capacity = max(2, 2 * row_count * top_k // experts)
    all_rows = row_count <= capacity and experts == owners == 4 * KEY_VALUE_HEADS
    if not all_rows:
        return routed_rows(*inputs)
    return every_row(*inputs)


def solution(mesh):
    return jax.shard_map(
        on_device,
        mesh=mesh,
        in_specs=(
            P(("groups", "ep"), None, None),
            P(("groups", "ep"), None, None, None),
            P(("groups", "ep"), None, None, None),
            P(("groups", "ep"), None, None),
            P(("groups", "ep"), None, None),
            P("groups"),
            P(("groups", "ep"), None),
            P("ep", None, None),
            P(),
            P(("groups", "ep"), None),
            P(("groups", "ep"), None),
            P("ep", None, None),
            P("ep", None, None),
            P("ep", None, None),
        ),
        out_specs=(P(("groups", "ep"), None), P(("groups", "ep"), None)),
        check_vma=False,
    )
```

```python
import functools
import math

import jax
import jax.numpy as jnp
from jax import lax
from jax.experimental import pallas as pl
from jax.experimental.pallas import tpu as pltpu
from jax.sharding import PartitionSpec as P


MODEL_WIDTH = 2048
QUERY_HEADS = 16
KEY_VALUE_HEADS = 4
HEAD_SIZE = 128


ROUTE_SCALE = 2.5
EPSILON = 1e-06
LANES = 128
WIDE = MODEL_WIDTH + LANES
CHUNK = 256


def exchanged(block, mask):
    count = lax.axis_size("ep")
    return lax.ppermute(block, "ep", [(index, index ^ mask) for index in range(count)])


def attend_kernel(
    lens_hbm, q_hbm, kc_hbm, vc_hbm, kb_hbm, vb_hbm, res_hbm, routes_hbm, logits_hbm, w_hbm,
    sent, kept,
    lens, q, kc, vc, kb, vb, res, routes, logits, w, attn, sems,
):
    pairs = (
        (lens_hbm, lens), (q_hbm, q), (kb_hbm, kb), (kc_hbm, kc), (vb_hbm, vb), (vc_hbm, vc),
        (routes_hbm, routes), (logits_hbm, logits), (res_hbm, res), (w_hbm, w),
    )
    copies = [pltpu.make_async_copy(a, b, sems.at[i]) for i, (a, b) in enumerate(pairs)]
    for copy in copies:
        copy.start()
    worker = lax.axis_index("ep")
    shard = lax.rem(worker, KEY_VALUE_HEADS)
    group = lax.div(worker, KEY_VALUE_HEADS)
    seqs = kc.shape[1]
    block = q.shape[1] // seqs
    heads = q.shape[2] // HEAD_SIZE
    rows = res.shape[0]
    scale = 1.0 / math.sqrt(HEAD_SIZE)
    nt = (((1,), (1,)), ((), ()))
    for copy in copies[:6]:
        copy.wait()
    for t in range(seqs):
        live = lens[group * seqs + t]
        part = slice(t * block, (t + 1) * block)
        queries = jnp.concatenate(
            [q[0, part, g * HEAD_SIZE : (g + 1) * HEAD_SIZE] for g in range(heads)], 0
        )
        cache = lax.dot_general(queries, kc[0, t], nt, preferred_element_type=jnp.float32) * scale
        fresh = lax.dot_general(queries, kb[0, part], nt, preferred_element_type=jnp.float32) * scale
        position = lax.broadcasted_iota(jnp.int32, cache.shape, 1)
        cache = jnp.where(position < live, cache, -1e30)
        largest = jnp.maximum(
            jnp.max(cache, -1, keepdims=True), jnp.max(fresh, -1, keepdims=True)
        )
        cache = jnp.exp(cache - largest)
        fresh = jnp.exp(fresh - largest)
        total = jnp.sum(cache, -1, keepdims=True) + jnp.sum(fresh, -1, keepdims=True)
        share = 1.0 / total
        mixed = jnp.dot(
            (cache * share).astype(jnp.bfloat16), vc[0, t], preferred_element_type=jnp.float32
        ) + jnp.dot(
            (fresh * share).astype(jnp.bfloat16), vb[0, part], preferred_element_type=jnp.float32
        )
        for g in range(heads):
            attn[part, g * HEAD_SIZE : (g + 1) * HEAD_SIZE] = mixed[
                g * block : (g + 1) * block
            ].astype(jnp.bfloat16)
    for copy in copies[6:9]:
        copy.wait()
    experts = lax.axis_size("ep")
    sig = 1.0 / (1.0 + jnp.exp(-logits[...]))
    weights = ROUTE_SCALE * sig / jnp.sum(sig, 0, keepdims=True)
    line = lax.broadcasted_iota(jnp.int32, (LANES, rows), 0)
    name = jnp.where(line < experts, line, line - experts)
    table = jnp.zeros((LANES, rows), jnp.float32)
    for k in range(routes.shape[0]):
        table = table + jnp.where(routes[k : k + 1, :] == name, weights[k : k + 1, :], 0.0)
    high = table.astype(jnp.bfloat16).astype(jnp.float32)
    table = jnp.where(line < experts, high, table - high).astype(jnp.bfloat16)
    row = lax.broadcasted_iota(jnp.int32, (rows, rows), 0)
    unit = jnp.where(row == lax.broadcasted_iota(jnp.int32, (rows, rows), 1), 1.0, 0.0)
    kept[:rows, MODEL_WIDTH:] = lax.dot_general(
        unit.astype(jnp.bfloat16), table, nt, preferred_element_type=jnp.float32
    )
    kept[rows:, MODEL_WIDTH:] = jnp.zeros((rows, LANES), jnp.float32)
    sent[:, MODEL_WIDTH:] = jnp.zeros((2 * rows, LANES), jnp.bfloat16)
    copies[9].wait()
    picked = [
        attn[pl.ds(pl.multiple_of((shard ^ mask) * rows, rows), rows), :] for mask in (1, 3, 0, 2)
    ]
    picked = jnp.concatenate(picked, 0)
    for n in range(0, MODEL_WIDTH, 2 * CHUNK):
        cols = slice(n, n + 2 * CHUNK)
        out = jnp.dot(picked, w[0, :, cols], preferred_element_type=jnp.float32)
        sent[:, cols] = out[: 2 * rows].astype(jnp.bfloat16)
        kept[:rows, cols] = out[2 * rows : 3 * rows] + res[:, cols].astype(jnp.float32)
        kept[rows:, cols] = out[3 * rows :]


def norm_kernel(block, kept, core, chip, gain, *outs):
    packet = outs[-1]
    rows = packet.shape[0]
    here = slice(block * rows, (block + 1) * rows)
    hidden = kept[here, :] + core[here, :].astype(jnp.float32) + chip[...].astype(jnp.float32)
    table = hidden[:, MODEL_WIDTH:]
    hidden = hidden[:, :MODEL_WIDTH]
    if block == 0:
        outs[0][...] = hidden.astype(jnp.bfloat16)
    mean = jnp.sum(hidden * hidden, -1, keepdims=True) * (1.0 / MODEL_WIDTH)
    packet[:, :MODEL_WIDTH] = (hidden * lax.rsqrt(mean + EPSILON) * gain[...]).astype(jnp.bfloat16)
    packet[:, MODEL_WIDTH:] = table.astype(jnp.bfloat16)


def expert_kernel(mine, other, w_gate, w_up, w_down, keep, send, x, act):
    half = mine.shape[0]
    experts = lax.axis_size("ep")
    own = lax.axis_index("ep")
    x[:half, :] = mine[...]
    x[half:, :] = other[...]
    lane = lax.broadcasted_iota(jnp.int32, (2 * half, LANES), 1)
    codes = x[:, MODEL_WIDTH:].astype(jnp.float32)
    chosen = (lane == own) | (lane == own + experts)
    weight = jnp.sum(jnp.where(chosen, codes, 0.0), 1, keepdims=True)
    rows = x[:, :MODEL_WIDTH]
    hidden_units = w_gate.shape[2]
    for n in range(0, hidden_units, CHUNK):
        cols = slice(n, n + CHUNK)
        gate = jnp.dot(rows, w_gate[0, :, cols], preferred_element_type=jnp.float32)
        up = jnp.dot(rows, w_up[0, :, cols], preferred_element_type=jnp.float32)
        act[:, cols] = (gate / (1.0 + jnp.exp(-gate)) * up).astype(jnp.bfloat16)
    for n in range(0, MODEL_WIDTH, CHUNK):
        cols = slice(n, n + CHUNK)
        out = jnp.dot(act[...], w_down[0, :, cols], preferred_element_type=jnp.float32) * weight
        keep[:, cols] = out[:half]
        send[:, cols] = out[half:].astype(jnp.bfloat16)


def sum_kernel(sums, got, out):
    out[...] = (sums[1, 0] + got[...].astype(jnp.float32)).astype(jnp.bfloat16)


def every_row(
    queries, key_cache, value_cache, key_block, value_block, cache_length_list, residual,
    output_weight, norm_gain, routes, route_logits, w_gate, w_up, w_down,
):
    rows = residual.shape[0]
    anywhere = pl.BlockSpec(memory_space=pl.ANY)
    whole = pl.BlockSpec(memory_space=pltpu.VMEM)
    operands = (
        cache_length_list, queries, key_cache, value_cache, key_block, value_block, residual,
        routes.T, route_logits.T, output_weight,
    )
    operands = tuple(pltpu.with_memory_space_constraint(a, pltpu.HBM) for a in operands)
    scratch = [pltpu.SMEM(cache_length_list.shape, jnp.int32)]
    scratch += [pltpu.VMEM(a.shape, a.dtype) for a in operands[1:]]
    scratch += [
        pltpu.VMEM((queries.shape[1], queries.shape[2]), jnp.bfloat16),
        pltpu.SemaphoreType.DMA((len(operands),)),
    ]
    sent, kept = pl.pallas_call(
        attend_kernel,
        out_shape=(
            jax.ShapeDtypeStruct((2 * rows, WIDE), jnp.bfloat16),
            jax.ShapeDtypeStruct((2 * rows, WIDE), jnp.float32),
        ),
        in_specs=[anywhere] * len(operands),
        out_specs=(whole, whole),
        scratch_shapes=scratch,
        compiler_params=pltpu.CompilerParams(vmem_limit_bytes=12 << 20),
        cost_estimate=pl.CostEstimate(flops=1 << 30, bytes_accessed=1 << 23, transcendentals=1 << 18),
        name="attend",
    )(*operands)
    sent, w_gate, w_up, w_down = lax.optimization_barrier((sent, w_gate, w_up, w_down))
    core = exchanged(sent, 1)
    sums = (kept + core.astype(jnp.float32)).astype(jnp.bfloat16)
    chip_own = exchanged(sums[rows:], 2)
    chip_pair = exchanged(sums[:rows], 2)

    def normed(block, chip):
        outs = (pltpu.VMEM((rows, MODEL_WIDTH), jnp.bfloat16),) * (block == 0)
        outs += (jax.ShapeDtypeStruct((rows, WIDE), jnp.bfloat16),)
        return pl.pallas_call(
            functools.partial(norm_kernel, block),
            out_shape=outs,
            in_specs=[whole] * 4,
            out_specs=(whole,) * len(outs),
            compiler_params=pltpu.CompilerParams(vmem_limit_bytes=6 << 20),
            cost_estimate=pl.CostEstimate(
                flops=1 << 34, bytes_accessed=1 << 20, transcendentals=1 << 10
            ),
            name="norm",
        )(kept, core, chip, norm_gain[None])

    def expert(mine):
        half = mine.shape[0]
        other = exchanged(mine, 1)
        keep, send = pl.pallas_call(
            expert_kernel,
            out_shape=(
                jax.ShapeDtypeStruct((half, MODEL_WIDTH), jnp.float32),
                jax.ShapeDtypeStruct((half, MODEL_WIDTH), jnp.bfloat16),
            ),
            in_specs=[whole] * 5,
            out_specs=(whole, whole),
            scratch_shapes=[
                pltpu.VMEM((2 * half, WIDE), jnp.bfloat16),
                pltpu.VMEM((2 * half, w_gate.shape[2]), jnp.bfloat16),
            ],
            compiler_params=pltpu.CompilerParams(vmem_limit_bytes=12 << 20),
            cost_estimate=pl.CostEstimate(
                flops=1 << 30, bytes_accessed=1 << 23, transcendentals=1 << 18
            ),
            name="expert",
        )(mine, other, w_gate, w_up, w_down)
        back = exchanged(send, 1)
        total = keep + back.astype(jnp.float32)
        return total.reshape(half // (2 * rows), 2, rows, MODEL_WIDTH)

    attended, own = normed(0, chip_own)
    far = exchanged(own, 8)
    (pair,) = normed(1, chip_pair)
    packet = jnp.concatenate([own, pair], 0)
    near = exchanged(packet, 4)
    across = exchanged(packet, 12)
    passed = exchanged(far, 2)
    sums = expert(jnp.concatenate([packet, near], 0))
    got = exchanged(sums[:, 1].astype(jnp.bfloat16), 2)
    summed = sums[0, 0] + got[0].astype(jnp.float32)
    near_sum = (sums[1, 0] + got[1].astype(jnp.float32)).astype(jnp.bfloat16)
    near = exchanged(near_sum, 4)
    sums = expert(jnp.concatenate([far, passed, across], 0))
    got_across = exchanged(sums[1, 1].astype(jnp.bfloat16), 2)
    got_far = exchanged(sums[0, 1].astype(jnp.bfloat16), 2)
    across_sum = pl.pallas_call(
        sum_kernel,
        out_shape=jax.ShapeDtypeStruct((rows, MODEL_WIDTH), jnp.bfloat16),
        in_specs=[whole] * 2,
        out_specs=whole,
        compiler_params=pltpu.CompilerParams(vmem_limit_bytes=4 << 20),
        cost_estimate=pl.CostEstimate(flops=1 << 16, bytes_accessed=1 << 18, transcendentals=0),
        name="acrosssum",
    )(sums, got_across)
    across = exchanged(across_sum, 12)
    far_sum = (sums[0, 0] + got_far.astype(jnp.float32)).astype(jnp.bfloat16)
    far = exchanged(far_sum, 8)
    summed = summed + near.astype(jnp.float32) + far.astype(jnp.float32) + across.astype(jnp.float32)
    return (attended, summed.astype(jnp.bfloat16))


def swapped(block, axis, distance):
    count = lax.axis_size(axis)
    route = []
    for low in range(count):
        high = low | 1 << distance
        if high != low and high < count:
            route += [(low, high), (high, low)]
    return lax.ppermute(block, axis, route)


def routed_rows(
    queries,
    key_cache,
    value_cache,
    key_block,
    value_block,
    cache_length_list,
    residual,
    output_weight,
    norm_gain,
    routes,
    route_logits,
    w_gate,
    w_up,
    w_down,
):
    group_results = QUERY_HEADS // KEY_VALUE_HEADS
    shard_worker = lax.axis_index("ep")
    sequence_group_index = shard_worker // KEY_VALUE_HEADS
    head_shard_index = shard_worker % KEY_VALUE_HEADS
    seq_grp = key_cache.shape[1]
    cache_len = key_cache.shape[2]
    rows_per_group = queries.shape[1]
    block_len = rows_per_group // seq_grp
    live_lens = lax.dynamic_slice_in_dim(cache_length_list, sequence_group_index * seq_grp, seq_grp)
    heads_of_query = queries[0].reshape(seq_grp, block_len, group_results, HEAD_SIZE)
    keys_of_block = key_block[0].reshape(seq_grp, block_len, HEAD_SIZE)
    values_of_block = value_block[0].reshape(seq_grp, block_len, HEAD_SIZE)
    score_cache = jnp.einsum(
        "srgd,spd->sgrp", heads_of_query, key_cache[0], preferred_element_type=jnp.float32
    ) / math.sqrt(HEAD_SIZE)
    score_block = jnp.einsum(
        "srgd,spd->sgrp", heads_of_query, keys_of_block, preferred_element_type=jnp.float32
    ) / math.sqrt(HEAD_SIZE)
    position = jnp.arange(cache_len, dtype=jnp.int32)
    live_slots = position[None, :] < live_lens[:, None]
    score_cache = jnp.where(live_slots[:, None, None, :], score_cache, -1e30)
    largest = jnp.maximum(
        jnp.max(score_cache, -1, keepdims=True), jnp.max(score_block, -1, keepdims=True)
    )
    exp_cache = jnp.exp(score_cache - largest)
    exp_block = jnp.exp(score_block - largest)
    denominator = jnp.sum(exp_cache, -1, keepdims=True) + jnp.sum(exp_block, -1, keepdims=True)
    prob_cache = (exp_cache / denominator).astype(jnp.bfloat16)
    prob_block = (exp_block / denominator).astype(jnp.bfloat16)
    mixed_heads = jnp.einsum(
        "sgrp,spd->srgd", prob_cache, value_cache[0], preferred_element_type=jnp.float32
    )
    mixed_heads = mixed_heads + jnp.einsum(
        "sgrp,spd->srgd", prob_block, values_of_block, preferred_element_type=jnp.float32
    )
    attn_rows = mixed_heads.reshape(rows_per_group, group_results * HEAD_SIZE).astype(jnp.bfloat16)
    partial_value = jnp.dot(attn_rows, output_weight[0], preferred_element_type=jnp.float32)
    tree_levels = KEY_VALUE_HEADS.bit_length() - 1
    projected = partial_value
    for bit_pos in reversed(range(tree_levels)):
        half_rows = projected.shape[0] // 2
        low_half = projected[:half_rows]
        high_half = projected[half_rows:]
        upper_side = head_shard_index >> bit_pos & 1 == 1
        kept_rows = jnp.where(upper_side, high_half, low_half)
        sent_rows = jnp.where(upper_side, low_half, high_half)
        projected = kept_rows + swapped(sent_rows, "ep", bit_pos)
    hidden = residual.astype(jnp.float32) + projected
    attended = hidden.astype(jnp.bfloat16)
    normed = (
        hidden * lax.rsqrt(jnp.mean(hidden * hidden, -1, keepdims=True) + EPSILON) * norm_gain
    ).astype(jnp.bfloat16)
    sig_values = jax.nn.sigmoid(route_logits)
    route_weights = ROUTE_SCALE * sig_values / jnp.sum(sig_values, -1, keepdims=True)
    owners = lax.axis_size("ep")
    exp_dev = w_gate.shape[0]
    experts = owners * exp_dev
    row_count = residual.shape[0]
    top_k = routes.shape[1]
    capacity = max(2, 2 * row_count * top_k // experts)
    flat_ids = routes.reshape(-1)
    onehot = (flat_ids[:, None] == jnp.arange(experts, dtype=jnp.int32)[None, :]).astype(jnp.int32)
    slot_rank = jnp.sum(jnp.cumsum(onehot, 0) * onehot, 1) - 1
    target = flat_ids * capacity + slot_rank
    source_rows = jnp.repeat(normed, top_k, axis=0)
    outgoing = (
        jnp.zeros((experts * capacity, MODEL_WIDTH), jnp.bfloat16).at[target].set(source_rows)
    )
    outgoing = outgoing.reshape(owners, exp_dev, capacity, MODEL_WIDTH)
    arrived = lax.all_to_all(outgoing, "ep", split_axis=0, concat_axis=0, tiled=True)
    gate_part = jnp.einsum("nesd,edh->nesh", arrived, w_gate, preferred_element_type=jnp.float32)
    up_part = jnp.einsum("nesd,edh->nesh", arrived, w_up, preferred_element_type=jnp.float32)
    active = (jax.nn.silu(gate_part) * up_part).astype(jnp.bfloat16)
    result = jnp.einsum(
        "nesh,ehd->nesd", active, w_down, preferred_element_type=jnp.float32
    ).astype(jnp.bfloat16)
    returned = lax.all_to_all(result, "ep", split_axis=0, concat_axis=0, tiled=True)
    fetched = returned.reshape(experts * capacity, MODEL_WIDTH)[target].reshape(
        row_count, top_k, MODEL_WIDTH
    )
    weighted = jnp.sum(route_weights[:, :, None] * fetched.astype(jnp.float32), 1)
    expert_out = weighted.astype(jnp.bfloat16)
    return (attended, expert_out)


def on_device(*inputs):
    row_count, top_k = inputs[9].shape
    owners = lax.axis_size("ep")
    experts = owners * inputs[11].shape[0]
    capacity = max(2, 2 * row_count * top_k // experts)
    all_rows = row_count <= capacity and experts == owners == 4 * KEY_VALUE_HEADS
    if not all_rows:
        return routed_rows(*inputs)
    return every_row(*inputs)


def solution(mesh):
    return jax.shard_map(
        on_device,
        mesh=mesh,
        in_specs=(
            P(("groups", "ep"), None, None),
            P(("groups", "ep"), None, None, None),
            P(("groups", "ep"), None, None, None),
            P(("groups", "ep"), None, None),
            P(("groups", "ep"), None, None),
            P("groups"),
            P(("groups", "ep"), None),
            P("ep", None, None),
            P(),
            P(("groups", "ep"), None),
            P(("groups", "ep"), None),
            P("ep", None, None),
            P("ep", None, None),
            P("ep", None, None),
        ),
        out_specs=(P(("groups", "ep"), None), P(("groups", "ep"), None)),
        check_vma=False,
    )
```

```python
import functools
import math

import jax
import jax.numpy as jnp
from jax import lax
from jax.experimental import pallas as pl
from jax.experimental.pallas import tpu as pltpu
from jax.sharding import PartitionSpec as P


MODEL_WIDTH = 2048
QUERY_HEADS = 16
KEY_VALUE_HEADS = 4
HEAD_SIZE = 128


ROUTE_SCALE = 2.5
EPSILON = 1e-06
LANES = 128
WIDE = MODEL_WIDTH + LANES
CHUNK = 256


def exchanged(block, mask):
    count = lax.axis_size("ep")
    return lax.ppermute(block, "ep", [(index, index ^ mask) for index in range(count)])


def attend_kernel(
    lens_hbm, q_hbm, kc_hbm, vc_hbm, kb_hbm, vb_hbm, res_hbm, routes_hbm, logits_hbm, w_hbm,
    sent, kept,
    lens, q, kc, vc, kb, vb, res, routes, logits, w, attn, sems,
):
    pairs = (
        (lens_hbm, lens), (q_hbm, q), (kb_hbm, kb), (kc_hbm, kc), (vb_hbm, vb), (vc_hbm, vc),
        (routes_hbm, routes), (logits_hbm, logits), (res_hbm, res), (w_hbm, w),
    )
    copies = [pltpu.make_async_copy(a, b, sems.at[i]) for i, (a, b) in enumerate(pairs)]
    for copy in copies:
        copy.start()
    worker = lax.axis_index("ep")
    shard = lax.rem(worker, KEY_VALUE_HEADS)
    group = lax.div(worker, KEY_VALUE_HEADS)
    seqs = kc.shape[1]
    block = q.shape[1] // seqs
    heads = q.shape[2] // HEAD_SIZE
    rows = res.shape[0]
    scale = 1.0 / math.sqrt(HEAD_SIZE)
    nt = (((1,), (1,)), ((), ()))
    for copy in copies[:6]:
        copy.wait()
    for t in range(seqs):
        live = lens[group * seqs + t]
        part = slice(t * block, (t + 1) * block)
        queries = jnp.concatenate(
            [q[0, part, g * HEAD_SIZE : (g + 1) * HEAD_SIZE] for g in range(heads)], 0
        )
        cache = lax.dot_general(queries, kc[0, t], nt, preferred_element_type=jnp.float32) * scale
        fresh = lax.dot_general(queries, kb[0, part], nt, preferred_element_type=jnp.float32) * scale
        position = lax.broadcasted_iota(jnp.int32, cache.shape, 1)
        cache = jnp.where(position < live, cache, -1e30)
        largest = jnp.maximum(
            jnp.max(cache, -1, keepdims=True), jnp.max(fresh, -1, keepdims=True)
        )
        cache = jnp.exp(cache - largest)
        fresh = jnp.exp(fresh - largest)
        total = jnp.sum(cache, -1, keepdims=True) + jnp.sum(fresh, -1, keepdims=True)
        share = 1.0 / total
        mixed = jnp.dot(
            (cache * share).astype(jnp.bfloat16), vc[0, t], preferred_element_type=jnp.float32
        ) + jnp.dot(
            (fresh * share).astype(jnp.bfloat16), vb[0, part], preferred_element_type=jnp.float32
        )
        for g in range(heads):
            attn[part, g * HEAD_SIZE : (g + 1) * HEAD_SIZE] = mixed[
                g * block : (g + 1) * block
            ].astype(jnp.bfloat16)
    for copy in copies[6:9]:
        copy.wait()
    experts = lax.axis_size("ep")
    sig = 1.0 / (1.0 + jnp.exp(-logits[...]))
    weights = ROUTE_SCALE * sig / jnp.sum(sig, 0, keepdims=True)
    line = lax.broadcasted_iota(jnp.int32, (LANES, rows), 0)
    name = jnp.where(line < experts, line, line - experts)
    table = jnp.zeros((LANES, rows), jnp.float32)
    for k in range(routes.shape[0]):
        table = table + jnp.where(routes[k : k + 1, :] == name, weights[k : k + 1, :], 0.0)
    high = table.astype(jnp.bfloat16).astype(jnp.float32)
    table = jnp.where(line < experts, high, table - high).astype(jnp.bfloat16)
    row = lax.broadcasted_iota(jnp.int32, (rows, rows), 0)
    unit = jnp.where(row == lax.broadcasted_iota(jnp.int32, (rows, rows), 1), 1.0, 0.0)
    kept[:rows, MODEL_WIDTH:] = lax.dot_general(
        unit.astype(jnp.bfloat16), table, nt, preferred_element_type=jnp.float32
    )
    kept[rows:, MODEL_WIDTH:] = jnp.zeros((rows, LANES), jnp.float32)
    sent[:, MODEL_WIDTH:] = jnp.zeros((2 * rows, LANES), jnp.bfloat16)
    copies[9].wait()
    picked = [
        attn[pl.ds(pl.multiple_of((shard ^ mask) * rows, rows), rows), :] for mask in (1, 3, 0, 2)
    ]
    picked = jnp.concatenate(picked, 0)
    for n in range(0, MODEL_WIDTH, 2 * CHUNK):
        cols = slice(n, n + 2 * CHUNK)
        out = jnp.dot(picked, w[0, :, cols], preferred_element_type=jnp.float32)
        sent[:, cols] = out[: 2 * rows].astype(jnp.bfloat16)
        kept[:rows, cols] = out[2 * rows : 3 * rows] + res[:, cols].astype(jnp.float32)
        kept[rows:, cols] = out[3 * rows :]


def norm_kernel(block, kept, core, chip, gain, *outs):
    packet = outs[-1]
    rows = packet.shape[0]
    here = slice(block * rows, (block + 1) * rows)
    hidden = kept[here, :] + core[here, :].astype(jnp.float32) + chip[...].astype(jnp.float32)
    table = hidden[:, MODEL_WIDTH:]
    hidden = hidden[:, :MODEL_WIDTH]
    if block == 0:
        outs[0][...] = hidden.astype(jnp.bfloat16)
    mean = jnp.sum(hidden * hidden, -1, keepdims=True) * (1.0 / MODEL_WIDTH)
    packet[:, :MODEL_WIDTH] = (hidden * lax.rsqrt(mean + EPSILON) * gain[...]).astype(jnp.bfloat16)
    packet[:, MODEL_WIDTH:] = table.astype(jnp.bfloat16)


def expert_kernel(mine, other, w_gate, w_up, w_down, keep, send, x, act):
    half = mine.shape[0]
    experts = lax.axis_size("ep")
    own = lax.axis_index("ep")
    x[:half, :] = mine[...]
    x[half:, :] = other[...]
    lane = lax.broadcasted_iota(jnp.int32, (2 * half, LANES), 1)
    codes = x[:, MODEL_WIDTH:].astype(jnp.float32)
    chosen = (lane == own) | (lane == own + experts)
    weight = jnp.sum(jnp.where(chosen, codes, 0.0), 1, keepdims=True)
    rows = x[:, :MODEL_WIDTH]
    hidden_units = w_gate.shape[2]
    for n in range(0, hidden_units, CHUNK):
        cols = slice(n, n + CHUNK)
        gate = jnp.dot(rows, w_gate[0, :, cols], preferred_element_type=jnp.float32)
        up = jnp.dot(rows, w_up[0, :, cols], preferred_element_type=jnp.float32)
        act[:, cols] = (gate / (1.0 + jnp.exp(-gate)) * up).astype(jnp.bfloat16)
    for n in range(0, MODEL_WIDTH, CHUNK):
        cols = slice(n, n + CHUNK)
        out = jnp.dot(act[...], w_down[0, :, cols], preferred_element_type=jnp.float32) * weight
        keep[:, cols] = out[:half]
        send[:, cols] = out[half:].astype(jnp.bfloat16)


def sum_kernel(sums, got, out):
    out[...] = (sums[1, 0] + got[...].astype(jnp.float32)).astype(jnp.bfloat16)


def every_row(
    queries, key_cache, value_cache, key_block, value_block, cache_length_list, residual,
    output_weight, norm_gain, routes, route_logits, w_gate, w_up, w_down,
):
    rows = residual.shape[0]
    anywhere = pl.BlockSpec(memory_space=pl.ANY)
    whole = pl.BlockSpec(memory_space=pltpu.VMEM)
    operands = (
        cache_length_list, queries, key_cache, value_cache, key_block, value_block, residual,
        routes.T, route_logits.T, output_weight,
    )
    operands = tuple(pltpu.with_memory_space_constraint(a, pltpu.HBM) for a in operands)
    scratch = [pltpu.SMEM(cache_length_list.shape, jnp.int32)]
    scratch += [pltpu.VMEM(a.shape, a.dtype) for a in operands[1:]]
    scratch += [
        pltpu.VMEM((queries.shape[1], queries.shape[2]), jnp.bfloat16),
        pltpu.SemaphoreType.DMA((len(operands),)),
    ]
    sent, kept = pl.pallas_call(
        attend_kernel,
        out_shape=(
            jax.ShapeDtypeStruct((2 * rows, WIDE), jnp.bfloat16),
            jax.ShapeDtypeStruct((2 * rows, WIDE), jnp.float32),
        ),
        in_specs=[anywhere] * len(operands),
        out_specs=(whole, whole),
        scratch_shapes=scratch,
        compiler_params=pltpu.CompilerParams(vmem_limit_bytes=12 << 20),
        cost_estimate=pl.CostEstimate(flops=1 << 30, bytes_accessed=1 << 23, transcendentals=1 << 18),
        name="attend",
    )(*operands)
    sent, w_gate, w_up, w_down = lax.optimization_barrier((sent, w_gate, w_up, w_down))
    core = exchanged(sent, 1)
    sums = (kept + core.astype(jnp.float32)).astype(jnp.bfloat16)
    chip_own = exchanged(sums[rows:], 2)
    chip_pair = exchanged(sums[:rows], 2)

    def normed(block, chip):
        outs = (pltpu.VMEM((rows, MODEL_WIDTH), jnp.bfloat16),) * (block == 0)
        outs += (jax.ShapeDtypeStruct((rows, WIDE), jnp.bfloat16),)
        return pl.pallas_call(
            functools.partial(norm_kernel, block),
            out_shape=outs,
            in_specs=[whole] * 4,
            out_specs=(whole,) * len(outs),
            compiler_params=pltpu.CompilerParams(vmem_limit_bytes=6 << 20),
            cost_estimate=pl.CostEstimate(
                flops=1 << 34, bytes_accessed=1 << 20, transcendentals=1 << 10
            ),
            name="norm",
        )(kept, core, chip, norm_gain[None])

    def expert(mine):
        half = mine.shape[0]
        other = exchanged(mine, 1)
        keep, send = pl.pallas_call(
            expert_kernel,
            out_shape=(
                jax.ShapeDtypeStruct((half, MODEL_WIDTH), jnp.float32),
                jax.ShapeDtypeStruct((half, MODEL_WIDTH), jnp.bfloat16),
            ),
            in_specs=[whole] * 5,
            out_specs=(whole, whole),
            scratch_shapes=[
                pltpu.VMEM((2 * half, WIDE), jnp.bfloat16),
                pltpu.VMEM((2 * half, w_gate.shape[2]), jnp.bfloat16),
            ],
            compiler_params=pltpu.CompilerParams(vmem_limit_bytes=12 << 20),
            cost_estimate=pl.CostEstimate(
                flops=1 << 30, bytes_accessed=1 << 23, transcendentals=1 << 18
            ),
            name="expert",
        )(mine, other, w_gate, w_up, w_down)
        back = exchanged(send, 1)
        total = keep + back.astype(jnp.float32)
        return total.reshape(half // (2 * rows), 2, rows, MODEL_WIDTH)

    attended, own = normed(0, chip_own)
    far = exchanged(own, 8)
    (pair,) = normed(1, chip_pair)
    packet = jnp.concatenate([own, pair], 0)
    near = exchanged(packet, 4)
    across = exchanged(packet, 12)
    passed = exchanged(far, 2)
    sums = expert(jnp.concatenate([packet, near], 0))
    got_near = exchanged(sums[1, 1].astype(jnp.bfloat16), 2)
    got_own = exchanged(sums[0, 1].astype(jnp.bfloat16), 2)
    near_sum = (sums[1, 0] + got_near.astype(jnp.float32)).astype(jnp.bfloat16)
    summed = sums[0, 0] + got_own.astype(jnp.float32)
    near = exchanged(near_sum, 4)
    sums = expert(jnp.concatenate([far, passed, across], 0))
    got_across = exchanged(sums[1, 1].astype(jnp.bfloat16), 2)
    got_far = exchanged(sums[0, 1].astype(jnp.bfloat16), 2)
    across_sum = pl.pallas_call(
        sum_kernel,
        out_shape=jax.ShapeDtypeStruct((rows, MODEL_WIDTH), jnp.bfloat16),
        in_specs=[whole] * 2,
        out_specs=whole,
        compiler_params=pltpu.CompilerParams(vmem_limit_bytes=4 << 20),
        cost_estimate=pl.CostEstimate(flops=1 << 16, bytes_accessed=1 << 18, transcendentals=0),
        name="acrosssum",
    )(sums, got_across)
    across = exchanged(across_sum, 12)
    far_sum = (sums[0, 0] + got_far.astype(jnp.float32)).astype(jnp.bfloat16)
    far = exchanged(far_sum, 8)
    summed = summed + near.astype(jnp.float32) + far.astype(jnp.float32) + across.astype(jnp.float32)
    return (attended, summed.astype(jnp.bfloat16))


def swapped(block, axis, distance):
    count = lax.axis_size(axis)
    route = []
    for low in range(count):
        high = low | 1 << distance
        if high != low and high < count:
            route += [(low, high), (high, low)]
    return lax.ppermute(block, axis, route)


def routed_rows(
    queries,
    key_cache,
    value_cache,
    key_block,
    value_block,
    cache_length_list,
    residual,
    output_weight,
    norm_gain,
    routes,
    route_logits,
    w_gate,
    w_up,
    w_down,
):
    group_results = QUERY_HEADS // KEY_VALUE_HEADS
    shard_worker = lax.axis_index("ep")
    sequence_group_index = shard_worker // KEY_VALUE_HEADS
    head_shard_index = shard_worker % KEY_VALUE_HEADS
    seq_grp = key_cache.shape[1]
    cache_len = key_cache.shape[2]
    rows_per_group = queries.shape[1]
    block_len = rows_per_group // seq_grp
    live_lens = lax.dynamic_slice_in_dim(cache_length_list, sequence_group_index * seq_grp, seq_grp)
    heads_of_query = queries[0].reshape(seq_grp, block_len, group_results, HEAD_SIZE)
    keys_of_block = key_block[0].reshape(seq_grp, block_len, HEAD_SIZE)
    values_of_block = value_block[0].reshape(seq_grp, block_len, HEAD_SIZE)
    score_cache = jnp.einsum(
        "srgd,spd->sgrp", heads_of_query, key_cache[0], preferred_element_type=jnp.float32
    ) / math.sqrt(HEAD_SIZE)
    score_block = jnp.einsum(
        "srgd,spd->sgrp", heads_of_query, keys_of_block, preferred_element_type=jnp.float32
    ) / math.sqrt(HEAD_SIZE)
    position = jnp.arange(cache_len, dtype=jnp.int32)
    live_slots = position[None, :] < live_lens[:, None]
    score_cache = jnp.where(live_slots[:, None, None, :], score_cache, -1e30)
    largest = jnp.maximum(
        jnp.max(score_cache, -1, keepdims=True), jnp.max(score_block, -1, keepdims=True)
    )
    exp_cache = jnp.exp(score_cache - largest)
    exp_block = jnp.exp(score_block - largest)
    denominator = jnp.sum(exp_cache, -1, keepdims=True) + jnp.sum(exp_block, -1, keepdims=True)
    prob_cache = (exp_cache / denominator).astype(jnp.bfloat16)
    prob_block = (exp_block / denominator).astype(jnp.bfloat16)
    mixed_heads = jnp.einsum(
        "sgrp,spd->srgd", prob_cache, value_cache[0], preferred_element_type=jnp.float32
    )
    mixed_heads = mixed_heads + jnp.einsum(
        "sgrp,spd->srgd", prob_block, values_of_block, preferred_element_type=jnp.float32
    )
    attn_rows = mixed_heads.reshape(rows_per_group, group_results * HEAD_SIZE).astype(jnp.bfloat16)
    partial_value = jnp.dot(attn_rows, output_weight[0], preferred_element_type=jnp.float32)
    tree_levels = KEY_VALUE_HEADS.bit_length() - 1
    projected = partial_value
    for bit_pos in reversed(range(tree_levels)):
        half_rows = projected.shape[0] // 2
        low_half = projected[:half_rows]
        high_half = projected[half_rows:]
        upper_side = head_shard_index >> bit_pos & 1 == 1
        kept_rows = jnp.where(upper_side, high_half, low_half)
        sent_rows = jnp.where(upper_side, low_half, high_half)
        projected = kept_rows + swapped(sent_rows, "ep", bit_pos)
    hidden = residual.astype(jnp.float32) + projected
    attended = hidden.astype(jnp.bfloat16)
    normed = (
        hidden * lax.rsqrt(jnp.mean(hidden * hidden, -1, keepdims=True) + EPSILON) * norm_gain
    ).astype(jnp.bfloat16)
    sig_values = jax.nn.sigmoid(route_logits)
    route_weights = ROUTE_SCALE * sig_values / jnp.sum(sig_values, -1, keepdims=True)
    owners = lax.axis_size("ep")
    exp_dev = w_gate.shape[0]
    experts = owners * exp_dev
    row_count = residual.shape[0]
    top_k = routes.shape[1]
    capacity = max(2, 2 * row_count * top_k // experts)
    flat_ids = routes.reshape(-1)
    onehot = (flat_ids[:, None] == jnp.arange(experts, dtype=jnp.int32)[None, :]).astype(jnp.int32)
    slot_rank = jnp.sum(jnp.cumsum(onehot, 0) * onehot, 1) - 1
    target = flat_ids * capacity + slot_rank
    source_rows = jnp.repeat(normed, top_k, axis=0)
    outgoing = (
        jnp.zeros((experts * capacity, MODEL_WIDTH), jnp.bfloat16).at[target].set(source_rows)
    )
    outgoing = outgoing.reshape(owners, exp_dev, capacity, MODEL_WIDTH)
    arrived = lax.all_to_all(outgoing, "ep", split_axis=0, concat_axis=0, tiled=True)
    gate_part = jnp.einsum("nesd,edh->nesh", arrived, w_gate, preferred_element_type=jnp.float32)
    up_part = jnp.einsum("nesd,edh->nesh", arrived, w_up, preferred_element_type=jnp.float32)
    active = (jax.nn.silu(gate_part) * up_part).astype(jnp.bfloat16)
    result = jnp.einsum(
        "nesh,ehd->nesd", active, w_down, preferred_element_type=jnp.float32
    ).astype(jnp.bfloat16)
    returned = lax.all_to_all(result, "ep", split_axis=0, concat_axis=0, tiled=True)
    fetched = returned.reshape(experts * capacity, MODEL_WIDTH)[target].reshape(
        row_count, top_k, MODEL_WIDTH
    )
    weighted = jnp.sum(route_weights[:, :, None] * fetched.astype(jnp.float32), 1)
    expert_out = weighted.astype(jnp.bfloat16)
    return (attended, expert_out)


def on_device(*inputs):
    row_count, top_k = inputs[9].shape
    owners = lax.axis_size("ep")
    experts = owners * inputs[11].shape[0]
    capacity = max(2, 2 * row_count * top_k // experts)
    all_rows = row_count <= capacity and experts == owners == 4 * KEY_VALUE_HEADS
    if not all_rows:
        return routed_rows(*inputs)
    return every_row(*inputs)


def solution(mesh):
    return jax.shard_map(
        on_device,
        mesh=mesh,
        in_specs=(
            P(("groups", "ep"), None, None),
            P(("groups", "ep"), None, None, None),
            P(("groups", "ep"), None, None, None),
            P(("groups", "ep"), None, None),
            P(("groups", "ep"), None, None),
            P("groups"),
            P(("groups", "ep"), None),
            P("ep", None, None),
            P(),
            P(("groups", "ep"), None),
            P(("groups", "ep"), None),
            P("ep", None, None),
            P("ep", None, None),
            P("ep", None, None),
        ),
        out_specs=(P(("groups", "ep"), None), P(("groups", "ep"), None)),
        check_vma=False,
    )
```

```python
import functools
import math

import jax
import jax.numpy as jnp
from jax import lax
from jax.experimental import pallas as pl
from jax.experimental.pallas import tpu as pltpu
from jax.sharding import PartitionSpec as P


MODEL_WIDTH = 2048
QUERY_HEADS = 16
KEY_VALUE_HEADS = 4
HEAD_SIZE = 128


ROUTE_SCALE = 2.5
EPSILON = 1e-06
LANES = 128
WIDE = MODEL_WIDTH + LANES
CHUNK = 256


def exchanged(block, mask):
    count = lax.axis_size("ep")
    return lax.ppermute(block, "ep", [(index, index ^ mask) for index in range(count)])


def attend_kernel(
    lens_hbm, q_hbm, kc_hbm, vc_hbm, kb_hbm, vb_hbm, res_hbm, routes_hbm, logits_hbm, w_hbm,
    sent, kept,
    lens, q, kc, vc, kb, vb, res, routes, logits, w, attn, sems,
):
    pairs = (
        (lens_hbm, lens), (q_hbm, q), (kb_hbm, kb), (kc_hbm, kc), (vb_hbm, vb), (vc_hbm, vc),
        (routes_hbm, routes), (logits_hbm, logits), (res_hbm, res), (w_hbm, w),
    )
    copies = [pltpu.make_async_copy(a, b, sems.at[i]) for i, (a, b) in enumerate(pairs)]
    for copy in copies:
        copy.start()
    worker = lax.axis_index("ep")
    shard = lax.rem(worker, KEY_VALUE_HEADS)
    group = lax.div(worker, KEY_VALUE_HEADS)
    seqs = kc.shape[1]
    block = q.shape[1] // seqs
    heads = q.shape[2] // HEAD_SIZE
    rows = res.shape[0]
    scale = 1.0 / math.sqrt(HEAD_SIZE)
    nt = (((1,), (1,)), ((), ()))
    for copy in copies[:6]:
        copy.wait()
    for t in range(seqs):
        live = lens[group * seqs + t]
        part = slice(t * block, (t + 1) * block)
        queries = jnp.concatenate(
            [q[0, part, g * HEAD_SIZE : (g + 1) * HEAD_SIZE] for g in range(heads)], 0
        )
        cache = lax.dot_general(queries, kc[0, t], nt, preferred_element_type=jnp.float32) * scale
        fresh = lax.dot_general(queries, kb[0, part], nt, preferred_element_type=jnp.float32) * scale
        position = lax.broadcasted_iota(jnp.int32, cache.shape, 1)
        cache = jnp.where(position < live, cache, -1e30)
        largest = jnp.maximum(
            jnp.max(cache, -1, keepdims=True), jnp.max(fresh, -1, keepdims=True)
        )
        cache = jnp.exp(cache - largest)
        fresh = jnp.exp(fresh - largest)
        total = jnp.sum(cache, -1, keepdims=True) + jnp.sum(fresh, -1, keepdims=True)
        share = 1.0 / total
        mixed = jnp.dot(
            (cache * share).astype(jnp.bfloat16), vc[0, t], preferred_element_type=jnp.float32
        ) + jnp.dot(
            (fresh * share).astype(jnp.bfloat16), vb[0, part], preferred_element_type=jnp.float32
        )
        for g in range(heads):
            attn[part, g * HEAD_SIZE : (g + 1) * HEAD_SIZE] = mixed[
                g * block : (g + 1) * block
            ].astype(jnp.bfloat16)
    for copy in copies[6:9]:
        copy.wait()
    experts = lax.axis_size("ep")
    sig = 1.0 / (1.0 + jnp.exp(-logits[...]))
    weights = ROUTE_SCALE * sig / jnp.sum(sig, 0, keepdims=True)
    line = lax.broadcasted_iota(jnp.int32, (LANES, rows), 0)
    name = jnp.where(line < experts, line, line - experts)
    table = jnp.zeros((LANES, rows), jnp.float32)
    for k in range(routes.shape[0]):
        table = table + jnp.where(routes[k : k + 1, :] == name, weights[k : k + 1, :], 0.0)
    high = table.astype(jnp.bfloat16).astype(jnp.float32)
    table = jnp.where(line < experts, high, table - high).astype(jnp.bfloat16)
    row = lax.broadcasted_iota(jnp.int32, (rows, rows), 0)
    unit = jnp.where(row == lax.broadcasted_iota(jnp.int32, (rows, rows), 1), 1.0, 0.0)
    kept[:rows, MODEL_WIDTH:] = lax.dot_general(
        unit.astype(jnp.bfloat16), table, nt, preferred_element_type=jnp.float32
    )
    kept[rows:, MODEL_WIDTH:] = jnp.zeros((rows, LANES), jnp.float32)
    sent[:, MODEL_WIDTH:] = jnp.zeros((2 * rows, LANES), jnp.bfloat16)
    copies[9].wait()
    picked = [
        attn[pl.ds(pl.multiple_of((shard ^ mask) * rows, rows), rows), :] for mask in (1, 3, 0, 2)
    ]
    picked = jnp.concatenate(picked, 0)
    for n in range(0, MODEL_WIDTH, 2 * CHUNK):
        cols = slice(n, n + 2 * CHUNK)
        out = jnp.dot(picked, w[0, :, cols], preferred_element_type=jnp.float32)
        sent[:, cols] = out[: 2 * rows].astype(jnp.bfloat16)
        kept[:rows, cols] = out[2 * rows : 3 * rows] + res[:, cols].astype(jnp.float32)
        kept[rows:, cols] = out[3 * rows :]


def norm_kernel(block, kept, core, chip, gain, *outs):
    packet = outs[-1]
    rows = packet.shape[0]
    here = slice(block * rows, (block + 1) * rows)
    hidden = kept[here, :] + core[here, :].astype(jnp.float32) + chip[...].astype(jnp.float32)
    table = hidden[:, MODEL_WIDTH:]
    hidden = hidden[:, :MODEL_WIDTH]
    if block == 0:
        outs[0][...] = hidden.astype(jnp.bfloat16)
    mean = jnp.sum(hidden * hidden, -1, keepdims=True) * (1.0 / MODEL_WIDTH)
    packet[:, :MODEL_WIDTH] = (hidden * lax.rsqrt(mean + EPSILON) * gain[...]).astype(jnp.bfloat16)
    packet[:, MODEL_WIDTH:] = table.astype(jnp.bfloat16)


def expert_kernel(mine, other, w_gate, w_up, w_down, keep, send, x, act):
    half = mine.shape[0]
    experts = lax.axis_size("ep")
    own = lax.axis_index("ep")
    x[:half, :] = mine[...]
    x[half:, :] = other[...]
    lane = lax.broadcasted_iota(jnp.int32, (2 * half, LANES), 1)
    codes = x[:, MODEL_WIDTH:].astype(jnp.float32)
    chosen = (lane == own) | (lane == own + experts)
    weight = jnp.sum(jnp.where(chosen, codes, 0.0), 1, keepdims=True)
    rows = x[:, :MODEL_WIDTH]
    hidden_units = w_gate.shape[2]
    for n in range(0, hidden_units, CHUNK):
        cols = slice(n, n + CHUNK)
        gate = jnp.dot(rows, w_gate[0, :, cols], preferred_element_type=jnp.float32)
        up = jnp.dot(rows, w_up[0, :, cols], preferred_element_type=jnp.float32)
        act[:, cols] = (gate / (1.0 + jnp.exp(-gate)) * up).astype(jnp.bfloat16)
    for n in range(0, MODEL_WIDTH, CHUNK):
        cols = slice(n, n + CHUNK)
        out = jnp.dot(act[...], w_down[0, :, cols], preferred_element_type=jnp.float32) * weight
        keep[:, cols] = out[:half]
        send[:, cols] = out[half:].astype(jnp.bfloat16)


def sum_kernel(sums, got, out):
    out[...] = (sums[0, 0] + got[...].astype(jnp.float32)).astype(jnp.bfloat16)


def every_row(
    queries, key_cache, value_cache, key_block, value_block, cache_length_list, residual,
    output_weight, norm_gain, routes, route_logits, w_gate, w_up, w_down,
):
    rows = residual.shape[0]
    anywhere = pl.BlockSpec(memory_space=pl.ANY)
    whole = pl.BlockSpec(memory_space=pltpu.VMEM)
    operands = (
        cache_length_list, queries, key_cache, value_cache, key_block, value_block, residual,
        routes.T, route_logits.T, output_weight,
    )
    operands = tuple(pltpu.with_memory_space_constraint(a, pltpu.HBM) for a in operands)
    scratch = [pltpu.SMEM(cache_length_list.shape, jnp.int32)]
    scratch += [pltpu.VMEM(a.shape, a.dtype) for a in operands[1:]]
    scratch += [
        pltpu.VMEM((queries.shape[1], queries.shape[2]), jnp.bfloat16),
        pltpu.SemaphoreType.DMA((len(operands),)),
    ]
    sent, kept = pl.pallas_call(
        attend_kernel,
        out_shape=(
            jax.ShapeDtypeStruct((2 * rows, WIDE), jnp.bfloat16),
            jax.ShapeDtypeStruct((2 * rows, WIDE), jnp.float32),
        ),
        in_specs=[anywhere] * len(operands),
        out_specs=(whole, whole),
        scratch_shapes=scratch,
        compiler_params=pltpu.CompilerParams(vmem_limit_bytes=12 << 20),
        cost_estimate=pl.CostEstimate(flops=1 << 30, bytes_accessed=1 << 23, transcendentals=1 << 18),
        name="attend",
    )(*operands)
    sent, w_gate, w_up, w_down = lax.optimization_barrier((sent, w_gate, w_up, w_down))
    core = exchanged(sent, 1)
    sums = (kept + core.astype(jnp.float32)).astype(jnp.bfloat16)
    chip_own = exchanged(sums[rows:], 2)
    chip_pair = exchanged(sums[:rows], 2)

    def normed(block, chip):
        outs = (pltpu.VMEM((rows, MODEL_WIDTH), jnp.bfloat16),) * (block == 0)
        outs += (jax.ShapeDtypeStruct((rows, WIDE), jnp.bfloat16),)
        return pl.pallas_call(
            functools.partial(norm_kernel, block),
            out_shape=outs,
            in_specs=[whole] * 4,
            out_specs=(whole,) * len(outs),
            compiler_params=pltpu.CompilerParams(vmem_limit_bytes=6 << 20),
            cost_estimate=pl.CostEstimate(
                flops=1 << 34, bytes_accessed=1 << 20, transcendentals=1 << 10
            ),
            name="norm",
        )(kept, core, chip, norm_gain[None])

    def expert(mine):
        half = mine.shape[0]
        other = exchanged(mine, 1)
        keep, send = pl.pallas_call(
            expert_kernel,
            out_shape=(
                jax.ShapeDtypeStruct((half, MODEL_WIDTH), jnp.float32),
                jax.ShapeDtypeStruct((half, MODEL_WIDTH), jnp.bfloat16),
            ),
            in_specs=[whole] * 5,
            out_specs=(whole, whole),
            scratch_shapes=[
                pltpu.VMEM((2 * half, WIDE), jnp.bfloat16),
                pltpu.VMEM((2 * half, w_gate.shape[2]), jnp.bfloat16),
            ],
            compiler_params=pltpu.CompilerParams(vmem_limit_bytes=12 << 20),
            cost_estimate=pl.CostEstimate(
                flops=1 << 30, bytes_accessed=1 << 23, transcendentals=1 << 18
            ),
            name="expert",
        )(mine, other, w_gate, w_up, w_down)
        back = exchanged(send, 1)
        total = keep + back.astype(jnp.float32)
        return total.reshape(half // (2 * rows), 2, rows, MODEL_WIDTH)

    attended, own = normed(0, chip_own)
    far = exchanged(own, 8)
    (pair,) = normed(1, chip_pair)
    packet = jnp.concatenate([own, pair], 0)
    near = exchanged(packet, 4)
    across = exchanged(packet, 12)
    passed = exchanged(far, 2)
    sums = expert(jnp.concatenate([packet, near], 0))
    got_near = exchanged(sums[1, 1].astype(jnp.bfloat16), 2)
    got_own = exchanged(sums[0, 1].astype(jnp.bfloat16), 2)
    near_sum = (sums[1, 0] + got_near.astype(jnp.float32)).astype(jnp.bfloat16)
    summed = sums[0, 0] + got_own.astype(jnp.float32)
    near = exchanged(near_sum, 4)
    sums = expert(jnp.concatenate([far, passed, across], 0))
    got_far = exchanged(sums[0, 1].astype(jnp.bfloat16), 2)
    got_across = exchanged(sums[1, 1].astype(jnp.bfloat16), 2)
    far_sum = pl.pallas_call(
        sum_kernel,
        out_shape=jax.ShapeDtypeStruct((rows, MODEL_WIDTH), jnp.bfloat16),
        in_specs=[whole] * 2,
        out_specs=whole,
        compiler_params=pltpu.CompilerParams(vmem_limit_bytes=4 << 20),
        cost_estimate=pl.CostEstimate(flops=1 << 16, bytes_accessed=1 << 18, transcendentals=0),
        name="farsum",
    )(sums, got_far)
    far = exchanged(far_sum, 8)
    across_sum = (sums[1, 0] + got_across.astype(jnp.float32)).astype(jnp.bfloat16)
    across = exchanged(across_sum, 12)
    summed = summed + near.astype(jnp.float32) + far.astype(jnp.float32) + across.astype(jnp.float32)
    return (attended, summed.astype(jnp.bfloat16))


def swapped(block, axis, distance):
    count = lax.axis_size(axis)
    route = []
    for low in range(count):
        high = low | 1 << distance
        if high != low and high < count:
            route += [(low, high), (high, low)]
    return lax.ppermute(block, axis, route)


def routed_rows(
    queries,
    key_cache,
    value_cache,
    key_block,
    value_block,
    cache_length_list,
    residual,
    output_weight,
    norm_gain,
    routes,
    route_logits,
    w_gate,
    w_up,
    w_down,
):
    group_results = QUERY_HEADS // KEY_VALUE_HEADS
    shard_worker = lax.axis_index("ep")
    sequence_group_index = shard_worker // KEY_VALUE_HEADS
    head_shard_index = shard_worker % KEY_VALUE_HEADS
    seq_grp = key_cache.shape[1]
    cache_len = key_cache.shape[2]
    rows_per_group = queries.shape[1]
    block_len = rows_per_group // seq_grp
    live_lens = lax.dynamic_slice_in_dim(cache_length_list, sequence_group_index * seq_grp, seq_grp)
    heads_of_query = queries[0].reshape(seq_grp, block_len, group_results, HEAD_SIZE)
    keys_of_block = key_block[0].reshape(seq_grp, block_len, HEAD_SIZE)
    values_of_block = value_block[0].reshape(seq_grp, block_len, HEAD_SIZE)
    score_cache = jnp.einsum(
        "srgd,spd->sgrp", heads_of_query, key_cache[0], preferred_element_type=jnp.float32
    ) / math.sqrt(HEAD_SIZE)
    score_block = jnp.einsum(
        "srgd,spd->sgrp", heads_of_query, keys_of_block, preferred_element_type=jnp.float32
    ) / math.sqrt(HEAD_SIZE)
    position = jnp.arange(cache_len, dtype=jnp.int32)
    live_slots = position[None, :] < live_lens[:, None]
    score_cache = jnp.where(live_slots[:, None, None, :], score_cache, -1e30)
    largest = jnp.maximum(
        jnp.max(score_cache, -1, keepdims=True), jnp.max(score_block, -1, keepdims=True)
    )
    exp_cache = jnp.exp(score_cache - largest)
    exp_block = jnp.exp(score_block - largest)
    denominator = jnp.sum(exp_cache, -1, keepdims=True) + jnp.sum(exp_block, -1, keepdims=True)
    prob_cache = (exp_cache / denominator).astype(jnp.bfloat16)
    prob_block = (exp_block / denominator).astype(jnp.bfloat16)
    mixed_heads = jnp.einsum(
        "sgrp,spd->srgd", prob_cache, value_cache[0], preferred_element_type=jnp.float32
    )
    mixed_heads = mixed_heads + jnp.einsum(
        "sgrp,spd->srgd", prob_block, values_of_block, preferred_element_type=jnp.float32
    )
    attn_rows = mixed_heads.reshape(rows_per_group, group_results * HEAD_SIZE).astype(jnp.bfloat16)
    partial_value = jnp.dot(attn_rows, output_weight[0], preferred_element_type=jnp.float32)
    tree_levels = KEY_VALUE_HEADS.bit_length() - 1
    projected = partial_value
    for bit_pos in reversed(range(tree_levels)):
        half_rows = projected.shape[0] // 2
        low_half = projected[:half_rows]
        high_half = projected[half_rows:]
        upper_side = head_shard_index >> bit_pos & 1 == 1
        kept_rows = jnp.where(upper_side, high_half, low_half)
        sent_rows = jnp.where(upper_side, low_half, high_half)
        projected = kept_rows + swapped(sent_rows, "ep", bit_pos)
    hidden = residual.astype(jnp.float32) + projected
    attended = hidden.astype(jnp.bfloat16)
    normed = (
        hidden * lax.rsqrt(jnp.mean(hidden * hidden, -1, keepdims=True) + EPSILON) * norm_gain
    ).astype(jnp.bfloat16)
    sig_values = jax.nn.sigmoid(route_logits)
    route_weights = ROUTE_SCALE * sig_values / jnp.sum(sig_values, -1, keepdims=True)
    owners = lax.axis_size("ep")
    exp_dev = w_gate.shape[0]
    experts = owners * exp_dev
    row_count = residual.shape[0]
    top_k = routes.shape[1]
    capacity = max(2, 2 * row_count * top_k // experts)
    flat_ids = routes.reshape(-1)
    onehot = (flat_ids[:, None] == jnp.arange(experts, dtype=jnp.int32)[None, :]).astype(jnp.int32)
    slot_rank = jnp.sum(jnp.cumsum(onehot, 0) * onehot, 1) - 1
    target = flat_ids * capacity + slot_rank
    source_rows = jnp.repeat(normed, top_k, axis=0)
    outgoing = (
        jnp.zeros((experts * capacity, MODEL_WIDTH), jnp.bfloat16).at[target].set(source_rows)
    )
    outgoing = outgoing.reshape(owners, exp_dev, capacity, MODEL_WIDTH)
    arrived = lax.all_to_all(outgoing, "ep", split_axis=0, concat_axis=0, tiled=True)
    gate_part = jnp.einsum("nesd,edh->nesh", arrived, w_gate, preferred_element_type=jnp.float32)
    up_part = jnp.einsum("nesd,edh->nesh", arrived, w_up, preferred_element_type=jnp.float32)
    active = (jax.nn.silu(gate_part) * up_part).astype(jnp.bfloat16)
    result = jnp.einsum(
        "nesh,ehd->nesd", active, w_down, preferred_element_type=jnp.float32
    ).astype(jnp.bfloat16)
    returned = lax.all_to_all(result, "ep", split_axis=0, concat_axis=0, tiled=True)
    fetched = returned.reshape(experts * capacity, MODEL_WIDTH)[target].reshape(
        row_count, top_k, MODEL_WIDTH
    )
    weighted = jnp.sum(route_weights[:, :, None] * fetched.astype(jnp.float32), 1)
    expert_out = weighted.astype(jnp.bfloat16)
    return (attended, expert_out)


def on_device(*inputs):
    row_count, top_k = inputs[9].shape
    owners = lax.axis_size("ep")
    experts = owners * inputs[11].shape[0]
    capacity = max(2, 2 * row_count * top_k // experts)
    all_rows = row_count <= capacity and experts == owners == 4 * KEY_VALUE_HEADS
    if not all_rows:
        return routed_rows(*inputs)
    return every_row(*inputs)


def solution(mesh):
    return jax.shard_map(
        on_device,
        mesh=mesh,
        in_specs=(
            P(("groups", "ep"), None, None),
            P(("groups", "ep"), None, None, None),
            P(("groups", "ep"), None, None, None),
            P(("groups", "ep"), None, None),
            P(("groups", "ep"), None, None),
            P("groups"),
            P(("groups", "ep"), None),
            P("ep", None, None),
            P(),
            P(("groups", "ep"), None),
            P(("groups", "ep"), None),
            P("ep", None, None),
            P("ep", None, None),
            P("ep", None, None),
        ),
        out_specs=(P(("groups", "ep"), None), P(("groups", "ep"), None)),
        check_vma=False,
    )
```

```python
import functools
import math

import jax
import jax.numpy as jnp
from jax import lax
from jax.experimental import pallas as pl
from jax.experimental.pallas import tpu as pltpu
from jax.sharding import PartitionSpec as P


MODEL_WIDTH = 2048
QUERY_HEADS = 16
KEY_VALUE_HEADS = 4
HEAD_SIZE = 128


ROUTE_SCALE = 2.5
EPSILON = 1e-06
LANES = 128
WIDE = MODEL_WIDTH + LANES
CHUNK = 256


def exchanged(block, mask):
    count = lax.axis_size("ep")
    return lax.ppermute(block, "ep", [(index, index ^ mask) for index in range(count)])


def attend_kernel(
    lens_hbm, q_hbm, kc_hbm, vc_hbm, kb_hbm, vb_hbm, res_hbm, routes_hbm, logits_hbm, w_hbm,
    sent, kept,
    lens, q, kc, vc, kb, vb, res, routes, logits, w, attn, sems,
):
    pairs = (
        (lens_hbm, lens), (q_hbm, q), (kb_hbm, kb), (kc_hbm, kc), (vb_hbm, vb), (vc_hbm, vc),
        (routes_hbm, routes), (logits_hbm, logits), (res_hbm, res), (w_hbm, w),
    )
    copies = [pltpu.make_async_copy(a, b, sems.at[i]) for i, (a, b) in enumerate(pairs)]
    for copy in copies:
        copy.start()
    worker = lax.axis_index("ep")
    shard = lax.rem(worker, KEY_VALUE_HEADS)
    group = lax.div(worker, KEY_VALUE_HEADS)
    seqs = kc.shape[1]
    block = q.shape[1] // seqs
    heads = q.shape[2] // HEAD_SIZE
    rows = res.shape[0]
    scale = 1.0 / math.sqrt(HEAD_SIZE)
    nt = (((1,), (1,)), ((), ()))
    for copy in copies[:4]:
        copy.wait()
    probs = []
    for t in range(seqs):
        live = lens[group * seqs + t]
        part = slice(t * block, (t + 1) * block)
        queries = jnp.concatenate(
            [q[0, part, g * HEAD_SIZE : (g + 1) * HEAD_SIZE] for g in range(heads)], 0
        )
        cache = lax.dot_general(queries, kc[0, t], nt, preferred_element_type=jnp.float32) * scale
        fresh = lax.dot_general(queries, kb[0, part], nt, preferred_element_type=jnp.float32) * scale
        position = lax.broadcasted_iota(jnp.int32, cache.shape, 1)
        cache = jnp.where(position < live, cache, -1e30)
        probs.append((cache, fresh))
    for t in range(seqs):
        cache, fresh = probs[t]
        largest = jnp.maximum(
            jnp.max(cache, -1, keepdims=True), jnp.max(fresh, -1, keepdims=True)
        )
        cache = jnp.exp(cache - largest)
        fresh = jnp.exp(fresh - largest)
        total = jnp.sum(cache, -1, keepdims=True) + jnp.sum(fresh, -1, keepdims=True)
        share = 1.0 / total
        probs[t] = (cache * share).astype(jnp.bfloat16), (fresh * share).astype(jnp.bfloat16)
    copies[4].wait()
    copies[5].wait()
    for t in range(seqs):
        cache, fresh = probs[t]
        part = slice(t * block, (t + 1) * block)
        mixed = jnp.dot(cache, vc[0, t], preferred_element_type=jnp.float32) + jnp.dot(
            fresh, vb[0, part], preferred_element_type=jnp.float32
        )
        for g in range(heads):
            attn[part, g * HEAD_SIZE : (g + 1) * HEAD_SIZE] = mixed[
                g * block : (g + 1) * block
            ].astype(jnp.bfloat16)
    for copy in copies[6:9]:
        copy.wait()
    experts = lax.axis_size("ep")
    sig = 1.0 / (1.0 + jnp.exp(-logits[...]))
    weights = ROUTE_SCALE * sig / jnp.sum(sig, 0, keepdims=True)
    line = lax.broadcasted_iota(jnp.int32, (LANES, rows), 0)
    name = jnp.where(line < experts, line, line - experts)
    table = jnp.zeros((LANES, rows), jnp.float32)
    for k in range(routes.shape[0]):
        table = table + jnp.where(routes[k : k + 1, :] == name, weights[k : k + 1, :], 0.0)
    high = table.astype(jnp.bfloat16).astype(jnp.float32)
    table = jnp.where(line < experts, high, table - high).astype(jnp.bfloat16)
    row = lax.broadcasted_iota(jnp.int32, (rows, rows), 0)
    unit = jnp.where(row == lax.broadcasted_iota(jnp.int32, (rows, rows), 1), 1.0, 0.0)
    kept[:rows, MODEL_WIDTH:] = lax.dot_general(
        unit.astype(jnp.bfloat16), table, nt, preferred_element_type=jnp.float32
    )
    kept[rows:, MODEL_WIDTH:] = jnp.zeros((rows, LANES), jnp.float32)
    sent[:, MODEL_WIDTH:] = jnp.zeros((2 * rows, LANES), jnp.bfloat16)
    copies[9].wait()
    picked = [
        attn[pl.ds(pl.multiple_of((shard ^ mask) * rows, rows), rows), :] for mask in (1, 3, 0, 2)
    ]
    picked = jnp.concatenate(picked, 0)
    for n in range(0, MODEL_WIDTH, 2 * CHUNK):
        cols = slice(n, n + 2 * CHUNK)
        out = jnp.dot(picked, w[0, :, cols], preferred_element_type=jnp.float32)
        sent[:, cols] = out[: 2 * rows].astype(jnp.bfloat16)
        kept[:rows, cols] = out[2 * rows : 3 * rows] + res[:, cols].astype(jnp.float32)
        kept[rows:, cols] = out[3 * rows :]


def norm_kernel(block, kept, core, chip, gain, *outs):
    packet = outs[-1]
    rows = packet.shape[0]
    here = slice(block * rows, (block + 1) * rows)
    hidden = kept[here, :] + core[here, :].astype(jnp.float32) + chip[...].astype(jnp.float32)
    table = hidden[:, MODEL_WIDTH:]
    hidden = hidden[:, :MODEL_WIDTH]
    if block == 0:
        outs[0][...] = hidden.astype(jnp.bfloat16)
    mean = jnp.sum(hidden * hidden, -1, keepdims=True) * (1.0 / MODEL_WIDTH)
    packet[:, :MODEL_WIDTH] = (hidden * lax.rsqrt(mean + EPSILON) * gain[...]).astype(jnp.bfloat16)
    packet[:, MODEL_WIDTH:] = table.astype(jnp.bfloat16)


def expert_kernel(mine, other, w_gate, w_up, w_down, keep, send, x, act):
    half = mine.shape[0]
    experts = lax.axis_size("ep")
    own = lax.axis_index("ep")
    x[:half, :] = mine[...]
    x[half : 2 * half, :] = other[...]
    if x.shape[0] > 2 * half:
        x[2 * half :, :] = jnp.zeros((x.shape[0] - 2 * half, WIDE), jnp.bfloat16)
    lane = lax.broadcasted_iota(jnp.int32, (x.shape[0], LANES), 1)
    codes = x[:, MODEL_WIDTH:].astype(jnp.float32)
    chosen = (lane == own) | (lane == own + experts)
    weight = jnp.sum(jnp.where(chosen, codes, 0.0), 1, keepdims=True)
    rows = x[:, :MODEL_WIDTH]
    hidden_units = w_gate.shape[2]
    for n in range(0, hidden_units, CHUNK):
        cols = slice(n, n + CHUNK)
        gate = jnp.dot(rows, w_gate[0, :, cols], preferred_element_type=jnp.float32)
        up = jnp.dot(rows, w_up[0, :, cols], preferred_element_type=jnp.float32)
        act[:, cols] = (gate / (1.0 + jnp.exp(-gate)) * up).astype(jnp.bfloat16)
    for n in range(0, MODEL_WIDTH, CHUNK):
        cols = slice(n, n + CHUNK)
        out = jnp.dot(act[...], w_down[0, :, cols], preferred_element_type=jnp.float32) * weight
        keep[:, cols] = out[:half]
        send[:, cols] = out[half : 2 * half].astype(jnp.bfloat16)


def sum_kernel(sums, got, out):
    out[...] = (sums[0, 0] + got[...].astype(jnp.float32)).astype(jnp.bfloat16)


def every_row(
    queries, key_cache, value_cache, key_block, value_block, cache_length_list, residual,
    output_weight, norm_gain, routes, route_logits, w_gate, w_up, w_down,
):
    rows = residual.shape[0]
    anywhere = pl.BlockSpec(memory_space=pl.ANY)
    whole = pl.BlockSpec(memory_space=pltpu.VMEM)
    operands = (
        cache_length_list, queries, key_cache, value_cache, key_block, value_block, residual,
        routes.T, route_logits.T, output_weight,
    )
    operands = tuple(pltpu.with_memory_space_constraint(a, pltpu.HBM) for a in operands)
    scratch = [pltpu.SMEM(cache_length_list.shape, jnp.int32)]
    scratch += [pltpu.VMEM(a.shape, a.dtype) for a in operands[1:]]
    scratch += [
        pltpu.VMEM((queries.shape[1], queries.shape[2]), jnp.bfloat16),
        pltpu.SemaphoreType.DMA((len(operands),)),
    ]
    sent, kept = pl.pallas_call(
        attend_kernel,
        out_shape=(
            jax.ShapeDtypeStruct((2 * rows, WIDE), jnp.bfloat16),
            jax.ShapeDtypeStruct((2 * rows, WIDE), jnp.float32),
        ),
        in_specs=[anywhere] * len(operands),
        out_specs=(whole, whole),
        scratch_shapes=scratch,
        compiler_params=pltpu.CompilerParams(vmem_limit_bytes=12 << 20),
        cost_estimate=pl.CostEstimate(flops=1 << 30, bytes_accessed=1 << 23, transcendentals=1 << 18),
        name="attend",
    )(*operands)
    sent, w_gate, w_up, w_down = lax.optimization_barrier((sent, w_gate, w_up, w_down))
    core = exchanged(sent, 1)
    sums = (kept + core.astype(jnp.float32)).astype(jnp.bfloat16)
    chip_own = exchanged(sums[rows:], 2)
    chip_pair = exchanged(sums[:rows], 2)

    def normed(block, chip):
        outs = (pltpu.VMEM((rows, MODEL_WIDTH), jnp.bfloat16),) * (block == 0)
        outs += (jax.ShapeDtypeStruct((rows, WIDE), jnp.bfloat16),)
        return pl.pallas_call(
            functools.partial(norm_kernel, block),
            out_shape=outs,
            in_specs=[whole] * 4,
            out_specs=(whole,) * len(outs),
            compiler_params=pltpu.CompilerParams(vmem_limit_bytes=6 << 20),
            cost_estimate=pl.CostEstimate(
                flops=1 << 34, bytes_accessed=1 << 20, transcendentals=1 << 10
            ),
            name="norm",
        )(kept, core, chip, norm_gain[None])

    def expert(mine):
        half = mine.shape[0]
        other = exchanged(mine, 1)
        keep, send = pl.pallas_call(
            expert_kernel,
            out_shape=(
                jax.ShapeDtypeStruct((half, MODEL_WIDTH), jnp.float32),
                jax.ShapeDtypeStruct((half, MODEL_WIDTH), jnp.bfloat16),
            ),
            in_specs=[whole] * 5,
            out_specs=(whole, whole),
            scratch_shapes=[
                pltpu.VMEM((max(2 * half, LANES), WIDE), jnp.bfloat16),
                pltpu.VMEM((max(2 * half, LANES), w_gate.shape[2]), jnp.bfloat16),
            ],
            compiler_params=pltpu.CompilerParams(vmem_limit_bytes=12 << 20),
            cost_estimate=pl.CostEstimate(
                flops=1 << 30, bytes_accessed=1 << 23, transcendentals=1 << 18
            ),
            name="expert",
        )(mine, other, w_gate, w_up, w_down)
        back = exchanged(send, 1)
        total = keep + back.astype(jnp.float32)
        return total.reshape(half // (2 * rows), 2, rows, MODEL_WIDTH)

    attended, own = normed(0, chip_own)
    far = exchanged(own, 8)
    (pair,) = normed(1, chip_pair)
    packet = jnp.concatenate([own, pair], 0)
    near = exchanged(packet, 4)
    across = exchanged(packet, 12)
    passed = exchanged(far, 2)
    sums = expert(jnp.concatenate([packet, near], 0))
    got_near = exchanged(sums[1, 1].astype(jnp.bfloat16), 2)
    got_own = exchanged(sums[0, 1].astype(jnp.bfloat16), 2)
    near_sum = (sums[1, 0] + got_near.astype(jnp.float32)).astype(jnp.bfloat16)
    summed = sums[0, 0] + got_own.astype(jnp.float32)
    near = exchanged(near_sum, 4)
    sums = expert(jnp.concatenate([far, passed], 0))
    got_far = exchanged(sums[0, 1].astype(jnp.bfloat16), 2)
    far_sum = pl.pallas_call(
        sum_kernel,
        out_shape=jax.ShapeDtypeStruct((rows, MODEL_WIDTH), jnp.bfloat16),
        in_specs=[whole] * 2,
        out_specs=whole,
        compiler_params=pltpu.CompilerParams(vmem_limit_bytes=4 << 20),
        cost_estimate=pl.CostEstimate(flops=1 << 16, bytes_accessed=1 << 18, transcendentals=0),
        name="farsum",
    )(sums, got_far)
    far = exchanged(far_sum, 8)
    sums = expert(across)
    got_across = exchanged(sums[0, 1].astype(jnp.bfloat16), 2)
    across_sum = (sums[0, 0] + got_across.astype(jnp.float32)).astype(jnp.bfloat16)
    across = exchanged(across_sum, 12)
    summed = summed + near.astype(jnp.float32) + far.astype(jnp.float32) + across.astype(jnp.float32)
    return (attended, summed.astype(jnp.bfloat16))


def swapped(block, axis, distance):
    count = lax.axis_size(axis)
    route = []
    for low in range(count):
        high = low | 1 << distance
        if high != low and high < count:
            route += [(low, high), (high, low)]
    return lax.ppermute(block, axis, route)


def routed_rows(
    queries,
    key_cache,
    value_cache,
    key_block,
    value_block,
    cache_length_list,
    residual,
    output_weight,
    norm_gain,
    routes,
    route_logits,
    w_gate,
    w_up,
    w_down,
):
    group_results = QUERY_HEADS // KEY_VALUE_HEADS
    shard_worker = lax.axis_index("ep")
    sequence_group_index = shard_worker // KEY_VALUE_HEADS
    head_shard_index = shard_worker % KEY_VALUE_HEADS
    seq_grp = key_cache.shape[1]
    cache_len = key_cache.shape[2]
    rows_per_group = queries.shape[1]
    block_len = rows_per_group // seq_grp
    live_lens = lax.dynamic_slice_in_dim(cache_length_list, sequence_group_index * seq_grp, seq_grp)
    heads_of_query = queries[0].reshape(seq_grp, block_len, group_results, HEAD_SIZE)
    keys_of_block = key_block[0].reshape(seq_grp, block_len, HEAD_SIZE)
    values_of_block = value_block[0].reshape(seq_grp, block_len, HEAD_SIZE)
    score_cache = jnp.einsum(
        "srgd,spd->sgrp", heads_of_query, key_cache[0], preferred_element_type=jnp.float32
    ) / math.sqrt(HEAD_SIZE)
    score_block = jnp.einsum(
        "srgd,spd->sgrp", heads_of_query, keys_of_block, preferred_element_type=jnp.float32
    ) / math.sqrt(HEAD_SIZE)
    position = jnp.arange(cache_len, dtype=jnp.int32)
    live_slots = position[None, :] < live_lens[:, None]
    score_cache = jnp.where(live_slots[:, None, None, :], score_cache, -1e30)
    largest = jnp.maximum(
        jnp.max(score_cache, -1, keepdims=True), jnp.max(score_block, -1, keepdims=True)
    )
    exp_cache = jnp.exp(score_cache - largest)
    exp_block = jnp.exp(score_block - largest)
    denominator = jnp.sum(exp_cache, -1, keepdims=True) + jnp.sum(exp_block, -1, keepdims=True)
    prob_cache = (exp_cache / denominator).astype(jnp.bfloat16)
    prob_block = (exp_block / denominator).astype(jnp.bfloat16)
    mixed_heads = jnp.einsum(
        "sgrp,spd->srgd", prob_cache, value_cache[0], preferred_element_type=jnp.float32
    )
    mixed_heads = mixed_heads + jnp.einsum(
        "sgrp,spd->srgd", prob_block, values_of_block, preferred_element_type=jnp.float32
    )
    attn_rows = mixed_heads.reshape(rows_per_group, group_results * HEAD_SIZE).astype(jnp.bfloat16)
    partial_value = jnp.dot(attn_rows, output_weight[0], preferred_element_type=jnp.float32)
    tree_levels = KEY_VALUE_HEADS.bit_length() - 1
    projected = partial_value
    for bit_pos in reversed(range(tree_levels)):
        half_rows = projected.shape[0] // 2
        low_half = projected[:half_rows]
        high_half = projected[half_rows:]
        upper_side = head_shard_index >> bit_pos & 1 == 1
        kept_rows = jnp.where(upper_side, high_half, low_half)
        sent_rows = jnp.where(upper_side, low_half, high_half)
        projected = kept_rows + swapped(sent_rows, "ep", bit_pos)
    hidden = residual.astype(jnp.float32) + projected
    attended = hidden.astype(jnp.bfloat16)
    normed = (
        hidden * lax.rsqrt(jnp.mean(hidden * hidden, -1, keepdims=True) + EPSILON) * norm_gain
    ).astype(jnp.bfloat16)
    sig_values = jax.nn.sigmoid(route_logits)
    route_weights = ROUTE_SCALE * sig_values / jnp.sum(sig_values, -1, keepdims=True)
    owners = lax.axis_size("ep")
    exp_dev = w_gate.shape[0]
    experts = owners * exp_dev
    row_count = residual.shape[0]
    top_k = routes.shape[1]
    capacity = max(2, 2 * row_count * top_k // experts)
    flat_ids = routes.reshape(-1)
    onehot = (flat_ids[:, None] == jnp.arange(experts, dtype=jnp.int32)[None, :]).astype(jnp.int32)
    slot_rank = jnp.sum(jnp.cumsum(onehot, 0) * onehot, 1) - 1
    target = flat_ids * capacity + slot_rank
    source_rows = jnp.repeat(normed, top_k, axis=0)
    outgoing = (
        jnp.zeros((experts * capacity, MODEL_WIDTH), jnp.bfloat16).at[target].set(source_rows)
    )
    outgoing = outgoing.reshape(owners, exp_dev, capacity, MODEL_WIDTH)
    arrived = lax.all_to_all(outgoing, "ep", split_axis=0, concat_axis=0, tiled=True)
    gate_part = jnp.einsum("nesd,edh->nesh", arrived, w_gate, preferred_element_type=jnp.float32)
    up_part = jnp.einsum("nesd,edh->nesh", arrived, w_up, preferred_element_type=jnp.float32)
    active = (jax.nn.silu(gate_part) * up_part).astype(jnp.bfloat16)
    result = jnp.einsum(
        "nesh,ehd->nesd", active, w_down, preferred_element_type=jnp.float32
    ).astype(jnp.bfloat16)
    returned = lax.all_to_all(result, "ep", split_axis=0, concat_axis=0, tiled=True)
    fetched = returned.reshape(experts * capacity, MODEL_WIDTH)[target].reshape(
        row_count, top_k, MODEL_WIDTH
    )
    weighted = jnp.sum(route_weights[:, :, None] * fetched.astype(jnp.float32), 1)
    expert_out = weighted.astype(jnp.bfloat16)
    return (attended, expert_out)


def on_device(*inputs):
    row_count, top_k = inputs[9].shape
    owners = lax.axis_size("ep")
    experts = owners * inputs[11].shape[0]
    capacity = max(2, 2 * row_count * top_k // experts)
    all_rows = row_count <= capacity and experts == owners == 4 * KEY_VALUE_HEADS
    if not all_rows:
        return routed_rows(*inputs)
    return every_row(*inputs)


def solution(mesh):
    return jax.shard_map(
        on_device,
        mesh=mesh,
        in_specs=(
            P(("groups", "ep"), None, None),
            P(("groups", "ep"), None, None, None),
            P(("groups", "ep"), None, None, None),
            P(("groups", "ep"), None, None),
            P(("groups", "ep"), None, None),
            P("groups"),
            P(("groups", "ep"), None),
            P("ep", None, None),
            P(),
            P(("groups", "ep"), None),
            P(("groups", "ep"), None),
            P("ep", None, None),
            P("ep", None, None),
            P("ep", None, None),
        ),
        out_specs=(P(("groups", "ep"), None), P(("groups", "ep"), None)),
        check_vma=False,
    )
```

```python
import functools
import math

import jax
import jax.numpy as jnp
from jax import lax
from jax.experimental import pallas as pl
from jax.experimental.pallas import tpu as pltpu
from jax.sharding import PartitionSpec as P


MODEL_WIDTH = 2048
QUERY_HEADS = 16
KEY_VALUE_HEADS = 4
HEAD_SIZE = 128


ROUTE_SCALE = 2.5
EPSILON = 1e-06
LANES = 128
WIDE = MODEL_WIDTH + LANES
CHUNK = 256


def exchanged(block, mask):
    count = lax.axis_size("ep")
    return lax.ppermute(block, "ep", [(index, index ^ mask) for index in range(count)])


def attend_kernel(
    lens_hbm, q_hbm, kc_hbm, vc_hbm, kb_hbm, vb_hbm, res_hbm, routes_hbm, logits_hbm, w_hbm,
    sent, kept,
    lens, q, kc, vc, kb, vb, res, routes, logits, w, attn, sems,
):
    pairs = (
        (lens_hbm, lens), (q_hbm, q), (kb_hbm, kb), (kc_hbm, kc), (vb_hbm, vb), (vc_hbm, vc),
        (routes_hbm, routes), (logits_hbm, logits), (res_hbm, res), (w_hbm, w),
    )
    copies = [pltpu.make_async_copy(a, b, sems.at[i]) for i, (a, b) in enumerate(pairs)]
    for copy in copies:
        copy.start()
    worker = lax.axis_index("ep")
    shard = lax.rem(worker, KEY_VALUE_HEADS)
    group = lax.div(worker, KEY_VALUE_HEADS)
    seqs = kc.shape[1]
    block = q.shape[1] // seqs
    heads = q.shape[2] // HEAD_SIZE
    rows = res.shape[0]
    scale = 1.0 / math.sqrt(HEAD_SIZE)
    nt = (((1,), (1,)), ((), ()))
    for copy in copies[:4]:
        copy.wait()
    probs = []
    for t in range(seqs):
        live = lens[group * seqs + t]
        part = slice(t * block, (t + 1) * block)
        queries = jnp.concatenate(
            [q[0, part, g * HEAD_SIZE : (g + 1) * HEAD_SIZE] for g in range(heads)], 0
        )
        cache = lax.dot_general(queries, kc[0, t], nt, preferred_element_type=jnp.float32) * scale
        fresh = lax.dot_general(queries, kb[0, part], nt, preferred_element_type=jnp.float32) * scale
        position = lax.broadcasted_iota(jnp.int32, cache.shape, 1)
        cache = jnp.where(position < live, cache, -1e30)
        probs.append((cache, fresh))
    for t in range(seqs):
        cache, fresh = probs[t]
        largest = jnp.maximum(
            jnp.max(cache, -1, keepdims=True), jnp.max(fresh, -1, keepdims=True)
        )
        cache = jnp.exp(cache - largest)
        fresh = jnp.exp(fresh - largest)
        total = jnp.sum(cache, -1, keepdims=True) + jnp.sum(fresh, -1, keepdims=True)
        share = 1.0 / total
        probs[t] = (cache * share).astype(jnp.bfloat16), (fresh * share).astype(jnp.bfloat16)
    copies[4].wait()
    copies[5].wait()
    for t in range(seqs):
        cache, fresh = probs[t]
        part = slice(t * block, (t + 1) * block)
        mixed = jnp.dot(cache, vc[0, t], preferred_element_type=jnp.float32) + jnp.dot(
            fresh, vb[0, part], preferred_element_type=jnp.float32
        )
        for g in range(heads):
            attn[part, g * HEAD_SIZE : (g + 1) * HEAD_SIZE] = mixed[
                g * block : (g + 1) * block
            ].astype(jnp.bfloat16)
    for copy in copies[6:9]:
        copy.wait()
    experts = lax.axis_size("ep")
    sig = 1.0 / (1.0 + jnp.exp(-logits[...]))
    weights = ROUTE_SCALE * sig / jnp.sum(sig, 0, keepdims=True)
    line = lax.broadcasted_iota(jnp.int32, (LANES, rows), 0)
    name = jnp.where(line < experts, line, line - experts)
    table = jnp.zeros((LANES, rows), jnp.float32)
    for k in range(routes.shape[0]):
        table = table + jnp.where(routes[k : k + 1, :] == name, weights[k : k + 1, :], 0.0)
    high = table.astype(jnp.bfloat16).astype(jnp.float32)
    table = jnp.where(line < experts, high, table - high).astype(jnp.bfloat16)
    row = lax.broadcasted_iota(jnp.int32, (rows, rows), 0)
    unit = jnp.where(row == lax.broadcasted_iota(jnp.int32, (rows, rows), 1), 1.0, 0.0)
    kept[:rows, MODEL_WIDTH:] = lax.dot_general(
        unit.astype(jnp.bfloat16), table, nt, preferred_element_type=jnp.float32
    )
    kept[rows:, MODEL_WIDTH:] = jnp.zeros((rows, LANES), jnp.float32)
    sent[:, MODEL_WIDTH:] = jnp.zeros((2 * rows, LANES), jnp.bfloat16)
    copies[9].wait()
    picked = [
        attn[pl.ds(pl.multiple_of((shard ^ mask) * rows, rows), rows), :] for mask in (1, 3, 0, 2)
    ]
    picked = jnp.concatenate(picked, 0)
    for n in range(0, MODEL_WIDTH, 2 * CHUNK):
        cols = slice(n, n + 2 * CHUNK)
        out = jnp.dot(picked, w[0, :, cols], preferred_element_type=jnp.float32)
        sent[:, cols] = out[: 2 * rows].astype(jnp.bfloat16)
        kept[:rows, cols] = out[2 * rows : 3 * rows] + res[:, cols].astype(jnp.float32)
        kept[rows:, cols] = out[3 * rows :]


def core_kernel(kept, core, own, pair):
    rows = own.shape[0]
    own[...] = (kept[:rows, :] + core[:rows, :].astype(jnp.float32)).astype(jnp.bfloat16)
    pair[...] = (kept[rows:, :] + core[rows:, :].astype(jnp.float32)).astype(jnp.bfloat16)


def norm_kernel(block, kept, core, chip, gain, *outs):
    packet = outs[-1]
    rows = packet.shape[0]
    here = slice(block * rows, (block + 1) * rows)
    hidden = kept[here, :] + core[here, :].astype(jnp.float32) + chip[...].astype(jnp.float32)
    table = hidden[:, MODEL_WIDTH:]
    hidden = hidden[:, :MODEL_WIDTH]
    if block == 0:
        outs[0][...] = hidden.astype(jnp.bfloat16)
    mean = jnp.sum(hidden * hidden, -1, keepdims=True) * (1.0 / MODEL_WIDTH)
    packet[:, :MODEL_WIDTH] = (hidden * lax.rsqrt(mean + EPSILON) * gain[...]).astype(jnp.bfloat16)
    packet[:, MODEL_WIDTH:] = table.astype(jnp.bfloat16)


def expert_kernel(mine, other, w_gate, w_up, w_down, keep, send, x, act):
    half = mine.shape[0]
    experts = lax.axis_size("ep")
    own = lax.axis_index("ep")
    x[:half, :] = mine[...]
    x[half:, :] = other[...]
    lane = lax.broadcasted_iota(jnp.int32, (2 * half, LANES), 1)
    codes = x[:, MODEL_WIDTH:].astype(jnp.float32)
    chosen = (lane == own) | (lane == own + experts)
    weight = jnp.sum(jnp.where(chosen, codes, 0.0), 1, keepdims=True)
    rows = x[:, :MODEL_WIDTH]
    hidden_units = w_gate.shape[2]
    for n in range(0, hidden_units, CHUNK):
        cols = slice(n, n + CHUNK)
        gate = jnp.dot(rows, w_gate[0, :, cols], preferred_element_type=jnp.float32)
        up = jnp.dot(rows, w_up[0, :, cols], preferred_element_type=jnp.float32)
        act[:, cols] = (gate / (1.0 + jnp.exp(-gate)) * up).astype(jnp.bfloat16)
    for n in range(0, MODEL_WIDTH, CHUNK):
        cols = slice(n, n + CHUNK)
        out = jnp.dot(act[...], w_down[0, :, cols], preferred_element_type=jnp.float32) * weight
        keep[:, cols] = out[:half]
        send[:, cols] = out[half:].astype(jnp.bfloat16)


def sum_kernel(sums, got, out):
    out[...] = (sums[0, 0] + got[...].astype(jnp.float32)).astype(jnp.bfloat16)


def every_row(
    queries, key_cache, value_cache, key_block, value_block, cache_length_list, residual,
    output_weight, norm_gain, routes, route_logits, w_gate, w_up, w_down,
):
    rows = residual.shape[0]
    anywhere = pl.BlockSpec(memory_space=pl.ANY)
    whole = pl.BlockSpec(memory_space=pltpu.VMEM)
    operands = (
        cache_length_list, queries, key_cache, value_cache, key_block, value_block, residual,
        routes.T, route_logits.T, output_weight,
    )
    operands = tuple(pltpu.with_memory_space_constraint(a, pltpu.HBM) for a in operands)
    scratch = [pltpu.SMEM(cache_length_list.shape, jnp.int32)]
    scratch += [pltpu.VMEM(a.shape, a.dtype) for a in operands[1:]]
    scratch += [
        pltpu.VMEM((queries.shape[1], queries.shape[2]), jnp.bfloat16),
        pltpu.SemaphoreType.DMA((len(operands),)),
    ]
    sent, kept = pl.pallas_call(
        attend_kernel,
        out_shape=(
            jax.ShapeDtypeStruct((2 * rows, WIDE), jnp.bfloat16),
            jax.ShapeDtypeStruct((2 * rows, WIDE), jnp.float32),
        ),
        in_specs=[anywhere] * len(operands),
        out_specs=(whole, whole),
        scratch_shapes=scratch,
        compiler_params=pltpu.CompilerParams(vmem_limit_bytes=12 << 20),
        cost_estimate=pl.CostEstimate(flops=1 << 30, bytes_accessed=1 << 23, transcendentals=1 << 18),
        name="attend",
    )(*operands)
    sent, w_gate, w_up, w_down = lax.optimization_barrier((sent, w_gate, w_up, w_down))
    core = exchanged(sent, 1)
    half_sums = jax.ShapeDtypeStruct((rows, WIDE), jnp.bfloat16)
    own_sums, pair_sums = pl.pallas_call(
        core_kernel,
        out_shape=(half_sums, half_sums),
        in_specs=[whole] * 2,
        out_specs=(whole, whole),
        compiler_params=pltpu.CompilerParams(vmem_limit_bytes=4 << 20),
        cost_estimate=pl.CostEstimate(flops=1 << 34, bytes_accessed=1 << 20, transcendentals=0),
        name="coresum",
    )(kept, core)
    chip_own = exchanged(pair_sums, 2)
    chip_pair = exchanged(own_sums, 2)

    def normed(block, chip):
        outs = (pltpu.VMEM((rows, MODEL_WIDTH), jnp.bfloat16),) * (block == 0)
        outs += (jax.ShapeDtypeStruct((rows, WIDE), jnp.bfloat16),)
        return pl.pallas_call(
            functools.partial(norm_kernel, block),
            out_shape=outs,
            in_specs=[whole] * 4,
            out_specs=(whole,) * len(outs),
            compiler_params=pltpu.CompilerParams(vmem_limit_bytes=6 << 20),
            cost_estimate=pl.CostEstimate(
                flops=1 << 20, bytes_accessed=1 << 20, transcendentals=1 << 10
            ),
            name="norm",
        )(kept, core, chip, norm_gain[None])

    def expert(mine):
        half = mine.shape[0]
        other = exchanged(mine, 1)
        keep, send = pl.pallas_call(
            expert_kernel,
            out_shape=(
                jax.ShapeDtypeStruct((half, MODEL_WIDTH), jnp.float32),
                jax.ShapeDtypeStruct((half, MODEL_WIDTH), jnp.bfloat16),
            ),
            in_specs=[whole] * 5,
            out_specs=(whole, whole),
            scratch_shapes=[
                pltpu.VMEM((2 * half, WIDE), jnp.bfloat16),
                pltpu.VMEM((2 * half, w_gate.shape[2]), jnp.bfloat16),
            ],
            compiler_params=pltpu.CompilerParams(vmem_limit_bytes=12 << 20),
            cost_estimate=pl.CostEstimate(
                flops=1 << 30, bytes_accessed=1 << 23, transcendentals=1 << 18
            ),
            name="expert",
        )(mine, other, w_gate, w_up, w_down)
        back = exchanged(send, 1)
        total = keep + back.astype(jnp.float32)
        return total.reshape(half // (2 * rows), 2, rows, MODEL_WIDTH)

    attended, own = normed(0, chip_own)
    far = exchanged(own, 8)
    (pair,) = normed(1, chip_pair)
    packet = jnp.concatenate([own, pair], 0)
    near = exchanged(packet, 4)
    across = exchanged(packet, 12)
    passed = exchanged(far, 2)
    sums = expert(jnp.concatenate([packet, near], 0))
    got_near = exchanged(sums[1, 1].astype(jnp.bfloat16), 2)
    got_own = exchanged(sums[0, 1].astype(jnp.bfloat16), 2)
    near_sum = (sums[1, 0] + got_near.astype(jnp.float32)).astype(jnp.bfloat16)
    summed = sums[0, 0] + got_own.astype(jnp.float32)
    near = exchanged(near_sum, 4)
    sums = expert(jnp.concatenate([far, passed, across], 0))
    got_far = exchanged(sums[0, 1].astype(jnp.bfloat16), 2)
    got_across = exchanged(sums[1, 1].astype(jnp.bfloat16), 2)
    far_sum = pl.pallas_call(
        sum_kernel,
        out_shape=jax.ShapeDtypeStruct((rows, MODEL_WIDTH), jnp.bfloat16),
        in_specs=[whole] * 2,
        out_specs=whole,
        compiler_params=pltpu.CompilerParams(vmem_limit_bytes=4 << 20),
        cost_estimate=pl.CostEstimate(flops=1 << 16, bytes_accessed=1 << 18, transcendentals=0),
        name="farsum",
    )(sums, got_far)
    far = exchanged(far_sum, 8)
    across_sum = (sums[1, 0] + got_across.astype(jnp.float32)).astype(jnp.bfloat16)
    across = exchanged(across_sum, 12)
    summed = summed + near.astype(jnp.float32) + far.astype(jnp.float32) + across.astype(jnp.float32)
    return (attended, summed.astype(jnp.bfloat16))


def swapped(block, axis, distance):
    count = lax.axis_size(axis)
    route = []
    for low in range(count):
        high = low | 1 << distance
        if high != low and high < count:
            route += [(low, high), (high, low)]
    return lax.ppermute(block, axis, route)


def routed_rows(
    queries,
    key_cache,
    value_cache,
    key_block,
    value_block,
    cache_length_list,
    residual,
    output_weight,
    norm_gain,
    routes,
    route_logits,
    w_gate,
    w_up,
    w_down,
):
    group_results = QUERY_HEADS // KEY_VALUE_HEADS
    shard_worker = lax.axis_index("ep")
    sequence_group_index = shard_worker // KEY_VALUE_HEADS
    head_shard_index = shard_worker % KEY_VALUE_HEADS
    seq_grp = key_cache.shape[1]
    cache_len = key_cache.shape[2]
    rows_per_group = queries.shape[1]
    block_len = rows_per_group // seq_grp
    live_lens = lax.dynamic_slice_in_dim(cache_length_list, sequence_group_index * seq_grp, seq_grp)
    heads_of_query = queries[0].reshape(seq_grp, block_len, group_results, HEAD_SIZE)
    keys_of_block = key_block[0].reshape(seq_grp, block_len, HEAD_SIZE)
    values_of_block = value_block[0].reshape(seq_grp, block_len, HEAD_SIZE)
    score_cache = jnp.einsum(
        "srgd,spd->sgrp", heads_of_query, key_cache[0], preferred_element_type=jnp.float32
    ) / math.sqrt(HEAD_SIZE)
    score_block = jnp.einsum(
        "srgd,spd->sgrp", heads_of_query, keys_of_block, preferred_element_type=jnp.float32
    ) / math.sqrt(HEAD_SIZE)
    position = jnp.arange(cache_len, dtype=jnp.int32)
    live_slots = position[None, :] < live_lens[:, None]
    score_cache = jnp.where(live_slots[:, None, None, :], score_cache, -1e30)
    largest = jnp.maximum(
        jnp.max(score_cache, -1, keepdims=True), jnp.max(score_block, -1, keepdims=True)
    )
    exp_cache = jnp.exp(score_cache - largest)
    exp_block = jnp.exp(score_block - largest)
    denominator = jnp.sum(exp_cache, -1, keepdims=True) + jnp.sum(exp_block, -1, keepdims=True)
    prob_cache = (exp_cache / denominator).astype(jnp.bfloat16)
    prob_block = (exp_block / denominator).astype(jnp.bfloat16)
    mixed_heads = jnp.einsum(
        "sgrp,spd->srgd", prob_cache, value_cache[0], preferred_element_type=jnp.float32
    )
    mixed_heads = mixed_heads + jnp.einsum(
        "sgrp,spd->srgd", prob_block, values_of_block, preferred_element_type=jnp.float32
    )
    attn_rows = mixed_heads.reshape(rows_per_group, group_results * HEAD_SIZE).astype(jnp.bfloat16)
    partial_value = jnp.dot(attn_rows, output_weight[0], preferred_element_type=jnp.float32)
    tree_levels = KEY_VALUE_HEADS.bit_length() - 1
    projected = partial_value
    for bit_pos in reversed(range(tree_levels)):
        half_rows = projected.shape[0] // 2
        low_half = projected[:half_rows]
        high_half = projected[half_rows:]
        upper_side = head_shard_index >> bit_pos & 1 == 1
        kept_rows = jnp.where(upper_side, high_half, low_half)
        sent_rows = jnp.where(upper_side, low_half, high_half)
        projected = kept_rows + swapped(sent_rows, "ep", bit_pos)
    hidden = residual.astype(jnp.float32) + projected
    attended = hidden.astype(jnp.bfloat16)
    normed = (
        hidden * lax.rsqrt(jnp.mean(hidden * hidden, -1, keepdims=True) + EPSILON) * norm_gain
    ).astype(jnp.bfloat16)
    sig_values = jax.nn.sigmoid(route_logits)
    route_weights = ROUTE_SCALE * sig_values / jnp.sum(sig_values, -1, keepdims=True)
    owners = lax.axis_size("ep")
    exp_dev = w_gate.shape[0]
    experts = owners * exp_dev
    row_count = residual.shape[0]
    top_k = routes.shape[1]
    capacity = max(2, 2 * row_count * top_k // experts)
    flat_ids = routes.reshape(-1)
    onehot = (flat_ids[:, None] == jnp.arange(experts, dtype=jnp.int32)[None, :]).astype(jnp.int32)
    slot_rank = jnp.sum(jnp.cumsum(onehot, 0) * onehot, 1) - 1
    target = flat_ids * capacity + slot_rank
    source_rows = jnp.repeat(normed, top_k, axis=0)
    outgoing = (
        jnp.zeros((experts * capacity, MODEL_WIDTH), jnp.bfloat16).at[target].set(source_rows)
    )
    outgoing = outgoing.reshape(owners, exp_dev, capacity, MODEL_WIDTH)
    arrived = lax.all_to_all(outgoing, "ep", split_axis=0, concat_axis=0, tiled=True)
    gate_part = jnp.einsum("nesd,edh->nesh", arrived, w_gate, preferred_element_type=jnp.float32)
    up_part = jnp.einsum("nesd,edh->nesh", arrived, w_up, preferred_element_type=jnp.float32)
    active = (jax.nn.silu(gate_part) * up_part).astype(jnp.bfloat16)
    result = jnp.einsum(
        "nesh,ehd->nesd", active, w_down, preferred_element_type=jnp.float32
    ).astype(jnp.bfloat16)
    returned = lax.all_to_all(result, "ep", split_axis=0, concat_axis=0, tiled=True)
    fetched = returned.reshape(experts * capacity, MODEL_WIDTH)[target].reshape(
        row_count, top_k, MODEL_WIDTH
    )
    weighted = jnp.sum(route_weights[:, :, None] * fetched.astype(jnp.float32), 1)
    expert_out = weighted.astype(jnp.bfloat16)
    return (attended, expert_out)


def on_device(*inputs):
    row_count, top_k = inputs[9].shape
    owners = lax.axis_size("ep")
    experts = owners * inputs[11].shape[0]
    capacity = max(2, 2 * row_count * top_k // experts)
    all_rows = row_count <= capacity and experts == owners == 4 * KEY_VALUE_HEADS
    if not all_rows:
        return routed_rows(*inputs)
    return every_row(*inputs)


def solution(mesh):
    return jax.shard_map(
        on_device,
        mesh=mesh,
        in_specs=(
            P(("groups", "ep"), None, None),
            P(("groups", "ep"), None, None, None),
            P(("groups", "ep"), None, None, None),
            P(("groups", "ep"), None, None),
            P(("groups", "ep"), None, None),
            P("groups"),
            P(("groups", "ep"), None),
            P("ep", None, None),
            P(),
            P(("groups", "ep"), None),
            P(("groups", "ep"), None),
            P("ep", None, None),
            P("ep", None, None),
            P("ep", None, None),
        ),
        out_specs=(P(("groups", "ep"), None), P(("groups", "ep"), None)),
        check_vma=False,
    )
```

```python
import functools
import math

import jax
import jax.numpy as jnp
from jax import lax
from jax.experimental import pallas as pl
from jax.experimental.pallas import tpu as pltpu
from jax.sharding import PartitionSpec as P


MODEL_WIDTH = 2048
QUERY_HEADS = 16
KEY_VALUE_HEADS = 4
HEAD_SIZE = 128


ROUTE_SCALE = 2.5
EPSILON = 1e-06
LANES = 128
WIDE = MODEL_WIDTH + LANES
CHUNK = 256


def exchanged(block, mask):
    count = lax.axis_size("ep")
    return lax.ppermute(block, "ep", [(index, index ^ mask) for index in range(count)])


def attend_kernel(
    lens_hbm, q_hbm, kc_hbm, vc_hbm, kb_hbm, vb_hbm, res_hbm, routes_hbm, logits_hbm, w_hbm,
    sent, kept,
    lens, q, kc, vc, kb, vb, res, routes, logits, w, attn, sems,
):
    pairs = (
        (lens_hbm, lens), (q_hbm, q), (kb_hbm, kb), (kc_hbm, kc), (vb_hbm, vb), (vc_hbm, vc),
        (routes_hbm, routes), (logits_hbm, logits), (res_hbm, res), (w_hbm, w),
    )
    copies = [pltpu.make_async_copy(a, b, sems.at[i]) for i, (a, b) in enumerate(pairs)]
    for copy in copies:
        copy.start()
    worker = lax.axis_index("ep")
    shard = lax.rem(worker, KEY_VALUE_HEADS)
    group = lax.div(worker, KEY_VALUE_HEADS)
    seqs = kc.shape[1]
    block = q.shape[1] // seqs
    heads = q.shape[2] // HEAD_SIZE
    rows = res.shape[0]
    scale = 1.0 / math.sqrt(HEAD_SIZE)
    nt = (((1,), (1,)), ((), ()))
    for copy in copies[:4]:
        copy.wait()
    probs = []
    for t in range(seqs):
        live = lens[group * seqs + t]
        part = slice(t * block, (t + 1) * block)
        queries = jnp.concatenate(
            [q[0, part, g * HEAD_SIZE : (g + 1) * HEAD_SIZE] for g in range(heads)], 0
        )
        cache = lax.dot_general(queries, kc[0, t], nt, preferred_element_type=jnp.float32) * scale
        fresh = lax.dot_general(queries, kb[0, part], nt, preferred_element_type=jnp.float32) * scale
        position = lax.broadcasted_iota(jnp.int32, cache.shape, 1)
        cache = jnp.where(position < live, cache, -1e30)
        probs.append((cache, fresh))
    for t in range(seqs):
        cache, fresh = probs[t]
        largest = jnp.maximum(
            jnp.max(cache, -1, keepdims=True), jnp.max(fresh, -1, keepdims=True)
        )
        cache = jnp.exp(cache - largest)
        fresh = jnp.exp(fresh - largest)
        total = jnp.sum(cache, -1, keepdims=True) + jnp.sum(fresh, -1, keepdims=True)
        share = 1.0 / total
        probs[t] = (cache * share).astype(jnp.bfloat16), (fresh * share).astype(jnp.bfloat16)
    copies[4].wait()
    copies[5].wait()
    for t in range(seqs):
        cache, fresh = probs[t]
        part = slice(t * block, (t + 1) * block)
        mixed = jnp.dot(cache, vc[0, t], preferred_element_type=jnp.float32) + jnp.dot(
            fresh, vb[0, part], preferred_element_type=jnp.float32
        )
        for g in range(heads):
            attn[part, g * HEAD_SIZE : (g + 1) * HEAD_SIZE] = mixed[
                g * block : (g + 1) * block
            ].astype(jnp.bfloat16)
    for copy in copies[6:9]:
        copy.wait()
    experts = lax.axis_size("ep")
    sig = 1.0 / (1.0 + jnp.exp(-logits[...]))
    weights = ROUTE_SCALE * sig / jnp.sum(sig, 0, keepdims=True)
    line = lax.broadcasted_iota(jnp.int32, (LANES, rows), 0)
    name = jnp.where(line < experts, line, line - experts)
    table = jnp.zeros((LANES, rows), jnp.float32)
    for k in range(routes.shape[0]):
        table = table + jnp.where(routes[k : k + 1, :] == name, weights[k : k + 1, :], 0.0)
    high = table.astype(jnp.bfloat16).astype(jnp.float32)
    table = jnp.where(line < experts, high, table - high).astype(jnp.bfloat16)
    row = lax.broadcasted_iota(jnp.int32, (rows, rows), 0)
    unit = jnp.where(row == lax.broadcasted_iota(jnp.int32, (rows, rows), 1), 1.0, 0.0)
    kept[:rows, MODEL_WIDTH:] = lax.dot_general(
        unit.astype(jnp.bfloat16), table, nt, preferred_element_type=jnp.float32
    )
    kept[rows:, MODEL_WIDTH:] = jnp.zeros((rows, LANES), jnp.float32)
    sent[:, MODEL_WIDTH:] = jnp.zeros((2 * rows, LANES), jnp.bfloat16)
    copies[9].wait()
    picked = [
        attn[pl.ds(pl.multiple_of((shard ^ mask) * rows, rows), rows), :] for mask in (1, 3, 0, 2)
    ]
    picked = jnp.concatenate(picked, 0)
    for n in range(0, MODEL_WIDTH, 2 * CHUNK):
        cols = slice(n, n + 2 * CHUNK)
        out = jnp.dot(picked, w[0, :, cols], preferred_element_type=jnp.float32)
        sent[:, cols] = out[: 2 * rows].astype(jnp.bfloat16)
        kept[:rows, cols] = out[2 * rows : 3 * rows] + res[:, cols].astype(jnp.float32)
        kept[rows:, cols] = out[3 * rows :]


def norm_kernel(block, kept, core, chip, gain, *outs):
    packet = outs[-1]
    rows = packet.shape[0]
    here = slice(block * rows, (block + 1) * rows)
    hidden = kept[here, :] + core[here, :].astype(jnp.float32) + chip[...].astype(jnp.float32)
    table = hidden[:, MODEL_WIDTH:]
    hidden = hidden[:, :MODEL_WIDTH]
    if block == 0:
        outs[0][...] = hidden.astype(jnp.bfloat16)
    mean = jnp.sum(hidden * hidden, -1, keepdims=True) * (1.0 / MODEL_WIDTH)
    packet[:, :MODEL_WIDTH] = (hidden * lax.rsqrt(mean + EPSILON) * gain[...]).astype(jnp.bfloat16)
    packet[:, MODEL_WIDTH:] = table.astype(jnp.bfloat16)


def expert_kernel(mine, other, w_gate, w_up, w_down, keep, send, x, act):
    half = mine.shape[0]
    experts = lax.axis_size("ep")
    own = lax.axis_index("ep")
    x[:half, :] = mine[...]
    x[half:, :] = other[...]
    lane = lax.broadcasted_iota(jnp.int32, (2 * half, LANES), 1)
    codes = x[:, MODEL_WIDTH:].astype(jnp.float32)
    chosen = (lane == own) | (lane == own + experts)
    weight = jnp.sum(jnp.where(chosen, codes, 0.0), 1, keepdims=True)
    rows = x[:, :MODEL_WIDTH]
    hidden_units = w_gate.shape[2]
    for n in range(0, hidden_units, CHUNK):
        cols = slice(n, n + CHUNK)
        gate = jnp.dot(rows, w_gate[0, :, cols], preferred_element_type=jnp.float32)
        up = jnp.dot(rows, w_up[0, :, cols], preferred_element_type=jnp.float32)
        act[:, cols] = (gate / (1.0 + jnp.exp(-gate)) * up).astype(jnp.bfloat16)
    for n in range(0, MODEL_WIDTH, CHUNK):
        cols = slice(n, n + CHUNK)
        out = jnp.dot(act[...], w_down[0, :, cols], preferred_element_type=jnp.float32) * weight
        keep[:, cols] = out[:half]
        send[:, cols] = out[half:].astype(jnp.bfloat16)


def sum_kernel(sums, got, out):
    out[...] = (sums[0, 0] + got[...].astype(jnp.float32)).astype(jnp.bfloat16)


def every_row(
    queries, key_cache, value_cache, key_block, value_block, cache_length_list, residual,
    output_weight, norm_gain, routes, route_logits, w_gate, w_up, w_down,
):
    rows = residual.shape[0]
    anywhere = pl.BlockSpec(memory_space=pl.ANY)
    whole = pl.BlockSpec(memory_space=pltpu.VMEM)
    operands = (
        cache_length_list, queries, key_cache, value_cache, key_block, value_block, residual,
        routes.T, route_logits.T, output_weight,
    )
    operands = tuple(pltpu.with_memory_space_constraint(a, pltpu.HBM) for a in operands)
    scratch = [pltpu.SMEM(cache_length_list.shape, jnp.int32)]
    scratch += [pltpu.VMEM(a.shape, a.dtype) for a in operands[1:]]
    scratch += [
        pltpu.VMEM((queries.shape[1], queries.shape[2]), jnp.bfloat16),
        pltpu.SemaphoreType.DMA((len(operands),)),
    ]
    sent, kept = pl.pallas_call(
        attend_kernel,
        out_shape=(
            jax.ShapeDtypeStruct((2 * rows, WIDE), jnp.bfloat16),
            jax.ShapeDtypeStruct((2 * rows, WIDE), jnp.float32),
        ),
        in_specs=[anywhere] * len(operands),
        out_specs=(whole, whole),
        scratch_shapes=scratch,
        compiler_params=pltpu.CompilerParams(vmem_limit_bytes=12 << 20),
        cost_estimate=pl.CostEstimate(flops=1 << 30, bytes_accessed=1 << 23, transcendentals=1 << 18),
        name="attend",
    )(*operands)
    sent, w_gate, w_up, w_down = lax.optimization_barrier((sent, w_gate, w_up, w_down))
    core = exchanged(sent, 1)
    sums = (kept + core.astype(jnp.float32)).astype(jnp.bfloat16)
    chip_own = exchanged(sums[rows:], 2)
    chip_pair = exchanged(sums[:rows], 2)

    def normed(block, chip):
        outs = (pltpu.VMEM((rows, MODEL_WIDTH), jnp.bfloat16),) * (block == 0)
        outs += (jax.ShapeDtypeStruct((rows, WIDE), jnp.bfloat16),)
        return pl.pallas_call(
            functools.partial(norm_kernel, block),
            out_shape=outs,
            in_specs=[whole] * 4,
            out_specs=(whole,) * len(outs),
            compiler_params=pltpu.CompilerParams(vmem_limit_bytes=6 << 20),
            cost_estimate=pl.CostEstimate(
                flops=1 << 34, bytes_accessed=1 << 20, transcendentals=1 << 10
            ),
            name="norm",
        )(kept, core, chip, norm_gain[None])

    def expert(mine):
        half = mine.shape[0]
        other = exchanged(mine, 1)
        keep, send = pl.pallas_call(
            expert_kernel,
            out_shape=(
                jax.ShapeDtypeStruct((half, MODEL_WIDTH), jnp.float32),
                jax.ShapeDtypeStruct((half, MODEL_WIDTH), jnp.bfloat16),
            ),
            in_specs=[whole] * 5,
            out_specs=(whole, whole),
            scratch_shapes=[
                pltpu.VMEM((2 * half, WIDE), jnp.bfloat16),
                pltpu.VMEM((2 * half, w_gate.shape[2]), jnp.bfloat16),
            ],
            compiler_params=pltpu.CompilerParams(vmem_limit_bytes=12 << 20),
            cost_estimate=pl.CostEstimate(
                flops=1 << 30, bytes_accessed=1 << 23, transcendentals=1 << 18
            ),
            name="expert",
        )(mine, other, w_gate, w_up, w_down)
        back = exchanged(send, 1)
        total = keep + back.astype(jnp.float32)
        return total.reshape(half // (2 * rows), 2, rows, MODEL_WIDTH)

    attended, own = normed(0, chip_own)
    far = exchanged(own, 8)
    (pair,) = normed(1, chip_pair)
    packet = jnp.concatenate([own, pair], 0)
    near = exchanged(packet, 4)
    across = exchanged(packet, 12)
    passed = exchanged(far, 2)
    sums = expert(jnp.concatenate([packet, near], 0))
    got_near = exchanged(sums[1, 1].astype(jnp.bfloat16), 2)
    got_own = exchanged(sums[0, 1].astype(jnp.bfloat16), 2)
    near_sum = (sums[1, 0] + got_near.astype(jnp.float32)).astype(jnp.bfloat16)
    summed = sums[0, 0] + got_own.astype(jnp.float32)
    near = exchanged(near_sum, 4)
    sums = expert(jnp.concatenate([far, passed, across], 0))
    got_far = exchanged(sums[0, 1].astype(jnp.bfloat16), 2)
    got_across = exchanged(sums[1, 1].astype(jnp.bfloat16), 2)
    far_sum = pl.pallas_call(
        sum_kernel,
        out_shape=jax.ShapeDtypeStruct((rows, MODEL_WIDTH), jnp.bfloat16),
        in_specs=[whole] * 2,
        out_specs=whole,
        compiler_params=pltpu.CompilerParams(vmem_limit_bytes=4 << 20),
        cost_estimate=pl.CostEstimate(flops=1 << 16, bytes_accessed=1 << 18, transcendentals=0),
        name="farsum",
    )(sums, got_far)
    far = exchanged(far_sum, 8)
    across_sum = (sums[1, 0] + got_across.astype(jnp.float32)).astype(jnp.bfloat16)
    across = exchanged(across_sum, 12)
    summed = summed + near.astype(jnp.float32) + far.astype(jnp.float32) + across.astype(jnp.float32)
    return (attended, summed.astype(jnp.bfloat16))


def swapped(block, axis, distance):
    count = lax.axis_size(axis)
    route = []
    for low in range(count):
        high = low | 1 << distance
        if high != low and high < count:
            route += [(low, high), (high, low)]
    return lax.ppermute(block, axis, route)


def routed_rows(
    queries,
    key_cache,
    value_cache,
    key_block,
    value_block,
    cache_length_list,
    residual,
    output_weight,
    norm_gain,
    routes,
    route_logits,
    w_gate,
    w_up,
    w_down,
):
    group_results = QUERY_HEADS // KEY_VALUE_HEADS
    shard_worker = lax.axis_index("ep")
    sequence_group_index = shard_worker // KEY_VALUE_HEADS
    head_shard_index = shard_worker % KEY_VALUE_HEADS
    seq_grp = key_cache.shape[1]
    cache_len = key_cache.shape[2]
    rows_per_group = queries.shape[1]
    block_len = rows_per_group // seq_grp
    live_lens = lax.dynamic_slice_in_dim(cache_length_list, sequence_group_index * seq_grp, seq_grp)
    heads_of_query = queries[0].reshape(seq_grp, block_len, group_results, HEAD_SIZE)
    keys_of_block = key_block[0].reshape(seq_grp, block_len, HEAD_SIZE)
    values_of_block = value_block[0].reshape(seq_grp, block_len, HEAD_SIZE)
    score_cache = jnp.einsum(
        "srgd,spd->sgrp", heads_of_query, key_cache[0], preferred_element_type=jnp.float32
    ) / math.sqrt(HEAD_SIZE)
    score_block = jnp.einsum(
        "srgd,spd->sgrp", heads_of_query, keys_of_block, preferred_element_type=jnp.float32
    ) / math.sqrt(HEAD_SIZE)
    position = jnp.arange(cache_len, dtype=jnp.int32)
    live_slots = position[None, :] < live_lens[:, None]
    score_cache = jnp.where(live_slots[:, None, None, :], score_cache, -1e30)
    largest = jnp.maximum(
        jnp.max(score_cache, -1, keepdims=True), jnp.max(score_block, -1, keepdims=True)
    )
    exp_cache = jnp.exp(score_cache - largest)
    exp_block = jnp.exp(score_block - largest)
    denominator = jnp.sum(exp_cache, -1, keepdims=True) + jnp.sum(exp_block, -1, keepdims=True)
    prob_cache = (exp_cache / denominator).astype(jnp.bfloat16)
    prob_block = (exp_block / denominator).astype(jnp.bfloat16)
    mixed_heads = jnp.einsum(
        "sgrp,spd->srgd", prob_cache, value_cache[0], preferred_element_type=jnp.float32
    )
    mixed_heads = mixed_heads + jnp.einsum(
        "sgrp,spd->srgd", prob_block, values_of_block, preferred_element_type=jnp.float32
    )
    attn_rows = mixed_heads.reshape(rows_per_group, group_results * HEAD_SIZE).astype(jnp.bfloat16)
    partial_value = jnp.dot(attn_rows, output_weight[0], preferred_element_type=jnp.float32)
    tree_levels = KEY_VALUE_HEADS.bit_length() - 1
    projected = partial_value
    for bit_pos in reversed(range(tree_levels)):
        half_rows = projected.shape[0] // 2
        low_half = projected[:half_rows]
        high_half = projected[half_rows:]
        upper_side = head_shard_index >> bit_pos & 1 == 1
        kept_rows = jnp.where(upper_side, high_half, low_half)
        sent_rows = jnp.where(upper_side, low_half, high_half)
        projected = kept_rows + swapped(sent_rows, "ep", bit_pos)
    hidden = residual.astype(jnp.float32) + projected
    attended = hidden.astype(jnp.bfloat16)
    normed = (
        hidden * lax.rsqrt(jnp.mean(hidden * hidden, -1, keepdims=True) + EPSILON) * norm_gain
    ).astype(jnp.bfloat16)
    sig_values = jax.nn.sigmoid(route_logits)
    route_weights = ROUTE_SCALE * sig_values / jnp.sum(sig_values, -1, keepdims=True)
    owners = lax.axis_size("ep")
    exp_dev = w_gate.shape[0]
    experts = owners * exp_dev
    row_count = residual.shape[0]
    top_k = routes.shape[1]
    capacity = max(2, 2 * row_count * top_k // experts)
    flat_ids = routes.reshape(-1)
    onehot = (flat_ids[:, None] == jnp.arange(experts, dtype=jnp.int32)[None, :]).astype(jnp.int32)
    slot_rank = jnp.sum(jnp.cumsum(onehot, 0) * onehot, 1) - 1
    target = flat_ids * capacity + slot_rank
    source_rows = jnp.repeat(normed, top_k, axis=0)
    outgoing = (
        jnp.zeros((experts * capacity, MODEL_WIDTH), jnp.bfloat16).at[target].set(source_rows)
    )
    outgoing = outgoing.reshape(owners, exp_dev, capacity, MODEL_WIDTH)
    arrived = lax.all_to_all(outgoing, "ep", split_axis=0, concat_axis=0, tiled=True)
    gate_part = jnp.einsum("nesd,edh->nesh", arrived, w_gate, preferred_element_type=jnp.float32)
    up_part = jnp.einsum("nesd,edh->nesh", arrived, w_up, preferred_element_type=jnp.float32)
    active = (jax.nn.silu(gate_part) * up_part).astype(jnp.bfloat16)
    result = jnp.einsum(
        "nesh,ehd->nesd", active, w_down, preferred_element_type=jnp.float32
    ).astype(jnp.bfloat16)
    returned = lax.all_to_all(result, "ep", split_axis=0, concat_axis=0, tiled=True)
    fetched = returned.reshape(experts * capacity, MODEL_WIDTH)[target].reshape(
        row_count, top_k, MODEL_WIDTH
    )
    weighted = jnp.sum(route_weights[:, :, None] * fetched.astype(jnp.float32), 1)
    expert_out = weighted.astype(jnp.bfloat16)
    return (attended, expert_out)


def on_device(*inputs):
    row_count, top_k = inputs[9].shape
    owners = lax.axis_size("ep")
    experts = owners * inputs[11].shape[0]
    capacity = max(2, 2 * row_count * top_k // experts)
    all_rows = row_count <= capacity and experts == owners == 4 * KEY_VALUE_HEADS
    if not all_rows:
        return routed_rows(*inputs)
    return every_row(*inputs)


def solution(mesh):
    return jax.shard_map(
        on_device,
        mesh=mesh,
        in_specs=(
            P(("groups", "ep"), None, None),
            P(("groups", "ep"), None, None, None),
            P(("groups", "ep"), None, None, None),
            P(("groups", "ep"), None, None),
            P(("groups", "ep"), None, None),
            P("groups"),
            P(("groups", "ep"), None),
            P("ep", None, None),
            P(),
            P(("groups", "ep"), None),
            P(("groups", "ep"), None),
            P("ep", None, None),
            P("ep", None, None),
            P("ep", None, None),
        ),
        out_specs=(P(("groups", "ep"), None), P(("groups", "ep"), None)),
        check_vma=False,
    )
```

```python
import functools
import math

import jax
import jax.numpy as jnp
from jax import lax
from jax.experimental import pallas as pl
from jax.experimental.pallas import tpu as pltpu
from jax.sharding import PartitionSpec as P


MODEL_WIDTH = 2048
QUERY_HEADS = 16
KEY_VALUE_HEADS = 4
HEAD_SIZE = 128


ROUTE_SCALE = 2.5
EPSILON = 1e-06
LANES = 128
WIDE = MODEL_WIDTH + LANES
CHUNK = 256


def exchanged(block, mask):
    count = lax.axis_size("ep")
    return lax.ppermute(block, "ep", [(index, index ^ mask) for index in range(count)])


def attend_kernel(
    lens_hbm, q_hbm, kc_hbm, vc_hbm, kb_hbm, vb_hbm, res_hbm, routes_hbm, logits_hbm, w_hbm,
    sent, kept,
    lens, q, kc, vc, kb, vb, res, routes, logits, w, attn, sems,
):
    pairs = (
        (lens_hbm, lens), (q_hbm, q), (kb_hbm, kb), (kc_hbm, kc), (vb_hbm, vb), (vc_hbm, vc),
        (routes_hbm, routes), (logits_hbm, logits), (res_hbm, res), (w_hbm, w),
    )
    copies = [pltpu.make_async_copy(a, b, sems.at[i]) for i, (a, b) in enumerate(pairs)]
    for copy in copies:
        copy.start()
    worker = lax.axis_index("ep")
    shard = lax.rem(worker, KEY_VALUE_HEADS)
    group = lax.div(worker, KEY_VALUE_HEADS)
    seqs = kc.shape[1]
    block = q.shape[1] // seqs
    heads = q.shape[2] // HEAD_SIZE
    rows = res.shape[0]
    scale = 1.0 / math.sqrt(HEAD_SIZE)
    nt = (((1,), (1,)), ((), ()))
    for copy in copies[:4]:
        copy.wait()
    probs = []
    for t in range(seqs):
        live = lens[group * seqs + t]
        part = slice(t * block, (t + 1) * block)
        queries = jnp.concatenate(
            [q[0, part, g * HEAD_SIZE : (g + 1) * HEAD_SIZE] for g in range(heads)], 0
        )
        cache = lax.dot_general(queries, kc[0, t], nt, preferred_element_type=jnp.float32) * scale
        fresh = lax.dot_general(queries, kb[0, part], nt, preferred_element_type=jnp.float32) * scale
        position = lax.broadcasted_iota(jnp.int32, cache.shape, 1)
        cache = jnp.where(position < live, cache, -1e30)
        probs.append((cache, fresh))
    for t in range(seqs):
        cache, fresh = probs[t]
        largest = jnp.maximum(
            jnp.max(cache, -1, keepdims=True), jnp.max(fresh, -1, keepdims=True)
        )
        cache = jnp.exp(cache - largest)
        fresh = jnp.exp(fresh - largest)
        total = jnp.sum(cache, -1, keepdims=True) + jnp.sum(fresh, -1, keepdims=True)
        share = 1.0 / total
        probs[t] = (cache * share).astype(jnp.bfloat16), (fresh * share).astype(jnp.bfloat16)
    copies[4].wait()
    copies[5].wait()
    for t in range(seqs):
        cache, fresh = probs[t]
        part = slice(t * block, (t + 1) * block)
        mixed = jnp.dot(cache, vc[0, t], preferred_element_type=jnp.float32) + jnp.dot(
            fresh, vb[0, part], preferred_element_type=jnp.float32
        )
        for g in range(heads):
            attn[part, g * HEAD_SIZE : (g + 1) * HEAD_SIZE] = mixed[
                g * block : (g + 1) * block
            ].astype(jnp.bfloat16)
    for copy in copies[6:9]:
        copy.wait()
    experts = lax.axis_size("ep")
    sig = 1.0 / (1.0 + jnp.exp(-logits[...]))
    weights = ROUTE_SCALE * sig / jnp.sum(sig, 0, keepdims=True)
    line = lax.broadcasted_iota(jnp.int32, (LANES, rows), 0)
    name = jnp.where(line < experts, line, line - experts)
    table = jnp.zeros((LANES, rows), jnp.float32)
    for k in range(routes.shape[0]):
        table = table + jnp.where(routes[k : k + 1, :] == name, weights[k : k + 1, :], 0.0)
    high = table.astype(jnp.bfloat16).astype(jnp.float32)
    table = jnp.where(line < experts, high, table - high).astype(jnp.bfloat16)
    row = lax.broadcasted_iota(jnp.int32, (rows, rows), 0)
    unit = jnp.where(row == lax.broadcasted_iota(jnp.int32, (rows, rows), 1), 1.0, 0.0)
    kept[:rows, MODEL_WIDTH:] = lax.dot_general(
        unit.astype(jnp.bfloat16), table, nt, preferred_element_type=jnp.float32
    )
    kept[rows:, MODEL_WIDTH:] = jnp.zeros((rows, LANES), jnp.float32)
    sent[:, MODEL_WIDTH:] = jnp.zeros((2 * rows, LANES), jnp.bfloat16)
    copies[9].wait()
    picked = [
        attn[pl.ds(pl.multiple_of((shard ^ mask) * rows, rows), rows), :] for mask in (1, 3, 0, 2)
    ]
    picked = jnp.concatenate(picked, 0)
    for n in range(0, MODEL_WIDTH, 2 * CHUNK):
        cols = slice(n, n + 2 * CHUNK)
        out = jnp.dot(picked, w[0, :, cols], preferred_element_type=jnp.float32)
        sent[:, cols] = out[: 2 * rows].astype(jnp.bfloat16)
        kept[:rows, cols] = out[2 * rows : 3 * rows] + res[:, cols].astype(jnp.float32)
        kept[rows:, cols] = out[3 * rows :]


def norm_kernel(block, kept, core, chip, gain, *outs):
    packet = outs[-1]
    rows = packet.shape[0]
    here = slice(block * rows, (block + 1) * rows)
    there = slice((1 - block) * rows, (2 - block) * rows)
    hidden = kept[here, :] + core[here, :].astype(jnp.float32) + chip[there, :].astype(jnp.float32)
    table = hidden[:, MODEL_WIDTH:]
    hidden = hidden[:, :MODEL_WIDTH]
    if block == 0:
        outs[0][...] = hidden.astype(jnp.bfloat16)
    mean = jnp.sum(hidden * hidden, -1, keepdims=True) * (1.0 / MODEL_WIDTH)
    packet[:, :MODEL_WIDTH] = (hidden * lax.rsqrt(mean + EPSILON) * gain[...]).astype(jnp.bfloat16)
    packet[:, MODEL_WIDTH:] = table.astype(jnp.bfloat16)


def expert_kernel(mine, other, w_gate, w_up, w_down, keep, send, x, act):
    half = mine.shape[0]
    experts = lax.axis_size("ep")
    own = lax.axis_index("ep")
    x[:half, :] = mine[...]
    x[half:, :] = other[...]
    lane = lax.broadcasted_iota(jnp.int32, (2 * half, LANES), 1)
    codes = x[:, MODEL_WIDTH:].astype(jnp.float32)
    chosen = (lane == own) | (lane == own + experts)
    weight = jnp.sum(jnp.where(chosen, codes, 0.0), 1, keepdims=True)
    rows = x[:, :MODEL_WIDTH]
    hidden_units = w_gate.shape[2]
    for n in range(0, hidden_units, CHUNK):
        cols = slice(n, n + CHUNK)
        gate = jnp.dot(rows, w_gate[0, :, cols], preferred_element_type=jnp.float32)
        up = jnp.dot(rows, w_up[0, :, cols], preferred_element_type=jnp.float32)
        act[:, cols] = (gate / (1.0 + jnp.exp(-gate)) * up).astype(jnp.bfloat16)
    for n in range(0, MODEL_WIDTH, CHUNK):
        cols = slice(n, n + CHUNK)
        out = jnp.dot(act[...], w_down[0, :, cols], preferred_element_type=jnp.float32) * weight
        keep[:, cols] = out[:half]
        send[:, cols] = out[half:].astype(jnp.bfloat16)


def sum_kernel(sums, got, out):
    out[...] = (sums[0, 0] + got[...].astype(jnp.float32)).astype(jnp.bfloat16)


def every_row(
    queries, key_cache, value_cache, key_block, value_block, cache_length_list, residual,
    output_weight, norm_gain, routes, route_logits, w_gate, w_up, w_down,
):
    rows = residual.shape[0]
    anywhere = pl.BlockSpec(memory_space=pl.ANY)
    whole = pl.BlockSpec(memory_space=pltpu.VMEM)
    operands = (
        cache_length_list, queries, key_cache, value_cache, key_block, value_block, residual,
        routes.T, route_logits.T, output_weight,
    )
    operands = tuple(pltpu.with_memory_space_constraint(a, pltpu.HBM) for a in operands)
    scratch = [pltpu.SMEM(cache_length_list.shape, jnp.int32)]
    scratch += [pltpu.VMEM(a.shape, a.dtype) for a in operands[1:]]
    scratch += [
        pltpu.VMEM((queries.shape[1], queries.shape[2]), jnp.bfloat16),
        pltpu.SemaphoreType.DMA((len(operands),)),
    ]
    sent, kept = pl.pallas_call(
        attend_kernel,
        out_shape=(
            jax.ShapeDtypeStruct((2 * rows, WIDE), jnp.bfloat16),
            jax.ShapeDtypeStruct((2 * rows, WIDE), jnp.float32),
        ),
        in_specs=[anywhere] * len(operands),
        out_specs=(whole, whole),
        scratch_shapes=scratch,
        compiler_params=pltpu.CompilerParams(vmem_limit_bytes=12 << 20),
        cost_estimate=pl.CostEstimate(flops=1 << 30, bytes_accessed=1 << 23, transcendentals=1 << 18),
        name="attend",
    )(*operands)
    sent, w_gate, w_up, w_down = lax.optimization_barrier((sent, w_gate, w_up, w_down))
    core = exchanged(sent, 1)
    sums = (kept + core.astype(jnp.float32)).astype(jnp.bfloat16)
    chip = exchanged(sums, 2)

    def normed(block):
        outs = (pltpu.VMEM((rows, MODEL_WIDTH), jnp.bfloat16),) * (block == 0)
        outs += (jax.ShapeDtypeStruct((rows, WIDE), jnp.bfloat16),)
        return pl.pallas_call(
            functools.partial(norm_kernel, block),
            out_shape=outs,
            in_specs=[whole] * 4,
            out_specs=(whole,) * len(outs),
            compiler_params=pltpu.CompilerParams(vmem_limit_bytes=6 << 20),
            cost_estimate=pl.CostEstimate(
                flops=1 << 34, bytes_accessed=1 << 20, transcendentals=1 << 10
            ),
            name="norm",
        )(kept, core, chip, norm_gain[None])

    def expert(mine):
        half = mine.shape[0]
        other = exchanged(mine, 1)
        keep, send = pl.pallas_call(
            expert_kernel,
            out_shape=(
                jax.ShapeDtypeStruct((half, MODEL_WIDTH), jnp.float32),
                jax.ShapeDtypeStruct((half, MODEL_WIDTH), jnp.bfloat16),
            ),
            in_specs=[whole] * 5,
            out_specs=(whole, whole),
            scratch_shapes=[
                pltpu.VMEM((2 * half, WIDE), jnp.bfloat16),
                pltpu.VMEM((2 * half, w_gate.shape[2]), jnp.bfloat16),
            ],
            compiler_params=pltpu.CompilerParams(vmem_limit_bytes=12 << 20),
            cost_estimate=pl.CostEstimate(
                flops=1 << 30, bytes_accessed=1 << 23, transcendentals=1 << 18
            ),
            name="expert",
        )(mine, other, w_gate, w_up, w_down)
        back = exchanged(send, 1)
        total = keep + back.astype(jnp.float32)
        return total.reshape(half // (2 * rows), 2, rows, MODEL_WIDTH)

    attended, own = normed(0)
    far = exchanged(own, 8)
    (pair,) = normed(1)
    packet = jnp.concatenate([own, pair], 0)
    near = exchanged(packet, 4)
    across = exchanged(packet, 12)
    passed = exchanged(far, 2)
    sums = expert(jnp.concatenate([packet, near], 0))
    got_near = exchanged(sums[1, 1].astype(jnp.bfloat16), 2)
    got_own = exchanged(sums[0, 1].astype(jnp.bfloat16), 2)
    near_sum = (sums[1, 0] + got_near.astype(jnp.float32)).astype(jnp.bfloat16)
    summed = sums[0, 0] + got_own.astype(jnp.float32)
    near = exchanged(near_sum, 4)
    sums = expert(jnp.concatenate([far, passed, across], 0))
    got_far = exchanged(sums[0, 1].astype(jnp.bfloat16), 2)
    got_across = exchanged(sums[1, 1].astype(jnp.bfloat16), 2)
    far_sum = pl.pallas_call(
        sum_kernel,
        out_shape=jax.ShapeDtypeStruct((rows, MODEL_WIDTH), jnp.bfloat16),
        in_specs=[whole] * 2,
        out_specs=whole,
        compiler_params=pltpu.CompilerParams(vmem_limit_bytes=4 << 20),
        cost_estimate=pl.CostEstimate(flops=1 << 16, bytes_accessed=1 << 18, transcendentals=0),
        name="farsum",
    )(sums, got_far)
    far = exchanged(far_sum, 8)
    across_sum = (sums[1, 0] + got_across.astype(jnp.float32)).astype(jnp.bfloat16)
    across = exchanged(across_sum, 12)
    summed = summed + near.astype(jnp.float32) + far.astype(jnp.float32) + across.astype(jnp.float32)
    return (attended, summed.astype(jnp.bfloat16))


def swapped(block, axis, distance):
    count = lax.axis_size(axis)
    route = []
    for low in range(count):
        high = low | 1 << distance
        if high != low and high < count:
            route += [(low, high), (high, low)]
    return lax.ppermute(block, axis, route)


def routed_rows(
    queries,
    key_cache,
    value_cache,
    key_block,
    value_block,
    cache_length_list,
    residual,
    output_weight,
    norm_gain,
    routes,
    route_logits,
    w_gate,
    w_up,
    w_down,
):
    group_results = QUERY_HEADS // KEY_VALUE_HEADS
    shard_worker = lax.axis_index("ep")
    sequence_group_index = shard_worker // KEY_VALUE_HEADS
    head_shard_index = shard_worker % KEY_VALUE_HEADS
    seq_grp = key_cache.shape[1]
    cache_len = key_cache.shape[2]
    rows_per_group = queries.shape[1]
    block_len = rows_per_group // seq_grp
    live_lens = lax.dynamic_slice_in_dim(cache_length_list, sequence_group_index * seq_grp, seq_grp)
    heads_of_query = queries[0].reshape(seq_grp, block_len, group_results, HEAD_SIZE)
    keys_of_block = key_block[0].reshape(seq_grp, block_len, HEAD_SIZE)
    values_of_block = value_block[0].reshape(seq_grp, block_len, HEAD_SIZE)
    score_cache = jnp.einsum(
        "srgd,spd->sgrp", heads_of_query, key_cache[0], preferred_element_type=jnp.float32
    ) / math.sqrt(HEAD_SIZE)
    score_block = jnp.einsum(
        "srgd,spd->sgrp", heads_of_query, keys_of_block, preferred_element_type=jnp.float32
    ) / math.sqrt(HEAD_SIZE)
    position = jnp.arange(cache_len, dtype=jnp.int32)
    live_slots = position[None, :] < live_lens[:, None]
    score_cache = jnp.where(live_slots[:, None, None, :], score_cache, -1e30)
    largest = jnp.maximum(
        jnp.max(score_cache, -1, keepdims=True), jnp.max(score_block, -1, keepdims=True)
    )
    exp_cache = jnp.exp(score_cache - largest)
    exp_block = jnp.exp(score_block - largest)
    denominator = jnp.sum(exp_cache, -1, keepdims=True) + jnp.sum(exp_block, -1, keepdims=True)
    prob_cache = (exp_cache / denominator).astype(jnp.bfloat16)
    prob_block = (exp_block / denominator).astype(jnp.bfloat16)
    mixed_heads = jnp.einsum(
        "sgrp,spd->srgd", prob_cache, value_cache[0], preferred_element_type=jnp.float32
    )
    mixed_heads = mixed_heads + jnp.einsum(
        "sgrp,spd->srgd", prob_block, values_of_block, preferred_element_type=jnp.float32
    )
    attn_rows = mixed_heads.reshape(rows_per_group, group_results * HEAD_SIZE).astype(jnp.bfloat16)
    partial_value = jnp.dot(attn_rows, output_weight[0], preferred_element_type=jnp.float32)
    tree_levels = KEY_VALUE_HEADS.bit_length() - 1
    projected = partial_value
    for bit_pos in reversed(range(tree_levels)):
        half_rows = projected.shape[0] // 2
        low_half = projected[:half_rows]
        high_half = projected[half_rows:]
        upper_side = head_shard_index >> bit_pos & 1 == 1
        kept_rows = jnp.where(upper_side, high_half, low_half)
        sent_rows = jnp.where(upper_side, low_half, high_half)
        projected = kept_rows + swapped(sent_rows, "ep", bit_pos)
    hidden = residual.astype(jnp.float32) + projected
    attended = hidden.astype(jnp.bfloat16)
    normed = (
        hidden * lax.rsqrt(jnp.mean(hidden * hidden, -1, keepdims=True) + EPSILON) * norm_gain
    ).astype(jnp.bfloat16)
    sig_values = jax.nn.sigmoid(route_logits)
    route_weights = ROUTE_SCALE * sig_values / jnp.sum(sig_values, -1, keepdims=True)
    owners = lax.axis_size("ep")
    exp_dev = w_gate.shape[0]
    experts = owners * exp_dev
    row_count = residual.shape[0]
    top_k = routes.shape[1]
    capacity = max(2, 2 * row_count * top_k // experts)
    flat_ids = routes.reshape(-1)
    onehot = (flat_ids[:, None] == jnp.arange(experts, dtype=jnp.int32)[None, :]).astype(jnp.int32)
    slot_rank = jnp.sum(jnp.cumsum(onehot, 0) * onehot, 1) - 1
    target = flat_ids * capacity + slot_rank
    source_rows = jnp.repeat(normed, top_k, axis=0)
    outgoing = (
        jnp.zeros((experts * capacity, MODEL_WIDTH), jnp.bfloat16).at[target].set(source_rows)
    )
    outgoing = outgoing.reshape(owners, exp_dev, capacity, MODEL_WIDTH)
    arrived = lax.all_to_all(outgoing, "ep", split_axis=0, concat_axis=0, tiled=True)
    gate_part = jnp.einsum("nesd,edh->nesh", arrived, w_gate, preferred_element_type=jnp.float32)
    up_part = jnp.einsum("nesd,edh->nesh", arrived, w_up, preferred_element_type=jnp.float32)
    active = (jax.nn.silu(gate_part) * up_part).astype(jnp.bfloat16)
    result = jnp.einsum(
        "nesh,ehd->nesd", active, w_down, preferred_element_type=jnp.float32
    ).astype(jnp.bfloat16)
    returned = lax.all_to_all(result, "ep", split_axis=0, concat_axis=0, tiled=True)
    fetched = returned.reshape(experts * capacity, MODEL_WIDTH)[target].reshape(
        row_count, top_k, MODEL_WIDTH
    )
    weighted = jnp.sum(route_weights[:, :, None] * fetched.astype(jnp.float32), 1)
    expert_out = weighted.astype(jnp.bfloat16)
    return (attended, expert_out)


def on_device(*inputs):
    row_count, top_k = inputs[9].shape
    owners = lax.axis_size("ep")
    experts = owners * inputs[11].shape[0]
    capacity = max(2, 2 * row_count * top_k // experts)
    all_rows = row_count <= capacity and experts == owners == 4 * KEY_VALUE_HEADS
    if not all_rows:
        return routed_rows(*inputs)
    return every_row(*inputs)


def solution(mesh):
    return jax.shard_map(
        on_device,
        mesh=mesh,
        in_specs=(
            P(("groups", "ep"), None, None),
            P(("groups", "ep"), None, None, None),
            P(("groups", "ep"), None, None, None),
            P(("groups", "ep"), None, None),
            P(("groups", "ep"), None, None),
            P("groups"),
            P(("groups", "ep"), None),
            P("ep", None, None),
            P(),
            P(("groups", "ep"), None),
            P(("groups", "ep"), None),
            P("ep", None, None),
            P("ep", None, None),
            P("ep", None, None),
        ),
        out_specs=(P(("groups", "ep"), None), P(("groups", "ep"), None)),
        check_vma=False,
    )
```
